256 devices in a mesh: sub: 32 (over y, x, core), coarse: 8 (over z).
Axes of the slice: x: 4, y: 4, z: 8, core: 2. Of those that a mesh axis runs over, the one named last changes fastest.
Arguments:
- deflation: float32 [32, 64, 128, 512], P('sub', None, 'coarse')
- conductivity: float32 [32, 128, 512], P('sub', 'coarse'), may hold values from 0.1 to 10
- storage: float32 [32, 128, 512], P('sub', 'coarse'), may hold values from 0.5 to 4
- interface_rows: int32 [32, 8, 8, 512], P('sub', 'coarse'), may hold values from 0 to 8191, as said below
- interface_counts: int32 [32, 8, 8], P('sub', 'coarse'), may hold values from 0 to 512, as said below
Outputs:
- coarse_factor: float32 [32, 512, 512], P('sub')
- panel_rows: float32 [32, 8, 512, 512], P('sub', 'coarse')
The draws below stay inside these ranges and needn't reach their ends.
Inputs may be any that keep to these rules, and one draw needn't show every extreme that they name: Slot j of a subdomain names the column offset o = j - 4 for j < 4 and j - 3 otherwise; interface_counts[a, c, slot of o] equals interface_counts[a + o, c, slot of -o], and is 0 where a + o lies outside 0 to 31. The most, 512, is reached in every draw. `interface_rows`: slots j < 4 hold cells with x = 0, the others cells with x = 15. Entries past a slot's count are also such cells and carry no edge.
All inputs are finite; a program needn't handle non-finite values.
Results may differ from the reference program's by a relative error of at most 0.0003.
Values sent between devices are 32-bit elements; how exact they have to be, the bound alone decides.
No kernel may reach another device: no remote copies, remote signals or barrier semaphores. Data moves between devices by JAX's collectives and lax.ppermute only.
A program may use at most 64 MiB of HBM per device.

```python
import math
import jax
import jax.numpy as jnp
from jax import lax

K = 64
CX = 16
CY = 32
CZ = 16
PAD = 512
REACH = 4
COLUMNS = 32
NZ = 128
N_SUB = 32
N_COARSE = 8


def draw_deflation(key, part):
    noise_key = jax.random.fold_in(key, 21)
    amplitude_key = jax.random.fold_in(key, 22)
    noise = jax.random.normal(noise_key, (N_SUB, K, NZ, CX * CY), jnp.float32)
    amplitude = 1.5 * jax.random.normal(amplitude_key, (N_SUB, K, NZ, 1), jnp.float32)
    return ((noise + amplitude) / math.sqrt(CX * CY)).astype(jnp.float32)


def draw_interface_rows(key, part):
    row_key = jax.random.fold_in(key, 41)
    layer_key = jax.random.fold_in(key, 42)
    shape = (N_SUB, N_COARSE, 2 * REACH, PAD)
    row_y = jax.random.randint(row_key, shape, 0, CY)
    layer_z = jax.random.randint(layer_key, shape, 0, CZ)
    slot = jnp.arange(2 * REACH)[None, None, :, None]
    edge_x = jnp.where(slot < REACH, 0, CX - 1)
    return (layer_z * (CX * CY) + row_y * CX + edge_x).astype(jnp.int32)


def draw_interface_counts(key, part):
    first_key = jax.random.fold_in(key, 31)
    second_key = jax.random.fold_in(key, 32)
    third_key = jax.random.fold_in(key, 33)
    forward = jax.random.randint(first_key, (N_SUB, N_COARSE, REACH), 1, PAD + 1)
    absent = jax.random.randint(second_key, (N_SUB, N_COARSE, REACH), 0, 4) == 0
    forward = jnp.where(absent, 0, forward)
    chosen = jax.random.randint(third_key, (), 0, N_SUB - 1)
    column = jnp.arange(N_SUB)[:, None, None]
    reach_id = jnp.arange(REACH)[None, None, :]
    forward = jnp.where((column == chosen) & (reach_id == 0), PAD, forward)
    column_two = jnp.arange(N_SUB)[:, None]
    slots = []
    for offset in range(-REACH, 0):
        distance = -offset
        shifted = jnp.roll(forward[:, :, distance - 1], distance, axis=0)
        slots.append(jnp.where(column_two >= distance, shifted, 0))
    for offset in range(1, REACH + 1):
        slots.append(jnp.where(column_two < N_SUB - offset, forward[:, :, offset - 1], 0))
    return jnp.stack(slots, axis=-1).astype(jnp.int32)


def level_of(rng, shape, cuts, smallest, high):
    gain = 1.0
    for dim, shards_of in cuts:
        draws = jax.random.uniform(jax.random.fold_in(jax.random.fold_in(rng, 6), dim), (shards_of,), jnp.float32, smallest / len(cuts), high / len(cuts))
        gain = gain * jnp.repeat(jnp.exp(draws), shape[dim] // shards_of).reshape((-1,) + (1,) * (len(shape) - 1 - dim))
    return gain


def setup_inputs(seed: int = 0) -> dict:
    seeds = jax.random.split(jax.random.key(seed), 6)
    return {
        "deflation": draw_deflation(jax.random.fold_in(seeds[5], 71), 0),
        "conductivity": jnp.clip(jnp.exp(math.log(10.0) - 4.6051702 * jax.random.uniform(seeds[1], (COLUMNS, NZ, CX * CY), jnp.float32) ** level_of(seeds[1], (COLUMNS, NZ, CX * CY), ((0, 32), (1, 8)), -0.2, 0.2)), 0.1, 10.0),
        "storage": jnp.clip(jnp.exp(math.log(4.0) - 2.0794415 * jax.random.uniform(seeds[2], (COLUMNS, NZ, CX * CY), jnp.float32) ** level_of(seeds[2], (COLUMNS, NZ, CX * CY), ((0, 32), (1, 8)), -0.2, 0.2)), 0.5, 4.0),
        "interface_rows": draw_interface_rows(jax.random.fold_in(seeds[5], 71), 0),
        "interface_counts": draw_interface_counts(jax.random.fold_in(seeds[5], 71), 0),
    }


highest = lax.Precision.HIGHEST

def harmonic(first, second):
    return 2.0 * first * second / (first + second)

def slot_of(offset):
    return offset + REACH if offset < 0 else offset + REACH - 1

def interior(vectors, sigma_cells, storage_cells):
    width_xy = sigma_cells.shape[1]
    layers = sigma_cells.shape[0]
    position = jnp.arange(width_xy)
    result = storage_cells[None] * vectors
    for stride, at_edge in ((1, position % CX == CX - 1), (CX, position >= width_xy - CX)):
        weights = jnp.where(at_edge[None, :], 0.0, harmonic(sigma_cells, jnp.roll(sigma_cells, -stride, axis=1)))
        flow_term = weights[None] * (jnp.roll(vectors, -stride, axis=2) - vectors)
        result = result - flow_term + jnp.roll(flow_term, stride, axis=2)
    top_layer = (jnp.arange(layers) == layers - 1)[:, None]
    weights = jnp.where(top_layer, 0.0, harmonic(sigma_cells, jnp.roll(sigma_cells, -1, axis=0)))
    flow_term = weights[None] * (jnp.roll(vectors, -1, axis=1) - vectors)
    return result - flow_term + jnp.roll(flow_term, 1, axis=1)

def batch_gram(left, right):
    return jnp.einsum('sgkp,sglp->sgkl', left, right, precision=highest)

def reference(deflation, conductivity, storage, interface_rows, interface_counts):
    groups = N_COARSE
    cells = CZ * CX * CY
    vectors = deflation.reshape(N_SUB, K, groups, CZ, CX * CY).transpose(0, 2, 1, 3, 4)
    sigma_all = conductivity.reshape(N_SUB, groups, CZ, CX * CY)
    storage_all = storage.reshape(N_SUB, groups, CZ, CX * CY)
    applied = jax.vmap(jax.vmap(interior))(vectors, sigma_all, storage_all)
    own_block = jnp.einsum('sgkzx,sglzx->sgkl', vectors, applied, precision=highest)
    top_face = vectors[:, :, :, -1]
    bottom_face = vectors[:, :, :, 0]
    top_sigma = sigma_all[:, :, -1]
    bottom_sigma = sigma_all[:, :, 0]
    above = jnp.concatenate([bottom_face[:, 1:], jnp.zeros_like(bottom_face[:, :1])], axis=1)
    above_sigma = jnp.concatenate([bottom_sigma[:, 1:], jnp.zeros_like(bottom_sigma[:, :1])], axis=1)
    below = jnp.concatenate([jnp.zeros_like(top_face[:, :1]), top_face[:, :-1]], axis=1)
    below_sigma = jnp.concatenate([jnp.zeros_like(top_sigma[:, :1]), top_sigma[:, :-1]], axis=1)
    upper_weight = harmonic(top_sigma, above_sigma)[:, :, None]
    lower_weight = harmonic(bottom_sigma, below_sigma)[:, :, None]
    own_block = own_block + batch_gram(top_face * upper_weight, top_face)
    own_block = own_block + batch_gram(bottom_face * lower_weight, bottom_face)
    upper_block = -batch_gram(top_face * upper_weight, above)
    lower_block = -batch_gram(bottom_face * lower_weight, below)
    flat = vectors.reshape(N_SUB, groups, K, cells)
    flat_sigma = sigma_all.reshape(N_SUB, groups, cells)
    picked = jax.vmap(jax.vmap(lambda table, index: jnp.take(table, index.reshape(-1), axis=1)))(flat, interface_rows)
    picked = picked.reshape(N_SUB, groups, K, 2 * REACH, PAD)
    picked_sigma = jax.vmap(jax.vmap(lambda table, index: jnp.take(table, index.reshape(-1))))(flat_sigma, interface_rows)
    picked_sigma = picked_sigma.reshape(N_SUB, groups, 2 * REACH, PAD)
    column = jnp.arange(N_SUB)
    position = jnp.arange(PAD)
    lateral = [None] * (2 * REACH)
    for offset in list(range(-REACH, 0)) + list(range(1, REACH + 1)):
        slot = slot_of(offset)
        mirror = slot_of(-offset)
        valid = ((column + offset >= 0) & (column + offset < N_SUB)).astype(jnp.float32)
        partner = jnp.roll(picked[:, :, :, mirror], -offset, axis=0) * valid[:, None, None, None]
        partner_sigma = jnp.roll(picked_sigma[:, :, mirror], -offset, axis=0) * valid[:, None, None]
        own_rows = picked[:, :, :, slot]
        live = position[None, None, :] < interface_counts[:, :, slot][:, :, None]
        weights = jnp.where(live, harmonic(picked_sigma[:, :, slot], partner_sigma), 0.0)[:, :, None]
        own_block = own_block + batch_gram(own_rows * weights, own_rows)
        lateral[slot] = -batch_gram(own_rows * weights, partner)
    index_g = jnp.arange(groups)
    diag_mask = (index_g[:, None] == index_g[None, :]).astype(jnp.float32)[None, :, :, None, None]
    upper_mask = (index_g[None, :] == index_g[:, None] + 1).astype(jnp.float32)[None, :, :, None, None]
    lower_mask = (index_g[None, :] == index_g[:, None] - 1).astype(jnp.float32)[None, :, :, None, None]
    blocks = own_block[:, :, None] * diag_mask + upper_block[:, :, None] * upper_mask + lower_block[:, :, None] * lower_mask
    coarse = blocks.transpose(0, 1, 3, 2, 4).reshape(N_SUB, groups * K, groups * K)
    factor = jax.vmap(jnp.linalg.cholesky)(coarse)
    lateral_all = jnp.stack(lateral, axis=2)
    columns_all = lateral_all.transpose(0, 1, 3, 2, 4).reshape(N_SUB, groups, K, 2 * REACH * K)
    right_side = (columns_all[:, :, None] * diag_mask).reshape(N_SUB, groups, groups * K, 2 * REACH * K)

    def solve_column(lower_factor, stacked):
        return jax.vmap(lambda single: lax.linalg.triangular_solve(lower_factor, single, left_side=True, lower=True))(stacked)
    panel = jax.vmap(solve_column)(factor, right_side)
    return (factor, panel)
```

```python
import jax
import jax.numpy as jnp
from jax import lax
from jax.experimental import pallas as pl
from jax.experimental.pallas import tpu as pltpu
from jax.sharding import PartitionSpec as P

K = 64
CX = 16
CY = 32
CZ = 16
FACE = 512
REACH = 4
ROWS = K + 8

f32 = jnp.float32
bf16 = jnp.bfloat16
VMEM = pl.BlockSpec(memory_space=pltpu.VMEM)
SMEM = pl.BlockSpec(memory_space=pltpu.SMEM)
MATRIX = (((1,), (0,)), ((), ()))
GRAM = (((1,), (1,)), ((), ()))


def product(left, right, dims):
    return lax.dot_general(left, right, dims, preferred_element_type=f32)


def harmonic(first, second):
    return 2.0 * first * second / (first + second)


def halves(x):
    high = x.astype(bf16)
    return high, (x - high.astype(f32)).astype(bf16)


def stacked(x):
    return jnp.concatenate(halves(x), axis=0)


def quadrants(square):
    half = square[:K] + square[K:]
    return half[:, :K] + half[:, K:]


def rows_of(vectors, sigma):
    high, low = halves(sigma)
    tail = jnp.concatenate([high.astype(f32), low.astype(f32)], axis=0).astype(bf16)
    return jnp.concatenate([*halves(vectors), tail], axis=0)


def joined(found):
    return jnp.concatenate(
        [found[:K] + found[K : 2 * K], found[2 * K : 2 * K + 8] + found[2 * K + 8 :]], axis=0
    )


def fetch(source, strips, sems):
    copies = [
        pltpu.make_async_copy(source.at[:, pl.ds(128 * q, 128)], strips.at[q], sems.at[q])
        for q in range(4)
    ]
    for copy in copies:
        copy.start()
    return copies


def layer_of(strips, z):
    return jnp.concatenate([strips[q, pl.ds(z, K, stride=CZ), :] for q in range(4)], axis=1)


def pick_kernel(vectors_ref, sigma_ref, index_ref, *outs):
    picked, top_ref, bottom_ref, strips, sems = outs[:8], *outs[8:]
    copies = fetch(vectors_ref, strips, sems)
    lane = lax.broadcasted_iota(jnp.int32, (1, 256), 1)
    within = lane % 128
    cell_of_lane = (within % CY) * CX + jnp.where(lane >= 128, CX - 1, 0)
    cell = lax.broadcasted_iota(jnp.int32, (FACE, 256), 0)
    faces = jnp.zeros((4 * 144, 256), f32)
    for copy in copies:
        copy.wait()
    for step in range(4):
        groups = []
        for group in range(4):
            z = 4 * group + step
            layer = layer_of(strips, z)
            sigma = jnp.broadcast_to(sigma_ref[z : z + 1, :], (8, FACE))
            groups.append(rows_of(layer, sigma))
            if z == 0:
                bottom_ref[...] = jnp.concatenate([layer, sigma], axis=0)
            if z == CZ - 1:
                top_ref[...] = jnp.concatenate([layer, sigma], axis=0)
        chosen = jnp.where(within // CY == step, cell_of_lane, -1)
        select = jnp.where(cell == chosen, 1.0, 0.0).astype(bf16)
        faces = faces + product(jnp.concatenate(groups, axis=0), select, MATRIX)
    place = lax.broadcasted_iota(jnp.int32, (FACE, FACE), 0)
    for side in range(2):
        table = jnp.concatenate(
            [
                faces[144 * group : 144 * (group + 1), 128 * side : 128 * (side + 1)]
                for group in range(4)
            ],
            axis=1,
        ).astype(bf16)
        for slot in range(REACH * side, REACH * (side + 1)):
            cell_index = index_ref[slot : slot + 1, :]
            wanted = (cell_index >> 9) * CY + ((cell_index >> 4) & (CY - 1))
            select = jnp.where(place == wanted, 1.0, 0.0).astype(bf16)
            picked[slot][...] = joined(product(table, select, MATRIX))


def own_kernel(vectors_ref, sigma_ref, storage_ref, own_ref, strips, sems):
    copies = fetch(vectors_ref, strips, sems)
    sigma = sigma_ref[...]
    lane = lax.broadcasted_iota(jnp.int32, (CZ, FACE), 1)
    layer = lax.broadcasted_iota(jnp.int32, (CZ, FACE), 0)
    along_x = jnp.where(
        lane % CX == CX - 1, 0.0, harmonic(sigma, pltpu.roll(sigma, FACE - 1, 1))
    )
    along_y = jnp.where(
        lane >= FACE - CX, 0.0, harmonic(sigma, pltpu.roll(sigma, FACE - CX, 1))
    )
    along_z = jnp.where(layer == CZ - 1, 0.0, harmonic(sigma, pltpu.roll(sigma, CZ - 1, 0)))
    half = 0.5 * (
        storage_ref[...]
        + along_x
        + pltpu.roll(along_x, 1, 1)
        + along_y
        + pltpu.roll(along_y, CX, 1)
        + along_z
        + pltpu.roll(along_z, 1, 0)
    )
    total = jnp.zeros((2 * K, 2 * K), f32)
    for copy in copies:
        copy.wait()
    below = layer_of(strips, 0)
    for z in range(CZ):
        now = below
        applied = half[z : z + 1] * now
        applied = applied - along_x[z : z + 1] * pltpu.roll(now, FACE - 1, 1)
        applied = applied - along_y[z : z + 1] * pltpu.roll(now, FACE - CX, 1)
        if z < CZ - 1:
            below = layer_of(strips, z + 1)
            applied = applied - along_z[z : z + 1] * below
        total = total + product(stacked(now), stacked(applied), GRAM)
    own = quadrants(total)
    own_ref[...] = own + own.T


def weights_of(counts_ref, own_refs, partner_refs):
    place = lax.broadcasted_iota(jnp.int32, (1, FACE), 1)
    result = []
    for slot in range(2 * REACH):
        pair = harmonic(own_refs[slot][K : K + 1, :], partner_refs[slot][K : K + 1, :])
        result.append(jnp.where(place < counts_ref[slot], pair, 0.0))
    return result


def block_kernel(counts_ref, level_ref, own_ref, *refs):
    own_refs, partner_refs = refs[:8], refs[8:16]
    top_ref, bottom_ref, below_ref, above_ref, out_ref = refs[16:]
    weights = weights_of(counts_ref, own_refs, partner_refs)
    total = jnp.zeros((2 * K, 2 * K), f32)
    for slot in range(2 * REACH):
        rows = own_refs[slot][:K, :]
        total = total + product(stacked(rows * weights[slot]), stacked(rows), GRAM)
    top = top_ref[:K, :]
    upward = harmonic(top_ref[K : K + 1, :], above_ref[:1, :])
    total = total + product(stacked(top * upward), stacked(top), GRAM)
    bottom = bottom_ref[:K, :]
    downward = harmonic(bottom_ref[K : K + 1, :], below_ref[K : K + 1, :])
    weighted = stacked(bottom * downward)
    total = total + product(weighted, stacked(bottom), GRAM)
    own = own_ref[...] + quadrants(total)
    own = 0.5 * (own + own.T)
    lower = -quadrants(product(weighted, stacked(below_ref[:K, :]), GRAM))
    even = level_ref[0] % 2 == 0
    payload = jnp.where(
        even, jnp.concatenate([own, lower], axis=1), jnp.concatenate([lower, own], axis=1)
    )
    for copy in range(8):
        out_ref[copy] = payload


def lateral_kernel(counts_ref, *refs):
    own_refs, partner_refs, out_ref = refs[:8], refs[8:16], refs[16]
    weights = weights_of(counts_ref, own_refs, partner_refs)
    blocks = []
    for slot in range(2 * REACH):
        rows = own_refs[slot][:K, :] * -weights[slot]
        blocks.append(quadrants(product(stacked(rows), stacked(partner_refs[slot][:K, :]), GRAM)))
    out_ref[...] = jnp.concatenate(blocks, axis=1)


def eliminate(rows, right, offset, lane, sub):
    factor_rows, inverse_rows = [], []
    wide = (8, 128)
    for panel in range(8):
        first = offset + 8 * panel
        column = [[None] * 16 for _ in range(8)]
        for k in range(8):
            for g in range(panel, 16):
                column[k][g] = jnp.broadcast_to(rows[g][:, first + k : first + k + 1], wide)
        pivot = [[None] * 8 for _ in range(8)]
        for i in range(8):
            for k in range(i, 8):
                pivot[i][k] = jnp.broadcast_to(column[i][panel][k : k + 1, :], wide)
        left_row = [jnp.broadcast_to(rows[panel][k : k + 1, :], wide) for k in range(8)]
        right_row = [jnp.broadcast_to(right[panel][k : k + 1, :], wide) for k in range(8)]
        kept = jnp.zeros(wide, f32)
        kept_right = jnp.zeros(wide, f32)
        for i in range(8):
            scale = lax.rsqrt(pivot[i][i])
            inverse = 1.0 / pivot[i][i]
            kept = jnp.where(sub == i, jnp.where(lane >= first + i, left_row[i], 0.0) * scale if offset == 0 else jnp.where((lane >= first + i) | (lane < 64), left_row[i], 0.0) * scale, kept)
            kept_right = jnp.where(sub == i, right_row[i] * scale, kept_right)
            left_row[i] = left_row[i] * inverse
            right_row[i] = right_row[i] * inverse
            scaled = [None] * 8
            for l in range(i + 1, 8):
                scaled[l] = pivot[i][l] * inverse
            for k in range(8):
                if k == i:
                    continue
                by = pivot[i][k] if k > i else pivot[k][i]
                left_row[k] = left_row[k] - by * left_row[i]
                right_row[k] = right_row[k] - by * right_row[i]
                for l in range(max(i + 1, k), 8):
                    pivot[k][l] = pivot[k][l] - by * scaled[l]
            pivot[i] = scaled
        for g in range(panel + 1, 16):
            for k in range(8):
                rows[g] = rows[g] - column[k][g] * left_row[k]
                right[g] = right[g] - column[k][g] * right_row[k]
        factor_rows.append(kept)
        inverse_rows.append(kept_right)
    return factor_rows, inverse_rows

def chol_kernel(level_ref, blocks_ref, lateral_ref, factor_ref, panel_ref, cross, top, top_right, inverse):
    lane = lax.broadcasted_iota(jnp.int32, (8, 128), 1)
    sub = lax.broadcasted_iota(jnp.int32, (8, 128), 0)
    level = level_ref[0]
    zero = jnp.zeros((64, 128), f32)
    factor_ref[...] = jnp.zeros((512, 512), f32)
    for c in range(1, 8):
        block = blocks_ref[c]
        if c % 2 == 1:
            cross[c - 1] = jnp.concatenate([zero, block], axis=0).T[:64]
        else:
            cross[c - 1] = jnp.concatenate([block, zero], axis=0).T[64:]
    cross[7] = zero
    def unit(g, c):
        return jnp.where((lane == sub + 8 * g) & (level == c), 1.0, 0.0)
    for g in range(8):
        top[pl.ds(8 * g, 8), :] = blocks_ref[0, pl.ds(8 * g, 8), :]
        top_right[pl.ds(8 * g, 8), :] = unit(g, 0)

    @pl.loop(0, 4)
    def _(q):
        c = 2 * q
        last = q == 3
        at = [pl.ds(8 * g, 8) for g in range(8)]
        rows = [jnp.where(lane < 64, top[at[g], :], cross[c, at[g], :]) for g in range(8)]
        rows += [blocks_ref[c + 1, at[g], :] for g in range(8)]
        right = [top_right[at[g], :] for g in range(8)] + [unit(g, c + 1) for g in range(8)]
        even, even_right = eliminate(rows, right, 0, lane, sub)
        nxt = jnp.minimum(c + 2, 7)
        middle = [jnp.where(lane < 64, cross[c + 1, at[g], :], rows[8 + g]) for g in range(8)]
        middle += [jnp.where(last, 0.0, blocks_ref[nxt, at[g], :]) for g in range(8)]
        middle_right = right[8:] + [unit(g, c + 2) for g in range(8)]
        odd, odd_right = eliminate(middle, middle_right, 64, lane, sub)
        for g in range(8):
            top[at[g], :] = middle[8 + g]
            top_right[at[g], :] = middle_right[8 + g]
            inverse[pl.ds(pl.multiple_of(128 * q, 128) + 8 * g, 8), :] = even_right[g]
            inverse[pl.ds(pl.multiple_of(128 * q, 128) + 64 + 8 * g, 8), :] = odd_right[g]
        both = jnp.concatenate(even + odd, axis=0).T
        wide_lane = lax.broadcasted_iota(jnp.int32, (64, 128), 1)
        start = pl.multiple_of(128 * q, 128)
        cols = pl.ds(start, 128)
        factor_ref[pl.ds(start, 64), cols] = jnp.where(wide_lane < 64, both[:64], 0.0)
        factor_ref[pl.ds(start + 64, 64), cols] = both[64:]
        @pl.when(q < 3)
        def _():
            factor_ref[pl.ds(start + 128, 64), cols] = jnp.where(wide_lane < 64, 0.0, both[:64])
    gh, gm = halves(inverse[:, :64])
    bh, bm = halves(lateral_ref[...])
    left = jnp.concatenate([gh, gm, gh], axis=1)
    down = jnp.concatenate([bh, bh, bm], axis=0)
    panel_ref[...] = jnp.dot(left, down, preferred_element_type=f32)


ANYWHERE = pl.BlockSpec(memory_space=pl.ANY)
STRIPS = (pltpu.VMEM((4, K * CZ, 128), f32), pltpu.SemaphoreType.DMA((4,)))


def call(kernel, name, outs, operands, smem=0, anywhere=0, flops=10**8, scratch=()):
    return pl.pallas_call(
        kernel,
        out_shape=outs,
        in_specs=[SMEM] * smem + [ANYWHERE] * anywhere + [VMEM] * (len(operands) - smem - anywhere),
        out_specs=jax.tree.map(lambda _: VMEM, outs),
        scratch_shapes=scratch,
        compiler_params=pltpu.CompilerParams(vmem_limit_bytes=40 * 2**20),
        cost_estimate=pl.CostEstimate(flops=flops, bytes_accessed=2 * 10**6, transcendentals=1000),
        name=name,
    )(*operands)


def array(*shape):
    return jax.ShapeDtypeStruct(shape, f32)


def passed_along(block, axis, distance):
    devices = range(lax.axis_size(axis))
    route = [(i - distance, i) for i in devices if i - distance in devices]
    return lax.ppermute(block, axis, route)


def body(deflation, conductivity, storage, interface_rows, interface_counts):
    vectors = deflation[0].reshape(K * CZ, FACE)
    sigma = conductivity[0]
    counts = interface_counts.reshape(2 * REACH)
    level = lax.axis_index("coarse").reshape(1)
    *picked, top, bottom = call(
        pick_kernel,
        "pick",
        (array(ROWS, FACE),) * 10,
        (vectors, sigma, interface_rows[0, 0]),
        anywhere=1,
        scratch=STRIPS,
    )
    partners = [None] * (2 * REACH)
    for distance in (4, 3, 2, 1):
        ahead, behind = REACH + distance - 1, REACH - distance
        partners[behind] = passed_along(picked[ahead], "sub", distance)
        partners[ahead] = passed_along(picked[behind], "sub", -distance)
    below = passed_along(top, "coarse", 1)
    above = passed_along(bottom[K:], "coarse", -1)
    own = call(own_kernel, "own", array(K, K), (vectors, sigma, storage[0]), anywhere=1, scratch=STRIPS)
    payload = call(
        block_kernel,
        "block",
        array(8, K, 2 * K),
        (counts, level, own, *picked, *partners, top, bottom, below, above),
        smem=2,
    )
    blocks = lax.all_to_all(payload, "coarse", 0, 0)
    lateral = call(
        lateral_kernel, "lateral", array(K, 8 * K), (counts, *picked, *partners), smem=1
    )
    factor, panel = call(
        chol_kernel,
        "factor",
        (array(8 * K, 8 * K), array(8 * K, 8 * K)),
        (level, blocks, lateral),
        smem=1,
        flops=10**9,
        scratch=(
            pltpu.VMEM((8, K, 2 * K), f32),
            pltpu.VMEM((K, 2 * K), f32),
            pltpu.VMEM((K, 2 * K), f32),
            pltpu.VMEM((8 * K, 2 * K), f32),
        ),
    )
    return (factor[None], panel[None, None])


def solution(mesh):
    placed = (
        P("sub", None, "coarse", None),
        P("sub", "coarse", None),
        P("sub", "coarse", None),
        P("sub", "coarse", None, None),
        P("sub", "coarse", None),
    )
    return jax.shard_map(
        body,
        mesh=mesh,
        in_specs=placed,
        out_specs=(P("sub", None, None), P("sub", "coarse", None, None)),
        check_vma=False,
    )
```

```python
import functools

import jax
import jax.numpy as jnp
from jax import lax
from jax.experimental import pallas as pl
from jax.experimental.pallas import tpu as pltpu
from jax.sharding import PartitionSpec as P

K = 64
CX = 16
CY = 32
CZ = 16
FACE = 512
REACH = 4
ROWS = K + 8

f32 = jnp.float32
bf16 = jnp.bfloat16
VMEM = pl.BlockSpec(memory_space=pltpu.VMEM)
SMEM = pl.BlockSpec(memory_space=pltpu.SMEM)
MATRIX = (((1,), (0,)), ((), ()))
GRAM = (((1,), (1,)), ((), ()))


def product(left, right, dims):
    return lax.dot_general(left, right, dims, preferred_element_type=f32)


def harmonic(first, second):
    return 2.0 * first * second / (first + second)


def halves(x):
    high = x.astype(bf16)
    return high, (x - high.astype(f32)).astype(bf16)


def stacked(x):
    return jnp.concatenate(halves(x), axis=0)


def quadrants(square):
    half = square[:K] + square[K:]
    return half[:, :K] + half[:, K:]


def rows_of(vectors, sigma):
    high, low = halves(sigma)
    tail = jnp.concatenate([high.astype(f32), low.astype(f32)], axis=0).astype(bf16)
    return jnp.concatenate([*halves(vectors), tail], axis=0)


def joined(found):
    return jnp.concatenate(
        [found[:K] + found[K : 2 * K], found[2 * K : 2 * K + 8] + found[2 * K + 8 :]], axis=0
    )


def layer_of(strips, z):
    return jnp.concatenate([strips[q, pl.ds(z, K, stride=CZ), :] for q in range(4)], axis=1)


def pick_kernel(vectors_hbm, sigma_hbm, index_hbm, strips, own_ref, ahead_ref, behind_ref, top_ref, bottom_ref, first_ref, sigma_ref, index_ref, sems):
    copies = [
        pltpu.make_async_copy(vectors_hbm.at[:, pl.ds(128 * q, 128)], strips.at[q], sems.at[q])
        for q in range(4)
    ]
    copies.append(pltpu.make_async_copy(sigma_hbm, sigma_ref, sems.at[4]))
    copies.append(pltpu.make_async_copy(index_hbm, index_ref, sems.at[5]))
    for copy in copies:
        copy.start()
    lane = lax.broadcasted_iota(jnp.int32, (1, 256), 1)
    within = lane % 128
    cell_of_lane = (within % CY) * CX + jnp.where(lane >= 128, CX - 1, 0)
    cell = lax.broadcasted_iota(jnp.int32, (FACE, 256), 0)
    faces = jnp.zeros((4 * 144, 256), f32)
    for copy in copies:
        copy.wait()
    for step in range(4):
        groups = []
        for group in range(4):
            z = 4 * group + step
            layer = layer_of(strips, z)
            sigma = jnp.broadcast_to(sigma_ref[z : z + 1, :], (8, FACE))
            groups.append(rows_of(layer, sigma))
            if z == 0:
                bottom_ref[...] = jnp.concatenate([layer, sigma], axis=0)
                first_ref[...] = sigma
            if z == CZ - 1:
                top_ref[...] = jnp.concatenate([layer, sigma], axis=0)
        chosen = jnp.where(within // CY == step, cell_of_lane, -1)
        select = jnp.where(cell == chosen, 1.0, 0.0).astype(bf16)
        faces = faces + product(jnp.concatenate(groups, axis=0), select, MATRIX)
    place = lax.broadcasted_iota(jnp.int32, (FACE, FACE), 0)
    for side in range(2):
        wide = jnp.concatenate(
            [
                faces[144 * group : 144 * (group + 1), 128 * side : 128 * (side + 1)]
                for group in range(4)
            ],
            axis=1,
        )
        table = wide.astype(bf16)
        out_ref = ahead_ref if side else behind_ref
        out_ref[:K] = wide[:K] + wide[K : 2 * K]
        for slot in range(REACH * side, REACH * (side + 1)):
            cell_index = index_ref[slot : slot + 1, :]
            wanted = (cell_index >> 9) * CY + ((cell_index >> 4) & (CY - 1))
            select = jnp.where(place == wanted, 1.0, 0.0).astype(bf16)
            found = product(table, select, MATRIX)
            own_ref[slot] = found[: 2 * K].astype(bf16)
            reach = slot - REACH if side else REACH - 1 - slot
            out_ref[K + reach : K + reach + 1] = found[2 * K : 2 * K + 1] + found[2 * K + 8 : 2 * K + 9]
            out_ref[K + 4 + reach : K + 5 + reach] = wanted.astype(f32)


def own_kernel(strips, sigma_ref, storage_ref, top_ref, bottom_ref, below_ref, above_ref, own_ref, lower_ref):
    sigma = sigma_ref[...]
    lane = lax.broadcasted_iota(jnp.int32, (CZ, FACE), 1)
    layer = lax.broadcasted_iota(jnp.int32, (CZ, FACE), 0)
    along_x = jnp.where(
        lane % CX == CX - 1, 0.0, harmonic(sigma, pltpu.roll(sigma, FACE - 1, 1))
    )
    along_y = jnp.where(
        lane >= FACE - CX, 0.0, harmonic(sigma, pltpu.roll(sigma, FACE - CX, 1))
    )
    along_z = jnp.where(layer == CZ - 1, 0.0, harmonic(sigma, pltpu.roll(sigma, CZ - 1, 0)))
    downward = harmonic(bottom_ref[K : K + 1, :], below_ref[K : K + 1, :])
    upward = harmonic(top_ref[K : K + 1, :], above_ref[:1, :])
    half = 0.5 * (
        storage_ref[...]
        + along_x
        + pltpu.roll(along_x, 1, 1)
        + along_y
        + pltpu.roll(along_y, CX, 1)
        + along_z
        + pltpu.roll(along_z, 1, 0)
        + jnp.where(layer == 0, downward, 0.0)
        + jnp.where(layer == CZ - 1, upward, 0.0)
    )
    total = jnp.zeros((2 * K, 2 * K), f32)
    below = layer_of(strips, 0)
    for z in range(CZ):
        now = below
        applied = half[z : z + 1] * now
        applied = applied - along_x[z : z + 1] * pltpu.roll(now, FACE - 1, 1)
        applied = applied - along_y[z : z + 1] * pltpu.roll(now, FACE - CX, 1)
        if z < CZ - 1:
            below = layer_of(strips, z + 1)
            applied = applied - along_z[z : z + 1] * below
        total = total + product(stacked(now), stacked(applied), GRAM)
    own = quadrants(total)
    own_ref[...] = own + own.T
    weighted = stacked(bottom_ref[:K, :] * downward)
    lower_ref[...] = -quadrants(product(weighted, stacked(below_ref[:K, :]), GRAM))


def pack_kernel(core_ref, ahead, behind, ahead2, behind2, ahead4, behind4, out_ref, *, rows):
    count = rows.stop - rows.start
    for core, chosen in ((0, (ahead, ahead2, behind2, behind4)), (1, (ahead2, ahead4, behind, behind2))):
        @pl.when(core_ref[0] == core)
        def _(chosen=chosen):
            for at, ref in enumerate(chosen):
                out_ref[count * at : count * (at + 1)] = ref[rows]


def partner_tail(refs, offset):
    ahead2, behind2, ahead4, behind4, tails = refs
    if offset % 2:
        at = {-1: 0, -3: 1, 1: 2, 3: 3}[offset]
        return tails[8 * at : 8 * at + 8]
    return {-2: ahead2, -4: ahead4, 2: behind2, 4: behind4}[offset][K : K + 8]


def partner_face(refs, offset):
    ahead2, behind2, ahead4, behind4, faces = refs
    if offset % 2:
        at = {-1: 0, -3: 1, 1: 2, 3: 3}[offset]
        return faces[K * at : K * at + K]
    return {-2: ahead2, -4: ahead4, 2: behind2, 4: behind4}[offset][:K]


OFFSETS = (-4, -3, -2, -1, 1, 2, 3, 4)


def weight_of(counts_ref, ahead, behind, slot, tail):
    offset = OFFSETS[slot]
    reach = abs(offset) - 1
    place = lax.broadcasted_iota(jnp.int32, (1, FACE), 1)
    mine = (ahead if offset > 0 else behind)[K + reach : K + reach + 1]
    pair = harmonic(mine, tail[reach : reach + 1])
    return jnp.where(place < counts_ref[slot], pair, 0.0)


def weighted_rows(own_ref, slot, weight):
    rows = own_ref[slot]
    return stacked((rows[:K].astype(f32) + rows[K:].astype(f32)) * weight)


def block_kernel(counts_ref, level_ref, own_block, lower_block, own_ref, ahead, behind, *refs):
    *partners, out_ref = refs
    total = jnp.zeros((2 * K, 2 * K), f32)
    for slot, offset in enumerate(OFFSETS):
        weight = weight_of(counts_ref, ahead, behind, slot, partner_tail(partners, offset))
        total = total + product(weighted_rows(own_ref, slot, weight), own_ref[slot], GRAM)
    extra = quadrants(total)
    own = own_block[...] + 0.5 * (extra + extra.T)
    lower = lower_block[...]
    even = level_ref[0] % 2 == 0
    payload = jnp.where(
        even, jnp.concatenate([own, lower], axis=1), jnp.concatenate([lower, own], axis=1)
    )
    for copy in range(8):
        out_ref[copy] = payload


def lateral_kernel(counts_ref, own_ref, ahead, behind, ahead2, behind2, ahead4, behind4, tails, faces, out_ref):
    place = lax.broadcasted_iota(jnp.int32, (FACE, FACE), 0).astype(f32)
    blocks = []
    for slot, offset in enumerate(OFFSETS):
        tail = partner_tail((ahead2, behind2, ahead4, behind4, tails), offset)
        face = partner_face((ahead2, behind2, ahead4, behind4, faces), offset)
        weight = weight_of(counts_ref, ahead, behind, slot, tail)
        reach = abs(offset) - 1
        select = jnp.where(place == tail[4 + reach : 5 + reach], 1.0, 0.0).astype(bf16)
        found = product(stacked(face), select, MATRIX).astype(bf16)
        blocks.append(quadrants(product(weighted_rows(own_ref, slot, -weight), found, GRAM)))
    out_ref[...] = jnp.concatenate(blocks, axis=1)


def eliminate(rows, right, offset, lane, sub):
    factor_rows, inverse_rows = [], []
    wide = (8, 128)
    for panel in range(8):
        first = offset + 8 * panel
        column = [[None] * 16 for _ in range(8)]
        for k in range(8):
            for g in range(panel, 16):
                column[k][g] = jnp.broadcast_to(rows[g][:, first + k : first + k + 1], wide)
        pivot = [[None] * 8 for _ in range(8)]
        for i in range(8):
            for k in range(i, 8):
                pivot[i][k] = jnp.broadcast_to(column[i][panel][k : k + 1, :], wide)
        left_row = [jnp.broadcast_to(rows[panel][k : k + 1, :], wide) for k in range(8)]
        right_row = [jnp.broadcast_to(right[panel][k : k + 1, :], wide) for k in range(8)]
        kept = jnp.zeros(wide, f32)
        kept_right = jnp.zeros(wide, f32)
        for i in range(8):
            scale = lax.rsqrt(pivot[i][i])
            inverse = 1.0 / pivot[i][i]
            kept = jnp.where(sub == i, jnp.where(lane >= first + i, left_row[i], 0.0) * scale if offset == 0 else jnp.where((lane >= first + i) | (lane < 64), left_row[i], 0.0) * scale, kept)
            kept_right = jnp.where(sub == i, right_row[i] * scale, kept_right)
            left_row[i] = left_row[i] * inverse
            right_row[i] = right_row[i] * inverse
            scaled = [None] * 8
            for l in range(i + 1, 8):
                scaled[l] = pivot[i][l] * inverse
            for k in range(8):
                if k == i:
                    continue
                by = pivot[i][k] if k > i else pivot[k][i]
                left_row[k] = left_row[k] - by * left_row[i]
                right_row[k] = right_row[k] - by * right_row[i]
                for l in range(max(i + 1, k), 8):
                    pivot[k][l] = pivot[k][l] - by * scaled[l]
            pivot[i] = scaled
        for g in range(panel + 1, 16):
            for k in range(8):
                rows[g] = rows[g] - column[k][g] * left_row[k]
                right[g] = right[g] - column[k][g] * right_row[k]
        factor_rows.append(kept)
        inverse_rows.append(kept_right)
    return factor_rows, inverse_rows

def chol_kernel(level_ref, blocks_ref, lateral_ref, factor_ref, panel_ref, cross, top, top_right, inverse):
    lane = lax.broadcasted_iota(jnp.int32, (8, 128), 1)
    sub = lax.broadcasted_iota(jnp.int32, (8, 128), 0)
    level = level_ref[0]
    zero = jnp.zeros((64, 128), f32)
    factor_ref[...] = jnp.zeros((512, 512), f32)
    for c in range(1, 8):
        block = blocks_ref[c]
        if c % 2 == 1:
            cross[c - 1] = jnp.concatenate([zero, block], axis=0).T[:64]
        else:
            cross[c - 1] = jnp.concatenate([block, zero], axis=0).T[64:]
    cross[7] = zero
    def unit(g, c):
        return jnp.where((lane == sub + 8 * g) & (level == c), 1.0, 0.0)
    for g in range(8):
        top[pl.ds(8 * g, 8), :] = blocks_ref[0, pl.ds(8 * g, 8), :]
        top_right[pl.ds(8 * g, 8), :] = unit(g, 0)

    @pl.loop(0, 4)
    def _(q):
        c = 2 * q
        last = q == 3
        at = [pl.ds(8 * g, 8) for g in range(8)]
        rows = [jnp.where(lane < 64, top[at[g], :], cross[c, at[g], :]) for g in range(8)]
        rows += [blocks_ref[c + 1, at[g], :] for g in range(8)]
        right = [top_right[at[g], :] for g in range(8)] + [unit(g, c + 1) for g in range(8)]
        even, even_right = eliminate(rows, right, 0, lane, sub)
        nxt = jnp.minimum(c + 2, 7)
        middle = [jnp.where(lane < 64, cross[c + 1, at[g], :], rows[8 + g]) for g in range(8)]
        middle += [jnp.where(last, 0.0, blocks_ref[nxt, at[g], :]) for g in range(8)]
        middle_right = right[8:] + [unit(g, c + 2) for g in range(8)]
        odd, odd_right = eliminate(middle, middle_right, 64, lane, sub)
        for g in range(8):
            top[at[g], :] = middle[8 + g]
            top_right[at[g], :] = middle_right[8 + g]
            inverse[pl.ds(pl.multiple_of(128 * q, 128) + 8 * g, 8), :] = even_right[g]
            inverse[pl.ds(pl.multiple_of(128 * q, 128) + 64 + 8 * g, 8), :] = odd_right[g]
        both = jnp.concatenate(even + odd, axis=0).T
        wide_lane = lax.broadcasted_iota(jnp.int32, (64, 128), 1)
        start = pl.multiple_of(128 * q, 128)
        cols = pl.ds(start, 128)
        factor_ref[pl.ds(start, 64), cols] = jnp.where(wide_lane < 64, both[:64], 0.0)
        factor_ref[pl.ds(start + 64, 64), cols] = both[64:]
        @pl.when(q < 3)
        def _():
            factor_ref[pl.ds(start + 128, 64), cols] = jnp.where(wide_lane < 64, 0.0, both[:64])
    gh, gm = halves(inverse[:, :64])
    bh, bm = halves(lateral_ref[...])
    left = jnp.concatenate([gh, gm, gh], axis=1)
    down = jnp.concatenate([bh, bh, bm], axis=0)
    panel_ref[...] = jnp.dot(left, down, preferred_element_type=f32)


HBM = pl.BlockSpec(memory_space=pltpu.HBM)


def call(kernel, name, outs, operands, smem=0, hbm=0, flops=10**8, scratch=(), limit=16):
    return pl.pallas_call(
        kernel,
        out_shape=outs,
        in_specs=[SMEM] * smem + [HBM] * hbm + [VMEM] * (len(operands) - smem - hbm),
        out_specs=jax.tree.map(lambda _: VMEM, outs),
        scratch_shapes=scratch,
        compiler_params=pltpu.CompilerParams(vmem_limit_bytes=limit * 2**20),
        cost_estimate=pl.CostEstimate(flops=flops, bytes_accessed=2 * 10**6, transcendentals=1000),
        name=name,
    )(*operands)


def array(*shape, dtype=f32):
    return jax.ShapeDtypeStruct(shape, dtype)


def passed_along(block, axis, distance):
    devices = range(lax.axis_size(axis))
    route = [(i - distance, i) for i in devices if i - distance in devices]
    return lax.ppermute(block, axis, route)


def body(deflation, conductivity, storage, interface_rows, interface_counts):
    vectors = deflation[0].reshape(K * CZ, FACE)
    sigma = conductivity[0]
    counts = interface_counts.reshape(2 * REACH)
    level = lax.axis_index("coarse").reshape(1)
    core = (lax.axis_index("sub") % 2).reshape(1)
    strips, mine, ahead, behind, top, bottom, first = call(
        pick_kernel,
        "pick",
        (
            array(4, K * CZ, 128),
            array(8, 2 * K, FACE, dtype=bf16),
            array(ROWS, FACE),
            array(ROWS, FACE),
            array(ROWS, FACE),
            array(ROWS, FACE),
            array(8, FACE),
        ),
        tuple(
            pltpu.with_memory_space_constraint(x, pltpu.HBM)
            for x in (vectors, sigma, interface_rows[0, 0])
        ),
        hbm=3,
        scratch=(
            pltpu.VMEM((CZ, FACE), f32),
            pltpu.VMEM((2 * REACH, FACE), jnp.int32),
            pltpu.SemaphoreType.DMA((6,)),
        ),
    )
    below = passed_along(top, "coarse", 1)
    above = passed_along(first, "coarse", -1)
    ahead4 = passed_along(ahead, "sub", 4)
    behind4 = passed_along(behind, "sub", -4)
    ahead2 = passed_along(ahead, "sub", 2)
    behind2 = passed_along(behind, "sub", -2)
    own, lower = call(
        own_kernel,
        "own",
        (array(K, K), array(K, K)),
        (strips, sigma, storage[0], top, bottom, below, above),
    )
    direct = (ahead2, behind2, ahead4, behind4)

    def swapped(name, rows, after):
        kernel = functools.partial(pack_kernel, rows=rows)
        sent, after = lax.optimization_barrier(((core, ahead, behind, *direct), after))
        packed = call(
            kernel, name, array(4 * (rows.stop - rows.start), FACE), sent, smem=1, flops=10**6
        )
        route = [(i, i ^ 1) for i in range(lax.axis_size("sub"))]
        return lax.ppermute(packed, "sub", route), after

    tails, (own, lower) = swapped("tails", slice(K, ROWS), (own, lower))
    payload = call(
        block_kernel,
        "block",
        array(8, K, 2 * K),
        (counts, level, own, lower, mine, ahead, behind, *direct, tails),
        smem=2,
    )
    faces, payload = swapped("faces", slice(0, K), payload)
    blocks = lax.all_to_all(payload, "coarse", 0, 0)
    lateral = call(
        lateral_kernel,
        "lateral",
        array(K, 8 * K),
        (counts, mine, ahead, behind, *direct, tails, faces),
        smem=1,
    )
    factor, panel = call(
        chol_kernel,
        "factor",
        (array(8 * K, 8 * K), array(8 * K, 8 * K)),
        (level, blocks, lateral),
        smem=1,
        flops=10**9,
        scratch=(
            pltpu.VMEM((8, K, 2 * K), f32),
            pltpu.VMEM((K, 2 * K), f32),
            pltpu.VMEM((K, 2 * K), f32),
            pltpu.VMEM((8 * K, 2 * K), f32),
        ),
    )
    return (factor[None], panel[None, None])


def solution(mesh):
    placed = (
        P("sub", None, "coarse", None),
        P("sub", "coarse", None),
        P("sub", "coarse", None),
        P("sub", "coarse", None, None),
        P("sub", "coarse", None),
    )
    return jax.shard_map(
        body,
        mesh=mesh,
        in_specs=placed,
        out_specs=(P("sub", None, None), P("sub", "coarse", None, None)),
        check_vma=False,
    )
```

```python
import functools

import jax
import jax.numpy as jnp
from jax import lax
from jax.experimental import pallas as pl
from jax.experimental.pallas import tpu as pltpu
from jax.sharding import PartitionSpec as P

K = 64
CX = 16
CY = 32
CZ = 16
FACE = 512
REACH = 4
ROWS = K + 8

f32 = jnp.float32
bf16 = jnp.bfloat16
VMEM = pl.BlockSpec(memory_space=pltpu.VMEM)
MATRIX = (((1,), (0,)), ((), ()))
GRAM = (((1,), (1,)), ((), ()))


def product(left, right, dims):
    return lax.dot_general(left, right, dims, preferred_element_type=f32)


def harmonic(first, second):
    return 2.0 * first * second / (first + second)


def halves(x):
    high = x.astype(bf16)
    return high, (x - high.astype(f32)).astype(bf16)


def stacked(x):
    return jnp.concatenate(halves(x), axis=0)


def quadrants(square):
    half = square[:K] + square[K:]
    return half[:, :K] + half[:, K:]


def rows_of(vectors, sigma):
    high, low = halves(sigma)
    tail = jnp.concatenate([high.astype(f32), low.astype(f32)], axis=0).astype(bf16)
    return jnp.concatenate([*halves(vectors), tail], axis=0)


def joined(found):
    return jnp.concatenate(
        [found[:K] + found[K : 2 * K], found[2 * K : 2 * K + 8] + found[2 * K + 8 :]], axis=0
    )


def layer_of(strips, z):
    return jnp.concatenate([strips[q, pl.ds(z, K, stride=CZ), :] for q in range(4)], axis=1)


def pick_kernel(vectors_hbm, sigma_hbm, index_hbm, counts_hbm, strips, own_ref, ahead_ref, behind_ref, ahead_tail, behind_tail, top_ref, bottom_ref, first_ref, live_ref, sigma_ref, index_ref, counts_ref, sems):
    copies = [
        pltpu.make_async_copy(vectors_hbm.at[:, pl.ds(128 * q, 128)], strips.at[q], sems.at[q])
        for q in range(4)
    ]
    copies.append(pltpu.make_async_copy(sigma_hbm, sigma_ref, sems.at[4]))
    copies.append(pltpu.make_async_copy(index_hbm, index_ref, sems.at[5]))
    copies.append(pltpu.make_async_copy(counts_hbm, counts_ref, sems.at[6]))
    for copy in copies:
        copy.start()
    lane = lax.broadcasted_iota(jnp.int32, (1, 256), 1)
    within = lane % 128
    cell_of_lane = (within % CY) * CX + jnp.where(lane >= 128, CX - 1, 0)
    cell = lax.broadcasted_iota(jnp.int32, (FACE, 256), 0)
    faces = jnp.zeros((4 * 144, 256), f32)
    for copy in copies:
        copy.wait()
    for step in range(4):
        groups = []
        for group in range(4):
            z = 4 * group + step
            layer = layer_of(strips, z)
            sigma = jnp.broadcast_to(sigma_ref[z : z + 1, :], (8, FACE))
            groups.append(rows_of(layer, sigma))
            if z == 0:
                bottom_ref[...] = jnp.concatenate([layer, sigma], axis=0)
                first_ref[...] = sigma
            if z == CZ - 1:
                top_ref[...] = jnp.concatenate([layer, sigma], axis=0)
        chosen = jnp.where(within // CY == step, cell_of_lane, -1)
        select = jnp.where(cell == chosen, 1.0, 0.0).astype(bf16)
        faces = faces + product(jnp.concatenate(groups, axis=0), select, MATRIX)
    along = lax.broadcasted_iota(jnp.int32, (1, FACE), 1)
    for slot in range(2 * REACH):
        live_ref[slot : slot + 1] = jnp.where(along < counts_ref[slot], 1.0, 0.0)
    place = lax.broadcasted_iota(jnp.int32, (FACE, FACE), 0)
    for side in range(2):
        wide = jnp.concatenate(
            [
                faces[144 * group : 144 * (group + 1), 128 * side : 128 * (side + 1)]
                for group in range(4)
            ],
            axis=1,
        )
        table = wide.astype(bf16)
        face_ref, tail_ref = (ahead_ref, ahead_tail) if side else (behind_ref, behind_tail)
        face_ref[...] = wide[:K] + wide[K : 2 * K]
        for slot in range(REACH * side, REACH * (side + 1)):
            cell_index = index_ref[slot : slot + 1, :]
            wanted = (cell_index >> 9) * CY + ((cell_index >> 4) & (CY - 1))
            select = jnp.where(place == wanted, 1.0, 0.0).astype(bf16)
            found = product(table, select, MATRIX)
            own_ref[slot] = found[: 2 * K].astype(bf16)
            reach = slot - REACH if side else REACH - 1 - slot
            tail_ref[reach : reach + 1] = found[2 * K : 2 * K + 1] + found[2 * K + 8 : 2 * K + 9]
            tail_ref[4 + reach : 5 + reach] = wanted.astype(f32)


def own_kernel(strips, sigma_ref, storage_ref, top_ref, bottom_ref, below_ref, above_ref, own_ref, lower_ref):
    sigma = sigma_ref[...]
    lane = lax.broadcasted_iota(jnp.int32, (CZ, FACE), 1)
    layer = lax.broadcasted_iota(jnp.int32, (CZ, FACE), 0)
    along_x = jnp.where(
        lane % CX == CX - 1, 0.0, harmonic(sigma, pltpu.roll(sigma, FACE - 1, 1))
    )
    along_y = jnp.where(
        lane >= FACE - CX, 0.0, harmonic(sigma, pltpu.roll(sigma, FACE - CX, 1))
    )
    along_z = jnp.where(layer == CZ - 1, 0.0, harmonic(sigma, pltpu.roll(sigma, CZ - 1, 0)))
    downward = harmonic(bottom_ref[K : K + 1, :], below_ref[K : K + 1, :])
    upward = harmonic(top_ref[K : K + 1, :], above_ref[:1, :])
    half = 0.5 * (
        storage_ref[...]
        + along_x
        + pltpu.roll(along_x, 1, 1)
        + along_y
        + pltpu.roll(along_y, CX, 1)
        + along_z
        + pltpu.roll(along_z, 1, 0)
        + jnp.where(layer == 0, downward, 0.0)
        + jnp.where(layer == CZ - 1, upward, 0.0)
    )
    total = jnp.zeros((2 * K, 2 * K), f32)
    below = layer_of(strips, 0)
    for z in range(CZ):
        now = below
        applied = half[z : z + 1] * now
        applied = applied - along_x[z : z + 1] * pltpu.roll(now, FACE - 1, 1)
        applied = applied - along_y[z : z + 1] * pltpu.roll(now, FACE - CX, 1)
        if z < CZ - 1:
            below = layer_of(strips, z + 1)
            applied = applied - along_z[z : z + 1] * below
        total = total + product(stacked(now), stacked(applied), GRAM)
    own = quadrants(total)
    own_ref[...] = own + own.T
    weighted = stacked(bottom_ref[:K, :] * downward)
    lower_ref[...] = -quadrants(product(weighted, stacked(below_ref[:K, :]), GRAM))


def pack_kernel(ahead, behind, ahead2, behind2, ahead4, behind4, out_ref):
    count = ahead.shape[0]
    mine = lax.axis_index("sub") % 2
    for core, chosen in ((0, (ahead, ahead2, behind2, behind4)), (1, (ahead2, ahead4, behind, behind2))):
        @pl.when(mine == core)
        def _(chosen=chosen):
            for at, ref in enumerate(chosen):
                out_ref[count * at : count * (at + 1)] = ref[...]


OFFSETS = (-4, -3, -2, -1, 1, 2, 3, 4)


def partner(refs, offset):
    ahead2, behind2, ahead4, behind4, swapped = refs
    if offset % 2:
        at = {-1: 0, -3: 1, 1: 2, 3: 3}[offset]
        count = ahead2.shape[0]
        return swapped[count * at : count * at + count]
    return {-2: ahead2, -4: ahead4, 2: behind2, 4: behind4}[offset][...]


def weight_of(live_ref, ahead_tail, behind_tail, slot, tail):
    offset = OFFSETS[slot]
    reach = abs(offset) - 1
    mine = (ahead_tail if offset > 0 else behind_tail)[reach : reach + 1]
    pair = harmonic(mine, tail[reach : reach + 1])
    return jnp.where(live_ref[slot : slot + 1] > 0.0, pair, 0.0)


def weighted_rows(own_ref, slot, weight):
    rows = own_ref[slot]
    return stacked((rows[:K].astype(f32) + rows[K:].astype(f32)) * weight)


def block_kernel(live_ref, own_block, lower_block, own_ref, ahead, behind, *refs):
    *tails, out_ref = refs
    total = jnp.zeros((2 * K, 2 * K), f32)
    for slot, offset in enumerate(OFFSETS):
        weight = weight_of(live_ref, ahead, behind, slot, partner(tails, offset))
        total = total + product(weighted_rows(own_ref, slot, weight), own_ref[slot], GRAM)
    extra = quadrants(total)
    own = own_block[...] + 0.5 * (extra + extra.T)
    lower = lower_block[...]
    even = lax.axis_index("coarse") % 2 == 0
    payload = jnp.where(
        even, jnp.concatenate([own, lower], axis=1), jnp.concatenate([lower, own], axis=1)
    )
    for copy in range(8):
        out_ref[copy] = payload


def panel_kernel(live_ref, own_ref, ahead, behind, *refs):
    tails, faces, inverse, out_ref = refs[:5], refs[5:10], refs[10], refs[11]
    place = lax.broadcasted_iota(jnp.int32, (FACE, FACE), 0).astype(f32)
    blocks = []
    for slot, offset in enumerate(OFFSETS):
        tail = partner(tails, offset)
        weight = weight_of(live_ref, ahead, behind, slot, tail)
        reach = abs(offset) - 1
        select = jnp.where(place == tail[4 + reach : 5 + reach], 1.0, 0.0).astype(bf16)
        found = product(stacked(partner(faces, offset)), select, MATRIX).astype(bf16)
        blocks.append(quadrants(product(weighted_rows(own_ref, slot, -weight), found, GRAM)))
    high, low = halves(jnp.concatenate(blocks, axis=1))
    left_high, left_low = halves(inverse[:, :K])
    left = jnp.concatenate([left_high, left_low, left_high], axis=1)
    out_ref[...] = product(left, jnp.concatenate([high, high, low], axis=0), MATRIX)


def eliminate(rows, right, offset, lane, sub):
    factor_rows, inverse_rows = [], []
    wide = (8, 128)
    for panel in range(8):
        first = offset + 8 * panel
        column = [[None] * 16 for _ in range(8)]
        for k in range(8):
            for g in range(panel, 16):
                column[k][g] = jnp.broadcast_to(rows[g][:, first + k : first + k + 1], wide)
        pivot = [[None] * 8 for _ in range(8)]
        for i in range(8):
            for k in range(i, 8):
                pivot[i][k] = jnp.broadcast_to(column[i][panel][k : k + 1, :], wide)
        left_row = [jnp.broadcast_to(rows[panel][k : k + 1, :], wide) for k in range(8)]
        right_row = [jnp.broadcast_to(right[panel][k : k + 1, :], wide) for k in range(8)]
        kept = jnp.zeros(wide, f32)
        kept_right = jnp.zeros(wide, f32)
        for i in range(8):
            scale = lax.rsqrt(pivot[i][i])
            inverse = 1.0 / pivot[i][i]
            kept = jnp.where(sub == i, jnp.where(lane >= first + i, left_row[i], 0.0) * scale if offset == 0 else jnp.where((lane >= first + i) | (lane < 64), left_row[i], 0.0) * scale, kept)
            kept_right = jnp.where(sub == i, right_row[i] * scale, kept_right)
            left_row[i] = left_row[i] * inverse
            right_row[i] = right_row[i] * inverse
            scaled = [None] * 8
            for l in range(i + 1, 8):
                scaled[l] = pivot[i][l] * inverse
            for k in range(8):
                if k == i:
                    continue
                by = pivot[i][k] if k > i else pivot[k][i]
                left_row[k] = left_row[k] - by * left_row[i]
                right_row[k] = right_row[k] - by * right_row[i]
                for l in range(max(i + 1, k), 8):
                    pivot[k][l] = pivot[k][l] - by * scaled[l]
            pivot[i] = scaled
        for g in range(panel + 1, 16):
            for k in range(8):
                rows[g] = rows[g] - column[k][g] * left_row[k]
                right[g] = right[g] - column[k][g] * right_row[k]
        factor_rows.append(kept)
        inverse_rows.append(kept_right)
    return factor_rows, inverse_rows

def half_factor(begin, level, blocks_ref, factor_ref, cross, top, top_right, inverse):
    lane = lax.broadcasted_iota(jnp.int32, (8, 128), 1)
    sub = lax.broadcasted_iota(jnp.int32, (8, 128), 0)
    wide_lane = lax.broadcasted_iota(jnp.int32, (K, 2 * K), 1)
    zero = jnp.zeros((K, 2 * K), f32)
    at = [pl.ds(8 * g, 8) for g in range(8)]
    for c in range(4 * begin + 1, min(4 * begin + 5, 8)):
        block = blocks_ref[c]
        if c % 2 == 1:
            cross[c - 1] = jnp.concatenate([zero, block], axis=0).T[:K]
        else:
            cross[c - 1] = jnp.concatenate([block, zero], axis=0).T[K:]
    if begin:
        cross[7] = zero

    def unit(g, c):
        return jnp.where((lane == sub + 8 * g) & (level == c), 1.0, 0.0)

    if not begin:
        for g in range(8):
            top[at[g], :] = blocks_ref[0, at[g], :]
            top_right[at[g], :] = unit(g, 0)

    @pl.loop(2 * begin, 2 * begin + 2)
    def _(q):
        c = 2 * q
        last = q == 3
        rows = [jnp.where(lane < K, top[at[g], :], cross[c, at[g], :]) for g in range(8)]
        rows += [blocks_ref[c + 1, at[g], :] for g in range(8)]
        right = [top_right[at[g], :] for g in range(8)] + [unit(g, c + 1) for g in range(8)]
        even, even_right = eliminate(rows, right, 0, lane, sub)
        following = jnp.minimum(c + 2, 7)
        middle = [jnp.where(lane < K, cross[c + 1, at[g], :], rows[8 + g]) for g in range(8)]
        middle += [jnp.where(last, 0.0, blocks_ref[following, at[g], :]) for g in range(8)]
        middle_right = right[8:] + [unit(g, c + 2) for g in range(8)]
        odd, odd_right = eliminate(middle, middle_right, K, lane, sub)
        start = pl.multiple_of(128 * q, 128)
        for g in range(8):
            top[at[g], :] = middle[8 + g]
            top_right[at[g], :] = middle_right[8 + g]
            inverse[pl.ds(start + 8 * g, 8), :] = even_right[g]
            inverse[pl.ds(start + K + 8 * g, 8), :] = odd_right[g]
        both = jnp.concatenate(even + odd, axis=0).T
        cols = pl.ds(start, 128)
        factor_ref[pl.ds(start, K), cols] = jnp.where(wide_lane < K, both[:K], 0.0)
        factor_ref[pl.ds(start + K, K), cols] = both[K:]

        @pl.when(q < 3)
        def _():
            factor_ref[pl.ds(start + 128, K), cols] = jnp.where(wide_lane < K, 0.0, both[:K])


def first_half(blocks_ref, factor_ref, inverse, top, top_right, cross):
    factor_ref[...] = jnp.zeros((5 * K, 4 * K), f32)
    half_factor(0, lax.axis_index("coarse"), blocks_ref, factor_ref, cross, top, top_right, inverse)


def second_half(blocks_ref, part_ref, first_inverse, first_top, first_right, factor_ref, inverse, cross, top, top_right):
    factor_ref[: 5 * K, : 4 * K] = part_ref[...]
    factor_ref[5 * K :, : 4 * K] = jnp.zeros((3 * K, 4 * K), f32)
    factor_ref[:, 4 * K :] = jnp.zeros((8 * K, 4 * K), f32)
    inverse[: 4 * K, :] = first_inverse[...]
    top[...] = first_top[...]
    top_right[...] = first_right[...]
    half_factor(1, lax.axis_index("coarse"), blocks_ref, factor_ref, cross, top, top_right, inverse)


HBM = pl.BlockSpec(memory_space=pltpu.HBM)


def call(kernel, name, outs, operands, hbm=0, flops=10**8, scratch=(), limit=16):
    return pl.pallas_call(
        kernel,
        out_shape=outs,
        in_specs=[HBM] * hbm + [VMEM] * (len(operands) - hbm),
        out_specs=jax.tree.map(lambda _: VMEM, outs),
        scratch_shapes=scratch,
        compiler_params=pltpu.CompilerParams(vmem_limit_bytes=limit * 2**20),
        cost_estimate=pl.CostEstimate(flops=flops, bytes_accessed=2 * 10**6, transcendentals=1000),
        name=name,
    )(*operands)


def array(*shape, dtype=f32):
    return jax.ShapeDtypeStruct(shape, dtype)


FIRST = (array(5 * K, 4 * K), array(4 * K, 2 * K), array(K, 2 * K), array(K, 2 * K))


def passed_along(block, axis, distance):
    devices = range(lax.axis_size(axis))
    route = [(i - distance, i) for i in devices if i - distance in devices]
    return lax.ppermute(block, axis, route)


def body(deflation, conductivity, storage, interface_rows, interface_counts):
    vectors = deflation[0].reshape(K * CZ, FACE)
    sigma = conductivity[0]
    counts = interface_counts.reshape(2 * REACH)
    strips, mine, ahead, behind, ahead_tail, behind_tail, top, bottom, first, live = call(
        pick_kernel,
        "pick",
        (
            array(4, K * CZ, 128),
            array(8, 2 * K, FACE, dtype=bf16),
            array(K, FACE),
            array(K, FACE),
            array(8, FACE),
            array(8, FACE),
            array(ROWS, FACE),
            array(ROWS, FACE),
            array(8, FACE),
            array(8, FACE),
        ),
        tuple(
            pltpu.with_memory_space_constraint(x, pltpu.HBM)
            for x in (vectors, sigma, interface_rows[0, 0], counts)
        ),
        hbm=4,
        scratch=(
            pltpu.VMEM((CZ, FACE), f32),
            pltpu.VMEM((2 * REACH, FACE), jnp.int32),
            pltpu.SMEM((2 * REACH,), jnp.int32),
            pltpu.SemaphoreType.DMA((7,)),
        ),
    )
    below = passed_along(top, "coarse", 1)
    above = passed_along(first, "coarse", -1)

    def direct(ahead, behind):
        return (
            passed_along(ahead, "sub", 2),
            passed_along(behind, "sub", -2),
            passed_along(ahead, "sub", 4),
            passed_along(behind, "sub", -4),
        )

    def swapped(name, own, received):
        packed = call(
            pack_kernel,
            name,
            array(4 * own[0].shape[0], FACE),
            (*own, *received),
            flops=10**6,
        )
        return lax.ppermute(packed, "sub", [(i, i ^ 1) for i in range(lax.axis_size("sub"))])

    tails = direct(ahead_tail, behind_tail)
    own, lower = call(
        own_kernel,
        "own",
        (array(K, K), array(K, K)),
        (strips, sigma, storage[0], top, bottom, below, above),
    )
    tails, (own, lower) = lax.optimization_barrier((tails, (own, lower)))
    tails = (*tails, swapped("tails", (ahead_tail, behind_tail), tails))
    payload = call(
        block_kernel,
        "block",
        array(8, K, 2 * K),
        (live, own, lower, mine, ahead_tail, behind_tail, *tails),
    )
    (ahead, behind), payload = lax.optimization_barrier(((ahead, behind), payload))
    blocks = lax.all_to_all(payload, "coarse", 0, 0)
    faces = direct(ahead, behind)
    state = call(
        first_half,
        "factor_first",
        FIRST,
        (blocks,),
        flops=10**9,
        scratch=(pltpu.VMEM((8, K, 2 * K), f32),),
    )
    faces, state = lax.optimization_barrier((faces, state))
    faces = (*faces, swapped("faces", (ahead, behind), faces))
    factor, inverse = call(
        second_half,
        "factor_second",
        (array(8 * K, 8 * K), array(8 * K, 2 * K)),
        (blocks, *state),
        flops=10**9,
        scratch=(pltpu.VMEM((8, K, 2 * K), f32), pltpu.VMEM((K, 2 * K), f32), pltpu.VMEM((K, 2 * K), f32)),
    )
    panel = call(
        panel_kernel,
        "panel",
        array(8 * K, 8 * K),
        (live, mine, ahead_tail, behind_tail, *tails, *faces, inverse),
    )
    return (factor[None], panel[None, None])


def solution(mesh):
    placed = (
        P("sub", None, "coarse", None),
        P("sub", "coarse", None),
        P("sub", "coarse", None),
        P("sub", "coarse", None, None),
        P("sub", "coarse", None),
    )
    return jax.shard_map(
        body,
        mesh=mesh,
        in_specs=placed,
        out_specs=(P("sub", None, None), P("sub", "coarse", None, None)),
        check_vma=False,
    )
```

```python
import functools

import jax
import jax.numpy as jnp
from jax import lax
from jax.experimental import pallas as pl
from jax.experimental.pallas import tpu as pltpu
from jax.sharding import PartitionSpec as P

K = 64
CX = 16
CY = 32
CZ = 16
FACE = 512
REACH = 4
ROWS = K + 8

f32 = jnp.float32
bf16 = jnp.bfloat16
VMEM = pl.BlockSpec(memory_space=pltpu.VMEM)
MATRIX = (((1,), (0,)), ((), ()))
GRAM = (((1,), (1,)), ((), ()))


def product(left, right, dims):
    return lax.dot_general(left, right, dims, preferred_element_type=f32)


def harmonic(first, second):
    return 2.0 * first * second / (first + second)


def halves(x):
    high = x.astype(bf16)
    return high, (x - high.astype(f32)).astype(bf16)


def stacked(x):
    return jnp.concatenate(halves(x), axis=0)


def quadrants(square):
    half = square[:K] + square[K:]
    return half[:, :K] + half[:, K:]


def rows_of(vectors, sigma):
    high, low = halves(sigma)
    tail = jnp.concatenate([high.astype(f32), low.astype(f32)], axis=0).astype(bf16)
    return jnp.concatenate([*halves(vectors), tail], axis=0)


def joined(found):
    return jnp.concatenate(
        [found[:K] + found[K : 2 * K], found[2 * K : 2 * K + 8] + found[2 * K + 8 :]], axis=0
    )


def layer_of(strips, z):
    return jnp.concatenate([strips[q, pl.ds(z, K, stride=CZ), :] for q in range(4)], axis=1)


def pick_kernel(vectors_hbm, sigma_hbm, index_hbm, counts_hbm, strips, own_ref, ahead_ref, behind_ref, ahead_tail, behind_tail, top_ref, bottom_ref, first_ref, live_ref, sigma_ref, index_ref, counts_ref, sems):
    copies = [
        pltpu.make_async_copy(vectors_hbm.at[:, pl.ds(128 * q, 128)], strips.at[q], sems.at[q])
        for q in range(4)
    ]
    copies.append(pltpu.make_async_copy(sigma_hbm, sigma_ref, sems.at[4]))
    copies.append(pltpu.make_async_copy(index_hbm, index_ref, sems.at[5]))
    copies.append(pltpu.make_async_copy(counts_hbm, counts_ref, sems.at[6]))
    for copy in copies:
        copy.start()
    lane = lax.broadcasted_iota(jnp.int32, (1, 256), 1)
    within = lane % 128
    cell_of_lane = (within % CY) * CX + jnp.where(lane >= 128, CX - 1, 0)
    cell = lax.broadcasted_iota(jnp.int32, (FACE, 256), 0)
    faces = jnp.zeros((4 * 144, 256), f32)
    for copy in copies:
        copy.wait()
    for step in range(4):
        groups = []
        for group in range(4):
            z = 4 * group + step
            layer = layer_of(strips, z)
            sigma = jnp.broadcast_to(sigma_ref[z : z + 1, :], (8, FACE))
            groups.append(rows_of(layer, sigma))
            if z == 0:
                bottom_ref[...] = jnp.concatenate([layer, sigma], axis=0)
                first_ref[...] = sigma
            if z == CZ - 1:
                top_ref[...] = jnp.concatenate([layer, sigma], axis=0)
        chosen = jnp.where(within // CY == step, cell_of_lane, -1)
        select = jnp.where(cell == chosen, 1.0, 0.0).astype(bf16)
        faces = faces + product(jnp.concatenate(groups, axis=0), select, MATRIX)
    along = lax.broadcasted_iota(jnp.int32, (1, FACE), 1)
    for slot in range(2 * REACH):
        live_ref[slot : slot + 1] = jnp.where(along < counts_ref[slot], 1.0, 0.0)
    place = lax.broadcasted_iota(jnp.int32, (FACE, FACE), 0)
    for side in range(2):
        wide = jnp.concatenate(
            [
                faces[144 * group : 144 * (group + 1), 128 * side : 128 * (side + 1)]
                for group in range(4)
            ],
            axis=1,
        )
        table = wide.astype(bf16)
        face_ref, tail_ref = (ahead_ref, ahead_tail) if side else (behind_ref, behind_tail)
        face_ref[...] = wide[:K] + wide[K : 2 * K]
        for slot in range(REACH * side, REACH * (side + 1)):
            cell_index = index_ref[slot : slot + 1, :]
            wanted = (cell_index >> 9) * CY + ((cell_index >> 4) & (CY - 1))
            select = jnp.where(place == wanted, 1.0, 0.0).astype(bf16)
            found = product(table, select, MATRIX)
            own_ref[slot] = found[: 2 * K].astype(bf16)
            reach = slot - REACH if side else REACH - 1 - slot
            tail_ref[reach : reach + 1] = found[2 * K : 2 * K + 1] + found[2 * K + 8 : 2 * K + 9]
            tail_ref[4 + reach : 5 + reach] = wanted.astype(f32)


def own_kernel(strips, sigma_ref, storage_ref, top_ref, bottom_ref, below_ref, above_ref, own_ref, lower_ref):
    sigma = sigma_ref[...]
    lane = lax.broadcasted_iota(jnp.int32, (CZ, FACE), 1)
    layer = lax.broadcasted_iota(jnp.int32, (CZ, FACE), 0)
    along_x = jnp.where(
        lane % CX == CX - 1, 0.0, harmonic(sigma, pltpu.roll(sigma, FACE - 1, 1))
    )
    along_y = jnp.where(
        lane >= FACE - CX, 0.0, harmonic(sigma, pltpu.roll(sigma, FACE - CX, 1))
    )
    along_z = jnp.where(layer == CZ - 1, 0.0, harmonic(sigma, pltpu.roll(sigma, CZ - 1, 0)))
    level = lax.axis_index("coarse")
    downward = harmonic(bottom_ref[K : K + 1, :], below_ref[K : K + 1, :])
    downward = jnp.where(level == 0, 0.0, downward)
    upward = harmonic(top_ref[K : K + 1, :], above_ref[:1, :])
    upward = jnp.where(level == lax.axis_size("coarse") - 1, 0.0, upward)
    half = 0.5 * (
        storage_ref[...]
        + along_x
        + pltpu.roll(along_x, 1, 1)
        + along_y
        + pltpu.roll(along_y, CX, 1)
        + along_z
        + pltpu.roll(along_z, 1, 0)
        + jnp.where(layer == 0, downward, 0.0)
        + jnp.where(layer == CZ - 1, upward, 0.0)
    )
    total = jnp.zeros((2 * K, 2 * K), f32)
    below = layer_of(strips, 0)
    for z in range(CZ):
        now = below
        applied = half[z : z + 1] * now
        applied = applied - along_x[z : z + 1] * pltpu.roll(now, FACE - 1, 1)
        applied = applied - along_y[z : z + 1] * pltpu.roll(now, FACE - CX, 1)
        if z < CZ - 1:
            below = layer_of(strips, z + 1)
            applied = applied - along_z[z : z + 1] * below
        total = total + product(stacked(now), stacked(applied), GRAM)
    own = quadrants(total)
    own_ref[...] = own + own.T
    weighted = stacked(bottom_ref[:K, :] * downward)
    lower_ref[...] = -quadrants(product(weighted, stacked(below_ref[:K, :]), GRAM))


def pack_kernel(ahead, behind, ahead2, behind2, ahead4, behind4, out_ref):
    count = ahead.shape[0]
    mine = lax.axis_index("sub") % 2
    for core, chosen in ((0, (ahead, ahead2, behind2, behind4)), (1, (ahead2, ahead4, behind, behind2))):
        @pl.when(mine == core)
        def _(chosen=chosen):
            for at, ref in enumerate(chosen):
                out_ref[count * at : count * (at + 1)] = ref[...]


OFFSETS = (-4, -3, -2, -1, 1, 2, 3, 4)


def partner(refs, offset):
    ahead2, behind2, ahead4, behind4, swapped = refs
    if offset % 2:
        at = {-1: 0, -3: 1, 1: 2, 3: 3}[offset]
        count = ahead2.shape[0]
        return swapped[count * at : count * at + count]
    return {-2: ahead2, -4: ahead4, 2: behind2, 4: behind4}[offset][...]


def weight_of(live_ref, ahead_tail, behind_tail, slot, tail):
    offset = OFFSETS[slot]
    reach = abs(offset) - 1
    mine = (ahead_tail if offset > 0 else behind_tail)[reach : reach + 1]
    pair = harmonic(mine, tail[reach : reach + 1])
    return jnp.where(live_ref[slot : slot + 1] > 0.0, pair, 0.0)


def weighted_rows(own_ref, slot, weight):
    rows = own_ref[slot]
    return stacked((rows[:K].astype(f32) + rows[K:].astype(f32)) * weight)


def block_kernel(live_ref, own_block, lower_block, own_ref, ahead, behind, *refs):
    *tails, out_ref = refs
    total = jnp.zeros((2 * K, 2 * K), f32)
    for slot, offset in enumerate(OFFSETS):
        weight = weight_of(live_ref, ahead, behind, slot, partner(tails, offset))
        total = total + product(weighted_rows(own_ref, slot, weight), own_ref[slot], GRAM)
    extra = quadrants(total)
    own = own_block[...] + 0.5 * (extra + extra.T)
    lower = lower_block[...]
    even = lax.axis_index("coarse") % 2 == 0
    payload = jnp.where(
        even, jnp.concatenate([own, lower], axis=1), jnp.concatenate([lower, own], axis=1)
    )
    for copy in range(8):
        out_ref[copy] = payload


def panel_kernel(live_ref, own_ref, ahead, behind, *refs):
    tails, faces, inverse, out_ref = refs[:5], refs[5:10], refs[10], refs[11]
    place = lax.broadcasted_iota(jnp.int32, (FACE, FACE), 0).astype(f32)
    blocks = []
    for slot, offset in enumerate(OFFSETS):
        tail = partner(tails, offset)
        weight = weight_of(live_ref, ahead, behind, slot, tail)
        reach = abs(offset) - 1
        select = jnp.where(place == tail[4 + reach : 5 + reach], 1.0, 0.0).astype(bf16)
        found = product(stacked(partner(faces, offset)), select, MATRIX).astype(bf16)
        blocks.append(quadrants(product(weighted_rows(own_ref, slot, -weight), found, GRAM)))
    high, low = halves(jnp.concatenate(blocks, axis=1))
    left_high, left_low = halves(inverse[:, :K])
    left = jnp.concatenate([left_high, left_low, left_high], axis=1)
    out_ref[...] = product(left, jnp.concatenate([high, high, low], axis=0), MATRIX)


def eliminate(rows, right, offset, lane, sub):
    factor_rows, inverse_rows = [], []
    wide = (8, 128)
    for panel in range(8):
        first = offset + 8 * panel
        column = [[None] * 16 for _ in range(8)]
        for k in range(8):
            for g in range(panel, 16):
                column[k][g] = jnp.broadcast_to(rows[g][:, first + k : first + k + 1], wide)
        pivot = [[None] * 8 for _ in range(8)]
        for i in range(8):
            for k in range(i, 8):
                pivot[i][k] = jnp.broadcast_to(column[i][panel][k : k + 1, :], wide)
        left_row = [jnp.broadcast_to(rows[panel][k : k + 1, :], wide) for k in range(8)]
        right_row = [jnp.broadcast_to(right[panel][k : k + 1, :], wide) for k in range(8)]
        kept = jnp.zeros(wide, f32)
        kept_right = jnp.zeros(wide, f32)
        for i in range(8):
            scale = lax.rsqrt(pivot[i][i])
            inverse = 1.0 / pivot[i][i]
            kept = jnp.where(sub == i, jnp.where(lane >= first + i, left_row[i], 0.0) * scale if offset == 0 else jnp.where((lane >= first + i) | (lane < 64), left_row[i], 0.0) * scale, kept)
            kept_right = jnp.where(sub == i, right_row[i] * scale, kept_right)
            left_row[i] = left_row[i] * inverse
            right_row[i] = right_row[i] * inverse
            scaled = [None] * 8
            for l in range(i + 1, 8):
                scaled[l] = pivot[i][l] * inverse
            for k in range(8):
                if k == i:
                    continue
                by = pivot[i][k] if k > i else pivot[k][i]
                left_row[k] = left_row[k] - by * left_row[i]
                right_row[k] = right_row[k] - by * right_row[i]
                for l in range(max(i + 1, k), 8):
                    pivot[k][l] = pivot[k][l] - by * scaled[l]
            pivot[i] = scaled
        for g in range(panel + 1, 16):
            for k in range(8):
                rows[g] = rows[g] - column[k][g] * left_row[k]
                right[g] = right[g] - column[k][g] * right_row[k]
        factor_rows.append(kept)
        inverse_rows.append(kept_right)
    return factor_rows, inverse_rows

def half_factor(begin, level, blocks_ref, factor_ref, cross, top, top_right, inverse):
    lane = lax.broadcasted_iota(jnp.int32, (8, 128), 1)
    sub = lax.broadcasted_iota(jnp.int32, (8, 128), 0)
    wide_lane = lax.broadcasted_iota(jnp.int32, (K, 2 * K), 1)
    zero = jnp.zeros((K, 2 * K), f32)
    at = [pl.ds(8 * g, 8) for g in range(8)]
    for c in range(4 * begin + 1, min(4 * begin + 5, 8)):
        block = blocks_ref[c]
        if c % 2 == 1:
            cross[c - 1] = jnp.concatenate([zero, block], axis=0).T[:K]
        else:
            cross[c - 1] = jnp.concatenate([block, zero], axis=0).T[K:]
    if begin:
        cross[7] = zero

    def unit(g, c):
        return jnp.where((lane == sub + 8 * g) & (level == c), 1.0, 0.0)

    if not begin:
        for g in range(8):
            top[at[g], :] = blocks_ref[0, at[g], :]
            top_right[at[g], :] = unit(g, 0)

    @pl.loop(2 * begin, 2 * begin + 2)
    def _(q):
        c = 2 * q
        last = q == 3
        rows = [jnp.where(lane < K, top[at[g], :], cross[c, at[g], :]) for g in range(8)]
        rows += [blocks_ref[c + 1, at[g], :] for g in range(8)]
        right = [top_right[at[g], :] for g in range(8)] + [unit(g, c + 1) for g in range(8)]
        even, even_right = eliminate(rows, right, 0, lane, sub)
        following = jnp.minimum(c + 2, 7)
        middle = [jnp.where(lane < K, cross[c + 1, at[g], :], rows[8 + g]) for g in range(8)]
        middle += [jnp.where(last, 0.0, blocks_ref[following, at[g], :]) for g in range(8)]
        middle_right = right[8:] + [unit(g, c + 2) for g in range(8)]
        odd, odd_right = eliminate(middle, middle_right, K, lane, sub)
        start = pl.multiple_of(128 * q, 128)
        for g in range(8):
            top[at[g], :] = middle[8 + g]
            top_right[at[g], :] = middle_right[8 + g]
            inverse[pl.ds(start + 8 * g, 8), :] = even_right[g]
            inverse[pl.ds(start + K + 8 * g, 8), :] = odd_right[g]
        both = jnp.concatenate(even + odd, axis=0).T
        cols = pl.ds(start, 128)
        factor_ref[pl.ds(start, K), cols] = jnp.where(wide_lane < K, both[:K], 0.0)
        factor_ref[pl.ds(start + K, K), cols] = both[K:]

        @pl.when(q < 3)
        def _():
            factor_ref[pl.ds(start + 128, K), cols] = jnp.where(wide_lane < K, 0.0, both[:K])


def first_half(blocks_ref, factor_ref, inverse, top, top_right, cross):
    factor_ref[...] = jnp.zeros((5 * K, 4 * K), f32)
    half_factor(0, lax.axis_index("coarse"), blocks_ref, factor_ref, cross, top, top_right, inverse)


def second_half(blocks_ref, part_ref, first_inverse, first_top, first_right, factor_ref, inverse, cross, top, top_right):
    factor_ref[: 5 * K, : 4 * K] = part_ref[...]
    factor_ref[5 * K :, : 4 * K] = jnp.zeros((3 * K, 4 * K), f32)
    factor_ref[:, 4 * K :] = jnp.zeros((8 * K, 4 * K), f32)
    inverse[: 4 * K, :] = first_inverse[...]
    top[...] = first_top[...]
    top_right[...] = first_right[...]
    half_factor(1, lax.axis_index("coarse"), blocks_ref, factor_ref, cross, top, top_right, inverse)


HBM = pl.BlockSpec(memory_space=pltpu.HBM)


def call(kernel, name, outs, operands, hbm=0, flops=10**8, scratch=(), limit=16):
    return pl.pallas_call(
        kernel,
        out_shape=outs,
        in_specs=[HBM] * hbm + [VMEM] * (len(operands) - hbm),
        out_specs=jax.tree.map(lambda _: VMEM, outs),
        scratch_shapes=scratch,
        compiler_params=pltpu.CompilerParams(vmem_limit_bytes=limit * 2**20),
        cost_estimate=pl.CostEstimate(flops=flops, bytes_accessed=2 * 10**6, transcendentals=1000),
        name=name,
    )(*operands)


def array(*shape, dtype=f32):
    return jax.ShapeDtypeStruct(shape, dtype)


FIRST = (array(5 * K, 4 * K), array(4 * K, 2 * K), array(K, 2 * K), array(K, 2 * K))


def passed_along(block, axis, distance):
    count = lax.axis_size(axis)
    return lax.ppermute(block, axis, [(i, (i + distance) % count) for i in range(count)])


def body(deflation, conductivity, storage, interface_rows, interface_counts):
    vectors = deflation[0].reshape(K * CZ, FACE)
    sigma = conductivity[0]
    counts = interface_counts.reshape(2 * REACH)
    strips, mine, ahead, behind, ahead_tail, behind_tail, top, bottom, first, live = call(
        pick_kernel,
        "pick",
        (
            array(4, K * CZ, 128),
            array(8, 2 * K, FACE, dtype=bf16),
            array(K, FACE),
            array(K, FACE),
            array(8, FACE),
            array(8, FACE),
            array(ROWS, FACE),
            array(ROWS, FACE),
            array(8, FACE),
            array(8, FACE),
        ),
        tuple(
            pltpu.with_memory_space_constraint(x, pltpu.HBM)
            for x in (vectors, sigma, interface_rows[0, 0], counts)
        ),
        hbm=4,
        scratch=(
            pltpu.VMEM((CZ, FACE), f32),
            pltpu.VMEM((2 * REACH, FACE), jnp.int32),
            pltpu.SMEM((2 * REACH,), jnp.int32),
            pltpu.SemaphoreType.DMA((7,)),
        ),
    )
    below = passed_along(top, "coarse", 1)
    above = passed_along(first, "coarse", -1)

    def direct(ahead, behind):
        return (
            passed_along(ahead, "sub", 2),
            passed_along(behind, "sub", -2),
            passed_along(ahead, "sub", 4),
            passed_along(behind, "sub", -4),
        )

    def swapped(name, own, received):
        packed = call(
            pack_kernel,
            name,
            array(4 * own[0].shape[0], FACE),
            (*own, *received),
            flops=10**6,
        )
        return lax.ppermute(packed, "sub", [(i, i ^ 1) for i in range(lax.axis_size("sub"))])

    tails = direct(ahead_tail, behind_tail)
    own, lower = call(
        own_kernel,
        "own",
        (array(K, K), array(K, K)),
        (strips, sigma, storage[0], top, bottom, below, above),
    )
    tails, (own, lower) = lax.optimization_barrier((tails, (own, lower)))
    tails = (*tails, swapped("tails", (ahead_tail, behind_tail), tails))
    payload = call(
        block_kernel,
        "block",
        array(8, K, 2 * K),
        (live, own, lower, mine, ahead_tail, behind_tail, *tails),
    )
    (ahead, behind), payload = lax.optimization_barrier(((ahead, behind), payload))
    blocks = lax.all_to_all(payload, "coarse", 0, 0)
    faces = direct(ahead, behind)
    state = call(
        first_half,
        "factor_first",
        FIRST,
        (blocks,),
        flops=10**9,
        scratch=(pltpu.VMEM((8, K, 2 * K), f32),),
    )
    faces, state = lax.optimization_barrier((faces, state))
    faces = (*faces, swapped("faces", (ahead, behind), faces))
    factor, inverse = call(
        second_half,
        "factor_second",
        (array(8 * K, 8 * K), array(8 * K, 2 * K)),
        (blocks, *state),
        flops=10**9,
        scratch=(pltpu.VMEM((8, K, 2 * K), f32), pltpu.VMEM((K, 2 * K), f32), pltpu.VMEM((K, 2 * K), f32)),
    )
    panel = call(
        panel_kernel,
        "panel",
        array(8 * K, 8 * K),
        (live, mine, ahead_tail, behind_tail, *tails, *faces, inverse),
    )
    return (factor[None], panel[None, None])


def solution(mesh):
    placed = (
        P("sub", None, "coarse", None),
        P("sub", "coarse", None),
        P("sub", "coarse", None),
        P("sub", "coarse", None, None),
        P("sub", "coarse", None),
    )
    return jax.shard_map(
        body,
        mesh=mesh,
        in_specs=placed,
        out_specs=(P("sub", None, None), P("sub", "coarse", None, None)),
        check_vma=False,
    )
```

```python
import functools

import jax
import jax.numpy as jnp
from jax import lax
from jax.experimental import pallas as pl
from jax.experimental.pallas import tpu as pltpu
from jax.sharding import PartitionSpec as P

K = 64
CX = 16
CY = 32
CZ = 16
FACE = 512
REACH = 4
ROWS = K + 8

f32 = jnp.float32
bf16 = jnp.bfloat16
VMEM = pl.BlockSpec(memory_space=pltpu.VMEM)
MATRIX = (((1,), (0,)), ((), ()))
GRAM = (((1,), (1,)), ((), ()))


def product(left, right, dims):
    return lax.dot_general(left, right, dims, preferred_element_type=f32)


def harmonic(first, second):
    return 2.0 * first * second / (first + second)


def halves(x):
    high = x.astype(bf16)
    return high, (x - high.astype(f32)).astype(bf16)


def stacked(x):
    return jnp.concatenate(halves(x), axis=0)


def quadrants(square):
    half = square[:K] + square[K:]
    return half[:, :K] + half[:, K:]


def rows_of(vectors, sigma):
    high, low = halves(sigma)
    tail = jnp.concatenate([high.astype(f32), low.astype(f32)], axis=0).astype(bf16)
    return jnp.concatenate([*halves(vectors), tail], axis=0)


def joined(found):
    return jnp.concatenate(
        [found[:K] + found[K : 2 * K], found[2 * K : 2 * K + 8] + found[2 * K + 8 :]], axis=0
    )


def layer_of(strips, z):
    return jnp.concatenate([strips[q, pl.ds(z, K, stride=CZ), :] for q in range(4)], axis=1)


def pick_kernel(vectors_hbm, sigma_hbm, index_hbm, counts_hbm, strips, own_ref, ahead_ref, behind_ref, ahead_tail, behind_tail, top_ref, bottom_ref, first_ref, live_ref, sigma_ref, index_ref, counts_ref, sems):
    copies = [
        pltpu.make_async_copy(vectors_hbm.at[:, pl.ds(128 * q, 128)], strips.at[q], sems.at[q])
        for q in range(4)
    ]
    copies.append(pltpu.make_async_copy(sigma_hbm, sigma_ref, sems.at[4]))
    copies.append(pltpu.make_async_copy(index_hbm, index_ref, sems.at[5]))
    copies.append(pltpu.make_async_copy(counts_hbm, counts_ref, sems.at[6]))
    for copy in copies:
        copy.start()
    lane = lax.broadcasted_iota(jnp.int32, (1, 256), 1)
    within = lane % 128
    cell_of_lane = (within % CY) * CX + jnp.where(lane >= 128, CX - 1, 0)
    cell = lax.broadcasted_iota(jnp.int32, (FACE, 256), 0)
    faces = jnp.zeros((4 * 144, 256), f32)
    for copy in copies:
        copy.wait()
    for step in range(4):
        groups = []
        for group in range(4):
            z = 4 * group + step
            layer = layer_of(strips, z)
            sigma = jnp.broadcast_to(sigma_ref[z : z + 1, :], (8, FACE))
            groups.append(rows_of(layer, sigma))
            if z == 0:
                bottom_ref[...] = jnp.concatenate([layer, sigma], axis=0)
                first_ref[...] = sigma
            if z == CZ - 1:
                top_ref[...] = jnp.concatenate([layer, sigma], axis=0)
        chosen = jnp.where(within // CY == step, cell_of_lane, -1)
        select = jnp.where(cell == chosen, 1.0, 0.0).astype(bf16)
        faces = faces + product(jnp.concatenate(groups, axis=0), select, MATRIX)
    along = lax.broadcasted_iota(jnp.int32, (1, FACE), 1)
    for slot in range(2 * REACH):
        live_ref[slot : slot + 1] = jnp.where(along < counts_ref[slot], 1.0, 0.0)
    place = lax.broadcasted_iota(jnp.int32, (FACE, FACE), 0)
    for side in range(2):
        wide = jnp.concatenate(
            [
                faces[144 * group : 144 * (group + 1), 128 * side : 128 * (side + 1)]
                for group in range(4)
            ],
            axis=1,
        )
        table = wide.astype(bf16)
        face_ref, tail_ref = (ahead_ref, ahead_tail) if side else (behind_ref, behind_tail)
        face_ref[...] = wide[:K] + wide[K : 2 * K]
        for slot in range(REACH * side, REACH * (side + 1)):
            cell_index = index_ref[slot : slot + 1, :]
            wanted = (cell_index >> 9) * CY + ((cell_index >> 4) & (CY - 1))
            select = jnp.where(place == wanted, 1.0, 0.0).astype(bf16)
            found = product(table, select, MATRIX)
            own_ref[slot] = found[: 2 * K].astype(bf16)
            reach = slot - REACH if side else REACH - 1 - slot
            tail_ref[reach : reach + 1] = found[2 * K : 2 * K + 1] + found[2 * K + 8 : 2 * K + 9]
            tail_ref[4 + reach : 5 + reach] = wanted.astype(f32)


def own_kernel(strips, sigma_ref, storage_ref, top_ref, bottom_ref, below_ref, above_ref, own_ref, lower_ref):
    sigma = sigma_ref[...]
    lane = lax.broadcasted_iota(jnp.int32, (CZ, FACE), 1)
    layer = lax.broadcasted_iota(jnp.int32, (CZ, FACE), 0)
    along_x = jnp.where(
        lane % CX == CX - 1, 0.0, harmonic(sigma, pltpu.roll(sigma, FACE - 1, 1))
    )
    along_y = jnp.where(
        lane >= FACE - CX, 0.0, harmonic(sigma, pltpu.roll(sigma, FACE - CX, 1))
    )
    along_z = jnp.where(layer == CZ - 1, 0.0, harmonic(sigma, pltpu.roll(sigma, CZ - 1, 0)))
    level = lax.axis_index("coarse")
    downward = harmonic(bottom_ref[K : K + 1, :], below_ref[K : K + 1, :])
    downward = jnp.where(level == 0, 0.0, downward)
    upward = harmonic(top_ref[K : K + 1, :], above_ref[:1, :])
    upward = jnp.where(level == lax.axis_size("coarse") - 1, 0.0, upward)
    half = 0.5 * (
        storage_ref[...]
        + along_x
        + pltpu.roll(along_x, 1, 1)
        + along_y
        + pltpu.roll(along_y, CX, 1)
        + along_z
        + pltpu.roll(along_z, 1, 0)
        + jnp.where(layer == 0, downward, 0.0)
        + jnp.where(layer == CZ - 1, upward, 0.0)
    )
    total = jnp.zeros((2 * K, 2 * K), f32)
    below = layer_of(strips, 0)
    for z in range(CZ):
        now = below
        applied = half[z : z + 1] * now
        applied = applied - along_x[z : z + 1] * pltpu.roll(now, FACE - 1, 1)
        applied = applied - along_y[z : z + 1] * pltpu.roll(now, FACE - CX, 1)
        if z < CZ - 1:
            below = layer_of(strips, z + 1)
            applied = applied - along_z[z : z + 1] * below
        total = total + product(stacked(now), stacked(applied), GRAM)
    own = quadrants(total)
    own_ref[...] = own + own.T
    weighted = stacked(bottom_ref[:K, :] * downward)
    lower_ref[...] = -quadrants(product(weighted, stacked(below_ref[:K, :]), GRAM))


def pack_kernel(ahead, behind, ahead2, behind2, ahead4, behind4, out_ref):
    count = ahead.shape[0]
    mine = lax.axis_index("sub") % 2
    for core, chosen in ((0, (ahead, ahead2, behind2, behind4)), (1, (ahead2, ahead4, behind, behind2))):
        @pl.when(mine == core)
        def _(chosen=chosen):
            for at, ref in enumerate(chosen):
                out_ref[count * at : count * (at + 1)] = ref[...]


OFFSETS = (-4, -3, -2, -1, 1, 2, 3, 4)


def partner(refs, offset):
    ahead2, behind2, ahead4, behind4, swapped = refs
    if offset % 2:
        at = {-1: 0, -3: 1, 1: 2, 3: 3}[offset]
        count = ahead2.shape[0]
        return swapped[count * at : count * at + count]
    return {-2: ahead2, -4: ahead4, 2: behind2, 4: behind4}[offset][...]


def weight_of(live_ref, ahead_tail, behind_tail, slot, tail):
    offset = OFFSETS[slot]
    reach = abs(offset) - 1
    mine = (ahead_tail if offset > 0 else behind_tail)[reach : reach + 1]
    pair = harmonic(mine, tail[reach : reach + 1])
    return jnp.where(live_ref[slot : slot + 1] > 0.0, pair, 0.0)


def weighted_rows(own_ref, slot, weight):
    rows = own_ref[slot]
    return stacked((rows[:K].astype(f32) + rows[K:].astype(f32)) * weight)


def block_kernel(live_ref, own_block, lower_block, own_ref, ahead, behind, *refs):
    *tails, out_ref = refs
    total = jnp.zeros((2 * K, 2 * K), f32)
    for slot, offset in enumerate(OFFSETS):
        weight = weight_of(live_ref, ahead, behind, slot, partner(tails, offset))
        total = total + product(weighted_rows(own_ref, slot, weight), own_ref[slot], GRAM)
    extra = quadrants(total)
    own = own_block[...] + 0.5 * (extra + extra.T)
    lower = lower_block[...]
    even = lax.axis_index("coarse") % 2 == 0
    payload = jnp.where(
        even, jnp.concatenate([own, lower], axis=1), jnp.concatenate([lower, own], axis=1)
    )
    for copy in range(8):
        out_ref[copy] = payload


def panel_kernel(live_ref, own_ref, ahead, behind, *refs):
    tails, faces, inverse, out_ref = refs[:5], refs[5:10], refs[10], refs[11]
    place = lax.broadcasted_iota(jnp.int32, (FACE, FACE), 0).astype(f32)
    blocks = []
    for slot, offset in enumerate(OFFSETS):
        tail = partner(tails, offset)
        weight = weight_of(live_ref, ahead, behind, slot, tail)
        reach = abs(offset) - 1
        select = jnp.where(place == tail[4 + reach : 5 + reach], 1.0, 0.0).astype(bf16)
        found = product(stacked(partner(faces, offset)), select, MATRIX).astype(bf16)
        blocks.append(quadrants(product(weighted_rows(own_ref, slot, -weight), found, GRAM)))
    high, low = halves(jnp.concatenate(blocks, axis=1))
    left_high, left_low = halves(inverse[:, :K])
    left = jnp.concatenate([left_high, left_low, left_high], axis=1)
    out_ref[...] = product(left, jnp.concatenate([high, high, low], axis=0), MATRIX)


def thirds(x):
    high = x.astype(bf16)
    rest = x - high.astype(f32)
    middle = rest.astype(bf16)
    return high, middle, (rest - middle.astype(f32)).astype(bf16)


def fine_product(left, right):
    a, b, c = thirds(left)
    p, q, r = thirds(right)
    first = product(jnp.concatenate([a, b, c], axis=0), p, MATRIX)
    second = product(jnp.concatenate([a, b], axis=0), q, MATRIX)
    small = product(a, r, MATRIX) + first[2 * K :] + second[K:]
    return first[:K] + (first[K : 2 * K] + second[:K] + small)


def lane_of(x, lane):
    index = jnp.full(x.shape, lane, jnp.int32)
    return jnp.take_along_axis(x, index, axis=1, mode="promise_in_bounds")


def sublane_of(x, sublane):
    index = jnp.full(x.shape, sublane, jnp.int32)
    return jnp.take_along_axis(x, index, axis=0, mode="promise_in_bounds")


def eliminate(rows, right, offset, lane, sub):
    wide = (8, 128)
    kept_rows, kept_right_rows = [], []
    for panel in range(8):
        first = offset + 8 * panel
        column = [
            {
                g: lane_of(rows[g], first + k)
                for g in range(panel, 8)
            }
            for k in range(8)
        ]
        pivot = [[None] * 8 for _ in range(8)]
        for i in range(8):
            for k in range(i, 8):
                pivot[i][k] = sublane_of(column[i][panel], k)
        left_row = [sublane_of(rows[panel], k) for k in range(8)]
        right_row = [sublane_of(right[panel], k) for k in range(8)]
        kept = jnp.zeros(wide, f32)
        kept_right = jnp.zeros(wide, f32)
        for i in range(8):
            scale = lax.rsqrt(pivot[i][i])
            inverse = 1.0 / pivot[i][i]
            kept = jnp.where(sub == i, left_row[i] * scale, kept)
            kept_right = jnp.where(sub == i, right_row[i] * scale, kept_right)
            left_row[i] = left_row[i] * inverse
            right_row[i] = right_row[i] * inverse
            scaled = [None] * 8
            for l in range(i + 1, 8):
                scaled[l] = pivot[i][l] * inverse
            for k in range(8):
                if k == i:
                    continue
                by = pivot[i][k] if k > i else pivot[k][i]
                left_row[k] = left_row[k] - by * left_row[i]
                right_row[k] = right_row[k] - by * right_row[i]
                for l in range(max(i + 1, k), 8):
                    pivot[k][l] = pivot[k][l] - by * scaled[l]
            pivot[i] = scaled
        for g in range(panel + 1, 8):
            for k in range(8):
                rows[g] = rows[g] - column[k][g] * left_row[k]
                right[g] = right[g] - column[k][g] * right_row[k]
        live = (lane >= first + sub) if offset else ((lane >= first + sub) | (lane >= K))
        if offset:
            live = live | (lane < K)
        kept_rows.append(jnp.where(live, kept, 0.0))
        kept_right_rows.append(kept_right)
    return jnp.concatenate(kept_rows, axis=0), jnp.concatenate(kept_right_rows, axis=0)


def half_factor(begin, level, blocks_ref, factor_ref, cross, top, top_right, inverse):
    lane = lax.broadcasted_iota(jnp.int32, (8, 128), 1)
    sub = lax.broadcasted_iota(jnp.int32, (8, 128), 0)
    wide_lane = lax.broadcasted_iota(jnp.int32, (K, 2 * K), 1)
    wide_sub = lax.broadcasted_iota(jnp.int32, (K, 2 * K), 0)
    zero = jnp.zeros((K, 2 * K), f32)
    at = [pl.ds(8 * g, 8) for g in range(8)]
    for c in range(4 * begin + 1, min(4 * begin + 5, 8)):
        block = blocks_ref[c]
        if c % 2 == 1:
            cross[c - 1] = jnp.concatenate([zero, block], axis=0).T[:K]
        else:
            cross[c - 1] = jnp.concatenate([block, zero], axis=0).T[K:]
    if begin:
        cross[7] = zero

    def unit(c):
        return jnp.where((wide_lane == wide_sub) & (level == c), 1.0, 0.0)

    if not begin:
        top[...] = blocks_ref[0]
        top_right[...] = unit(0)

    @pl.loop(2 * begin, 2 * begin + 2)
    def _(q):
        c = 2 * q
        last = q == 3
        rows = [jnp.where(lane < K, top[at[g], :], cross[c, at[g], :]) for g in range(8)]
        right = [top_right[at[g], :] for g in range(8)]
        even, even_right = eliminate(rows, right, 0, lane, sub)
        even_turned = even.T
        taken = fine_product(even_turned[K:], jnp.concatenate([even, even_right], axis=1))
        under = blocks_ref[c + 1] - taken[:, : 2 * K]
        under_right = unit(c + 1) - taken[:, 2 * K :]
        rows = [jnp.where(lane < K, cross[c + 1, at[g], :], under[8 * g : 8 * g + 8]) for g in range(8)]
        right = [under_right[8 * g : 8 * g + 8] for g in range(8)]
        odd, odd_right = eliminate(rows, right, K, lane, sub)
        odd_turned = odd.T
        taken = fine_product(odd_turned[:K], jnp.concatenate([odd, odd_right], axis=1))
        top[...] = jnp.where(last, 0.0, blocks_ref[jnp.minimum(c + 2, 7)]) - taken[:, : 2 * K]
        top_right[...] = unit(c + 2) - taken[:, 2 * K :]
        start = pl.multiple_of(128 * q, 128)
        inverse[pl.ds(start, K), :] = even_right
        inverse[pl.ds(start + K, K), :] = odd_right
        both = jnp.concatenate([even_turned, odd_turned], axis=1)
        cols = pl.ds(start, 128)
        factor_ref[pl.ds(start, K), cols] = jnp.where(wide_lane < K, both[:K], 0.0)
        factor_ref[pl.ds(start + K, K), cols] = both[K:]

        @pl.when(q < 3)
        def _():
            factor_ref[pl.ds(start + 128, K), cols] = jnp.where(wide_lane < K, 0.0, both[:K])


def first_half(blocks_ref, factor_ref, inverse, top, top_right, cross):
    factor_ref[...] = jnp.zeros((5 * K, 4 * K), f32)
    half_factor(0, lax.axis_index("coarse"), blocks_ref, factor_ref, cross, top, top_right, inverse)


def second_half(blocks_ref, part_ref, first_inverse, first_top, first_right, factor_ref, inverse, cross, top, top_right):
    factor_ref[: 5 * K, : 4 * K] = part_ref[...]
    factor_ref[5 * K :, : 4 * K] = jnp.zeros((3 * K, 4 * K), f32)
    factor_ref[:, 4 * K :] = jnp.zeros((8 * K, 4 * K), f32)
    inverse[: 4 * K, :] = first_inverse[...]
    top[...] = first_top[...]
    top_right[...] = first_right[...]
    half_factor(1, lax.axis_index("coarse"), blocks_ref, factor_ref, cross, top, top_right, inverse)


HBM = pl.BlockSpec(memory_space=pltpu.HBM)


def call(kernel, name, outs, operands, hbm=0, flops=10**8, scratch=(), limit=16):
    return pl.pallas_call(
        kernel,
        out_shape=outs,
        in_specs=[HBM] * hbm + [VMEM] * (len(operands) - hbm),
        out_specs=jax.tree.map(lambda _: VMEM, outs),
        scratch_shapes=scratch,
        compiler_params=pltpu.CompilerParams(vmem_limit_bytes=limit * 2**20),
        cost_estimate=pl.CostEstimate(flops=flops, bytes_accessed=2 * 10**6, transcendentals=1000),
        name=name,
    )(*operands)


def array(*shape, dtype=f32):
    return jax.ShapeDtypeStruct(shape, dtype)


FIRST = (array(5 * K, 4 * K), array(4 * K, 2 * K), array(K, 2 * K), array(K, 2 * K))


def passed_along(block, axis, distance):
    count = lax.axis_size(axis)
    return lax.ppermute(block, axis, [(i, (i + distance) % count) for i in range(count)])


def body(deflation, conductivity, storage, interface_rows, interface_counts):
    vectors = deflation[0].reshape(K * CZ, FACE)
    sigma = conductivity[0]
    counts = interface_counts.reshape(2 * REACH)
    strips, mine, ahead, behind, ahead_tail, behind_tail, top, bottom, first, live = call(
        pick_kernel,
        "pick",
        (
            array(4, K * CZ, 128),
            array(8, 2 * K, FACE, dtype=bf16),
            array(K, FACE),
            array(K, FACE),
            array(8, FACE),
            array(8, FACE),
            array(ROWS, FACE),
            array(ROWS, FACE),
            array(8, FACE),
            array(8, FACE),
        ),
        tuple(
            pltpu.with_memory_space_constraint(x, pltpu.HBM)
            for x in (vectors, sigma, interface_rows[0, 0], counts)
        ),
        hbm=4,
        scratch=(
            pltpu.VMEM((CZ, FACE), f32),
            pltpu.VMEM((2 * REACH, FACE), jnp.int32),
            pltpu.SMEM((2 * REACH,), jnp.int32),
            pltpu.SemaphoreType.DMA((7,)),
        ),
    )
    below = passed_along(top, "coarse", 1)
    above = passed_along(first, "coarse", -1)

    def direct(ahead, behind):
        return (
            passed_along(ahead, "sub", 2),
            passed_along(behind, "sub", -2),
            passed_along(ahead, "sub", 4),
            passed_along(behind, "sub", -4),
        )

    def swapped(name, own, received):
        packed = call(
            pack_kernel,
            name,
            array(4 * own[0].shape[0], FACE),
            (*own, *received),
            flops=10**6,
        )
        return lax.ppermute(packed, "sub", [(i, i ^ 1) for i in range(lax.axis_size("sub"))])

    tails = direct(ahead_tail, behind_tail)
    own, lower = call(
        own_kernel,
        "own",
        (array(K, K), array(K, K)),
        (strips, sigma, storage[0], top, bottom, below, above),
    )
    tails, (own, lower) = lax.optimization_barrier((tails, (own, lower)))
    tails = (*tails, swapped("tails", (ahead_tail, behind_tail), tails))
    payload = call(
        block_kernel,
        "block",
        array(8, K, 2 * K),
        (live, own, lower, mine, ahead_tail, behind_tail, *tails),
    )
    (ahead, behind), payload = lax.optimization_barrier(((ahead, behind), payload))
    blocks = lax.all_to_all(payload, "coarse", 0, 0)
    faces = direct(ahead, behind)
    state = call(
        first_half,
        "factor_first",
        FIRST,
        (blocks,),
        flops=10**9,
        scratch=(pltpu.VMEM((8, K, 2 * K), f32),),
    )
    faces, state = lax.optimization_barrier((faces, state))
    faces = (*faces, swapped("faces", (ahead, behind), faces))
    factor, inverse = call(
        second_half,
        "factor_second",
        (array(8 * K, 8 * K), array(8 * K, 2 * K)),
        (blocks, *state),
        flops=10**9,
        scratch=(pltpu.VMEM((8, K, 2 * K), f32), pltpu.VMEM((K, 2 * K), f32), pltpu.VMEM((K, 2 * K), f32)),
    )
    panel = call(
        panel_kernel,
        "panel",
        array(8 * K, 8 * K),
        (live, mine, ahead_tail, behind_tail, *tails, *faces, inverse),
    )
    return (factor[None], panel[None, None])


def solution(mesh):
    placed = (
        P("sub", None, "coarse", None),
        P("sub", "coarse", None),
        P("sub", "coarse", None),
        P("sub", "coarse", None, None),
        P("sub", "coarse", None),
    )
    return jax.shard_map(
        body,
        mesh=mesh,
        in_specs=placed,
        out_specs=(P("sub", None, None), P("sub", "coarse", None, None)),
        check_vma=False,
    )
```

```python
import functools

import jax
import jax.numpy as jnp
from jax import lax
from jax.experimental import pallas as pl
from jax.experimental.pallas import tpu as pltpu
from jax.sharding import PartitionSpec as P

K = 64
CX = 16
CY = 32
CZ = 16
FACE = 512
REACH = 4
ROWS = K + 8

f32 = jnp.float32
bf16 = jnp.bfloat16
VMEM = pl.BlockSpec(memory_space=pltpu.VMEM)
MATRIX = (((1,), (0,)), ((), ()))
GRAM = (((1,), (1,)), ((), ()))


def product(left, right, dims):
    return lax.dot_general(left, right, dims, preferred_element_type=f32)


def harmonic(first, second):
    return 2.0 * first * second / (first + second)


def halves(x):
    high = x.astype(bf16)
    return high, (x - high.astype(f32)).astype(bf16)


def stacked(x):
    return jnp.concatenate(halves(x), axis=0)


def quadrants(square):
    half = square[:K] + square[K:]
    return half[:, :K] + half[:, K:]


def gathered(table, index):
    strips = []
    for q in range(4):
        wanted = jnp.broadcast_to(index[:, 128 * q : 128 * (q + 1)], (8, 128))
        within, which = wanted & 127, wanted >> 7
        groups = []
        for g in range(0, table.shape[0], 8):
            found = None
            for strip in range(4):
                part = jnp.take_along_axis(
                    table[g : g + 8, 128 * strip : 128 * (strip + 1)],
                    within,
                    axis=1,
                    mode="promise_in_bounds",
                )
                found = part if strip == 0 else jnp.where(which == strip, part, found)
            groups.append(found)
        strips.append(jnp.concatenate(groups, axis=0))
    return jnp.concatenate(strips, axis=1)


def rows_of(vectors, sigma):
    high, low = halves(sigma)
    tail = jnp.concatenate([high.astype(f32), low.astype(f32)], axis=0).astype(bf16)
    return jnp.concatenate([*halves(vectors), tail], axis=0)


def joined(found):
    return jnp.concatenate(
        [found[:K] + found[K : 2 * K], found[2 * K : 2 * K + 8] + found[2 * K + 8 :]], axis=0
    )


def layer_of(strips, z):
    return jnp.concatenate([strips[q, pl.ds(z, K, stride=CZ), :] for q in range(4)], axis=1)


def pick_kernel(vectors_hbm, sigma_hbm, index_hbm, counts_hbm, strips, own_ref, ahead_ref, behind_ref, tails_ref, top_ref, bottom_ref, first_ref, live_ref, sigma_ref, index_ref, counts_ref, sems):
    copies = [
        pltpu.make_async_copy(vectors_hbm.at[:, pl.ds(128 * q, 128)], strips.at[q], sems.at[q])
        for q in range(4)
    ]
    copies.append(pltpu.make_async_copy(sigma_hbm, sigma_ref, sems.at[4]))
    copies.append(pltpu.make_async_copy(index_hbm, index_ref, sems.at[5]))
    copies.append(pltpu.make_async_copy(counts_hbm, counts_ref, sems.at[6]))
    for copy in copies:
        copy.start()
    lane = lax.broadcasted_iota(jnp.int32, (1, 256), 1)
    within = lane % 128
    cell_of_lane = (within % CY) * CX + jnp.where(lane >= 128, CX - 1, 0)
    cell = lax.broadcasted_iota(jnp.int32, (FACE, 256), 0)
    faces = jnp.zeros((4 * 144, 256), f32)
    for copy in copies:
        copy.wait()
    for step in range(4):
        groups = []
        for group in range(4):
            z = 4 * group + step
            layer = layer_of(strips, z)
            sigma = jnp.broadcast_to(sigma_ref[z : z + 1, :], (8, FACE))
            groups.append(rows_of(layer, sigma))
            if z == 0:
                bottom_ref[...] = jnp.concatenate([layer, sigma], axis=0)
                first_ref[...] = sigma
            if z == CZ - 1:
                top_ref[...] = jnp.concatenate([layer, sigma], axis=0)
        chosen = jnp.where(within // CY == step, cell_of_lane, -1)
        select = jnp.where(cell == chosen, 1.0, 0.0).astype(bf16)
        faces = faces + product(jnp.concatenate(groups, axis=0), select, MATRIX)
    along = lax.broadcasted_iota(jnp.int32, (1, FACE), 1)
    for slot in range(2 * REACH):
        live_ref[slot : slot + 1] = jnp.where(along < counts_ref[slot], 1.0, 0.0)
    for side in range(2):
        wide = jnp.concatenate(
            [
                faces[144 * group : 144 * (group + 1), 128 * side : 128 * (side + 1)]
                for group in range(4)
            ],
            axis=1,
        )
        face_ref = ahead_ref if side else behind_ref
        table = joined(wide)
        face_ref[...] = table[:K]
        for slot in range(REACH * side, REACH * (side + 1)):
            cell_index = index_ref[slot : slot + 1, :]
            wanted = (cell_index >> 9) * CY + ((cell_index >> 4) & (CY - 1))
            found = gathered(table, wanted)
            own_ref[slot] = stacked(found[:K])
            row = slot - REACH if side else 8 + REACH - 1 - slot
            tails_ref[row : row + 1] = found[K : K + 1]
            tails_ref[4 + row : 5 + row] = wanted.astype(f32)


def own_kernel(strips, sigma_ref, storage_ref, top_ref, bottom_ref, below_ref, above_ref, own_ref, lower_ref):
    sigma = sigma_ref[...]
    lane = lax.broadcasted_iota(jnp.int32, (CZ, FACE), 1)
    layer = lax.broadcasted_iota(jnp.int32, (CZ, FACE), 0)
    along_x = jnp.where(
        lane % CX == CX - 1, 0.0, harmonic(sigma, pltpu.roll(sigma, FACE - 1, 1))
    )
    along_y = jnp.where(
        lane >= FACE - CX, 0.0, harmonic(sigma, pltpu.roll(sigma, FACE - CX, 1))
    )
    along_z = jnp.where(layer == CZ - 1, 0.0, harmonic(sigma, pltpu.roll(sigma, CZ - 1, 0)))
    level = lax.axis_index("coarse")
    downward = harmonic(bottom_ref[K : K + 1, :], below_ref[K : K + 1, :])
    downward = jnp.where(level == 0, 0.0, downward)
    upward = harmonic(top_ref[K : K + 1, :], above_ref[:1, :])
    upward = jnp.where(level == lax.axis_size("coarse") - 1, 0.0, upward)
    half = 0.5 * (
        storage_ref[...]
        + along_x
        + pltpu.roll(along_x, 1, 1)
        + along_y
        + pltpu.roll(along_y, CX, 1)
        + along_z
        + pltpu.roll(along_z, 1, 0)
        + jnp.where(layer == 0, downward, 0.0)
        + jnp.where(layer == CZ - 1, upward, 0.0)
    )
    total = jnp.zeros((2 * K, 2 * K), f32)
    below = layer_of(strips, 0)
    for z in range(CZ):
        now = below
        applied = half[z : z + 1] * now
        applied = applied - along_x[z : z + 1] * pltpu.roll(now, FACE - 1, 1)
        applied = applied - along_y[z : z + 1] * pltpu.roll(now, FACE - CX, 1)
        if z < CZ - 1:
            below = layer_of(strips, z + 1)
            applied = applied - along_z[z : z + 1] * below
        total = total + product(stacked(now), stacked(applied), GRAM)
    own = quadrants(total)
    own_ref[...] = own + own.T
    weighted = stacked(bottom_ref[:K, :] * downward)
    lower_ref[...] = -quadrants(product(weighted, stacked(below_ref[:K, :]), GRAM))


def pack_kernel(ahead, behind, ahead2, behind2, ahead4, behind4, out_ref):
    mine = lax.axis_index("sub") % 2
    for core, chosen in ((0, (ahead, ahead2, behind2, behind4)), (1, (ahead2, ahead4, behind, behind2))):
        @pl.when(mine == core)
        def _(chosen=chosen):
            for at, ref in enumerate(chosen):
                out_ref[K * at : K * (at + 1)] = ref[...]


def pair_kernel(own, other, ahead_ref, behind_ref):
    ahead_ref[:8] = own[:8]
    ahead_ref[8:] = other[:8]
    behind_ref[:8] = own[8:]
    behind_ref[8:] = other[8:]


def join_kernel(first, second, out_ref):
    out_ref[:16] = first[...]
    out_ref[16:] = second[...]


OFFSETS = (-4, -3, -2, -1, 1, 2, 3, 4)


def tails_by_slot(other, before, after, swapped):
    even = lax.axis_index("sub") % 2 == 0
    low, high = slice(0, 8), slice(8, 16)
    before1 = jnp.where(even, before[...], swapped[:16])
    before2 = jnp.where(even, swapped[:16], before[...])
    after1 = jnp.where(even, after[...], swapped[16:])
    after2 = jnp.where(even, swapped[16:], after[...])
    on_even = (before2[high], before2[low], before1[low], before1[high], other[high], after1[low], after1[high], after2[high])
    on_odd = (before2[low], before1[low], before1[high], other[low], after1[low], after1[high], after2[high], after2[low])
    return [jnp.where(even, x, y) for x, y in zip(on_even, on_odd, strict=True)]


def partner_face(refs, offset):
    ahead2, behind2, ahead4, behind4, swapped = refs
    if offset % 2:
        at = {-1: 0, -3: 1, 1: 2, 3: 3}[offset]
        return swapped[K * at : K * at + K]
    return {-2: ahead2, -4: ahead4, 2: behind2, 4: behind4}[offset][...]


def weighted_rows(own_ref, slot, weight):
    rows = own_ref[slot]
    return stacked((rows[:K].astype(f32) + rows[K:].astype(f32)) * weight)


def block_kernel(live_ref, own_block, lower_block, own_ref, own_tails, *refs):
    *tails, out_ref, weight_ref, index_ref = refs
    total = jnp.zeros((2 * K, 2 * K), f32)
    found = tails_by_slot(*tails)
    for slot, offset in enumerate(OFFSETS):
        reach = abs(offset) - 1
        row = reach if offset > 0 else 8 + reach
        pair = harmonic(own_tails[row : row + 1], found[slot][reach : reach + 1])
        weight = jnp.where(live_ref[slot : slot + 1] > 0.0, pair, 0.0)
        weight_ref[slot : slot + 1] = weight
        index_ref[slot : slot + 1] = found[slot][4 + reach : 5 + reach].astype(jnp.int32)
        total = total + product(weighted_rows(own_ref, slot, weight), own_ref[slot], GRAM)
    extra = quadrants(total)
    own = own_block[...] + 0.5 * (extra + extra.T)
    lower = lower_block[...]
    even = lax.axis_index("coarse") % 2 == 0
    payload = jnp.where(
        even, jnp.concatenate([own, lower], axis=1), jnp.concatenate([lower, own], axis=1)
    )
    for copy in range(8):
        out_ref[copy] = payload


def panel_kernel(weight_ref, index_ref, own_ref, *refs):
    faces, inverse, out_ref = refs[:5], refs[5], refs[6]
    blocks = []
    for slot, offset in enumerate(OFFSETS):
        found = gathered(partner_face(faces, offset), index_ref[slot : slot + 1, :])
        weighted = weighted_rows(own_ref, slot, -weight_ref[slot : slot + 1])
        blocks.append(quadrants(product(weighted, stacked(found), GRAM)))
    high, low = halves(jnp.concatenate(blocks, axis=1))
    left_high, left_low = halves(inverse[:, :K])
    left = jnp.concatenate([left_high, left_low, left_high], axis=1)
    out_ref[...] = product(left, jnp.concatenate([high, high, low], axis=0), MATRIX)


def thirds(x):
    high = x.astype(bf16)
    rest = x - high.astype(f32)
    middle = rest.astype(bf16)
    return high, middle, (rest - middle.astype(f32)).astype(bf16)


def fine_product(left, right):
    a, b, c = thirds(left)
    p, q, r = thirds(right)
    first = product(jnp.concatenate([a, b, c], axis=0), p, MATRIX)
    second = product(jnp.concatenate([a, b], axis=0), q, MATRIX)
    small = product(a, r, MATRIX) + first[2 * K :] + second[K:]
    return first[:K] + (first[K : 2 * K] + second[:K] + small)


def lane_of(x, lane):
    index = jnp.full(x.shape, lane, jnp.int32)
    return jnp.take_along_axis(x, index, axis=1, mode="promise_in_bounds")


def sublane_of(x, sublane):
    index = jnp.full(x.shape, sublane, jnp.int32)
    return jnp.take_along_axis(x, index, axis=0, mode="promise_in_bounds")


def eliminate(rows, right, offset, lane, sub):
    wide = (8, 128)
    kept_rows, kept_right_rows = [], []
    for panel in range(8):
        first = offset + 8 * panel
        column = [
            {
                g: lane_of(rows[g], first + k)
                for g in range(panel, 8)
            }
            for k in range(8)
        ]
        pivot = [[None] * 8 for _ in range(8)]
        for i in range(8):
            for k in range(i, 8):
                pivot[i][k] = sublane_of(column[i][panel], k)
        left_row = [sublane_of(rows[panel], k) for k in range(8)]
        right_row = [sublane_of(right[panel], k) for k in range(8)]
        kept = jnp.zeros(wide, f32)
        kept_right = jnp.zeros(wide, f32)
        for i in range(8):
            scale = lax.rsqrt(pivot[i][i])
            inverse = 1.0 / pivot[i][i]
            kept = jnp.where(sub == i, left_row[i] * scale, kept)
            kept_right = jnp.where(sub == i, right_row[i] * scale, kept_right)
            left_row[i] = left_row[i] * inverse
            right_row[i] = right_row[i] * inverse
            scaled = [None] * 8
            for l in range(i + 1, 8):
                scaled[l] = pivot[i][l] * inverse
            for k in range(8):
                if k == i:
                    continue
                by = pivot[i][k] if k > i else pivot[k][i]
                left_row[k] = left_row[k] - by * left_row[i]
                right_row[k] = right_row[k] - by * right_row[i]
                for l in range(max(i + 1, k), 8):
                    pivot[k][l] = pivot[k][l] - by * scaled[l]
            pivot[i] = scaled
        for g in range(panel + 1, 8):
            for k in range(8):
                rows[g] = rows[g] - column[k][g] * left_row[k]
                right[g] = right[g] - column[k][g] * right_row[k]
        live = (lane >= first + sub) if offset else ((lane >= first + sub) | (lane >= K))
        if offset:
            live = live | (lane < K)
        kept_rows.append(jnp.where(live, kept, 0.0))
        kept_right_rows.append(kept_right)
    return jnp.concatenate(kept_rows, axis=0), jnp.concatenate(kept_right_rows, axis=0)


def half_factor(begin, level, blocks_ref, factor_ref, cross, top, top_right, inverse):
    lane = lax.broadcasted_iota(jnp.int32, (8, 128), 1)
    sub = lax.broadcasted_iota(jnp.int32, (8, 128), 0)
    wide_lane = lax.broadcasted_iota(jnp.int32, (K, 2 * K), 1)
    wide_sub = lax.broadcasted_iota(jnp.int32, (K, 2 * K), 0)
    zero = jnp.zeros((K, 2 * K), f32)
    at = [pl.ds(8 * g, 8) for g in range(8)]
    for c in range(4 * begin + 1, min(4 * begin + 5, 8)):
        block = blocks_ref[c]
        if c % 2 == 1:
            cross[c - 1] = jnp.concatenate([zero, block], axis=0).T[:K]
        else:
            cross[c - 1] = jnp.concatenate([block, zero], axis=0).T[K:]
    if begin:
        cross[7] = zero

    def unit(c):
        return jnp.where((wide_lane == wide_sub) & (level == c), 1.0, 0.0)

    if not begin:
        top[...] = blocks_ref[0]
        top_right[...] = unit(0)

    @pl.loop(2 * begin, 2 * begin + 2)
    def _(q):
        c = 2 * q
        last = q == 3
        rows = [jnp.where(lane < K, top[at[g], :], cross[c, at[g], :]) for g in range(8)]
        right = [top_right[at[g], :] for g in range(8)]
        even, even_right = eliminate(rows, right, 0, lane, sub)
        even_turned = even.T
        taken = fine_product(even_turned[K:], jnp.concatenate([even, even_right], axis=1))
        under = blocks_ref[c + 1] - taken[:, : 2 * K]
        under_right = unit(c + 1) - taken[:, 2 * K :]
        rows = [jnp.where(lane < K, cross[c + 1, at[g], :], under[8 * g : 8 * g + 8]) for g in range(8)]
        right = [under_right[8 * g : 8 * g + 8] for g in range(8)]
        odd, odd_right = eliminate(rows, right, K, lane, sub)
        odd_turned = odd.T
        taken = fine_product(odd_turned[:K], jnp.concatenate([odd, odd_right], axis=1))
        top[...] = jnp.where(last, 0.0, blocks_ref[jnp.minimum(c + 2, 7)]) - taken[:, : 2 * K]
        top_right[...] = unit(c + 2) - taken[:, 2 * K :]
        start = pl.multiple_of(128 * q, 128)
        inverse[pl.ds(start, K), :] = even_right
        inverse[pl.ds(start + K, K), :] = odd_right
        both = jnp.concatenate([even_turned, odd_turned], axis=1)
        cols = pl.ds(start, 128)
        factor_ref[pl.ds(start, K), cols] = jnp.where(wide_lane < K, both[:K], 0.0)
        factor_ref[pl.ds(start + K, K), cols] = both[K:]

        @pl.when(q < 3)
        def _():
            factor_ref[pl.ds(start + 128, K), cols] = jnp.where(wide_lane < K, 0.0, both[:K])


def first_half(blocks_ref, factor_ref, inverse, top, top_right, cross):
    factor_ref[...] = jnp.zeros((5 * K, 4 * K), f32)
    half_factor(0, lax.axis_index("coarse"), blocks_ref, factor_ref, cross, top, top_right, inverse)


def second_half(blocks_ref, part_ref, first_inverse, first_top, first_right, factor_ref, inverse, cross, top, top_right):
    factor_ref[: 5 * K, : 4 * K] = part_ref[...]
    factor_ref[5 * K :, : 4 * K] = jnp.zeros((3 * K, 4 * K), f32)
    factor_ref[:, 4 * K :] = jnp.zeros((8 * K, 4 * K), f32)
    inverse[: 4 * K, :] = first_inverse[...]
    top[...] = first_top[...]
    top_right[...] = first_right[...]
    half_factor(1, lax.axis_index("coarse"), blocks_ref, factor_ref, cross, top, top_right, inverse)


HBM = pl.BlockSpec(memory_space=pltpu.HBM)


def call(kernel, name, outs, operands, hbm=0, flops=10**8, scratch=(), limit=16):
    return pl.pallas_call(
        kernel,
        out_shape=outs,
        in_specs=[HBM] * hbm + [VMEM] * (len(operands) - hbm),
        out_specs=jax.tree.map(lambda _: VMEM, outs),
        scratch_shapes=scratch,
        compiler_params=pltpu.CompilerParams(vmem_limit_bytes=limit * 2**20),
        cost_estimate=pl.CostEstimate(flops=flops, bytes_accessed=2 * 10**6, transcendentals=1000),
        name=name,
    )(*operands)


def array(*shape, dtype=f32):
    return jax.ShapeDtypeStruct(shape, dtype)


FIRST = (array(5 * K, 4 * K), array(4 * K, 2 * K), array(K, 2 * K), array(K, 2 * K))


def passed_along(block, axis, distance):
    count = lax.axis_size(axis)
    return lax.ppermute(block, axis, [(i, (i + distance) % count) for i in range(count)])


def body(deflation, conductivity, storage, interface_rows, interface_counts):
    vectors = deflation[0].reshape(K * CZ, FACE)
    sigma = conductivity[0]
    counts = interface_counts.reshape(2 * REACH)
    strips, mine, ahead, behind, own_tails, top, bottom, first, live = call(
        pick_kernel,
        "pick",
        (
            array(4, K * CZ, 128),
            array(8, 2 * K, FACE, dtype=bf16),
            array(K, FACE),
            array(K, FACE),
            array(16, FACE),
            array(ROWS, FACE),
            array(ROWS, FACE),
            array(8, FACE),
            array(8, FACE),
        ),
        tuple(
            pltpu.with_memory_space_constraint(x, pltpu.HBM)
            for x in (vectors, sigma, interface_rows[0, 0], counts)
        ),
        hbm=4,
        scratch=(
            pltpu.VMEM((CZ, FACE), f32),
            pltpu.VMEM((2 * REACH, FACE), jnp.int32),
            pltpu.SMEM((2 * REACH,), jnp.int32),
            pltpu.SemaphoreType.DMA((7,)),
        ),
    )
    count = lax.axis_size("sub")
    swap = [(i, i ^ 1) for i in range(count)]
    other_tails = lax.ppermute(own_tails, "sub", swap)
    below = passed_along(top, "coarse", 1)
    above = passed_along(first, "coarse", -1)
    go_ahead, go_behind = call(
        pair_kernel, "pair", (array(16, FACE), array(16, FACE)), (own_tails, other_tails), flops=10**6
    )
    far = [(i, (i + 2 + 2 * (i % 2)) % count) for i in range(count)]
    before = lax.ppermute(go_ahead, "sub", far)
    after = lax.ppermute(go_behind, "sub", [(j, i) for i, j in far])
    own, lower = call(
        own_kernel,
        "own",
        (array(K, K), array(K, K)),
        (strips, sigma, storage[0], top, bottom, below, above),
    )
    (before, after), (own, lower) = lax.optimization_barrier(((before, after), (own, lower)))
    both = call(join_kernel, "join", array(32, FACE), (before, after), flops=10**6)
    swapped_tails = lax.ppermute(both, "sub", swap)
    payload, weight, index = call(
        block_kernel,
        "block",
        (array(8, K, 2 * K), array(8, FACE), array(8, FACE, dtype=jnp.int32)),
        (live, own, lower, mine, own_tails, other_tails, before, after, swapped_tails),
    )
    (ahead, behind), payload = lax.optimization_barrier(((ahead, behind), payload))
    blocks = lax.all_to_all(payload, "coarse", 0, 0)
    faces = (
        passed_along(ahead, "sub", 2),
        passed_along(behind, "sub", -2),
        passed_along(ahead, "sub", 4),
        passed_along(behind, "sub", -4),
    )
    state = call(
        first_half,
        "factor_first",
        FIRST,
        (blocks,),
        flops=10**9,
        scratch=(pltpu.VMEM((8, K, 2 * K), f32),),
    )
    faces, state = lax.optimization_barrier((faces, state))
    packed = call(pack_kernel, "faces", array(4 * K, FACE), (ahead, behind, *faces), flops=10**6)
    faces = (*faces, lax.ppermute(packed, "sub", swap))
    factor, inverse = call(
        second_half,
        "factor_second",
        (array(8 * K, 8 * K), array(8 * K, 2 * K)),
        (blocks, *state),
        flops=10**9,
        scratch=(pltpu.VMEM((8, K, 2 * K), f32), pltpu.VMEM((K, 2 * K), f32), pltpu.VMEM((K, 2 * K), f32)),
    )
    panel = call(
        panel_kernel,
        "panel",
        array(8 * K, 8 * K),
        (weight, index, mine, *faces, inverse),
    )
    return (factor[None], panel[None, None])


def solution(mesh):
    placed = (
        P("sub", None, "coarse", None),
        P("sub", "coarse", None),
        P("sub", "coarse", None),
        P("sub", "coarse", None, None),
        P("sub", "coarse", None),
    )
    return jax.shard_map(
        body,
        mesh=mesh,
        in_specs=placed,
        out_specs=(P("sub", None, None), P("sub", "coarse", None, None)),
        check_vma=False,
    )
```

```python
import functools

import jax
import jax.numpy as jnp
from jax import lax
from jax.experimental import pallas as pl
from jax.experimental.pallas import tpu as pltpu
from jax.sharding import PartitionSpec as P

K = 64
CX = 16
CY = 32
CZ = 16
FACE = 512
REACH = 4
ROWS = K + 8

f32 = jnp.float32
bf16 = jnp.bfloat16
VMEM = pl.BlockSpec(memory_space=pltpu.VMEM)
MATRIX = (((1,), (0,)), ((), ()))
GRAM = (((1,), (1,)), ((), ()))


def product(left, right, dims):
    return lax.dot_general(left, right, dims, preferred_element_type=f32)


def harmonic(first, second):
    return 2.0 * first * second / (first + second)


def halves(x):
    high = x.astype(bf16)
    return high, (x - high.astype(f32)).astype(bf16)


def stacked(x):
    return jnp.concatenate(halves(x), axis=0)


def quadrants(square):
    half = square[:K] + square[K:]
    return half[:, :K] + half[:, K:]


def one_hot(index):
    place = lax.broadcasted_iota(jnp.int32, (FACE, FACE), 0)
    return jnp.where(place == index, 1.0, 0.0).astype(bf16)


def layer_of(strips, z):
    return jnp.concatenate([strips[q, pl.ds(z, K, stride=CZ), :] for q in range(4)], axis=1)


def pick_kernel(vectors_hbm, sigma_hbm, index_hbm, counts_hbm, strips, own_ref, ahead_ref, behind_ref, tails_ref, top_ref, bottom_ref, live_ref, sigma_ref, index_ref, counts_ref, choice_ref, hot_ref, sems):
    small = [
        pltpu.make_async_copy(sigma_hbm, sigma_ref, sems.at[4]),
        pltpu.make_async_copy(index_hbm, index_ref, sems.at[5]),
        pltpu.make_async_copy(counts_hbm, counts_ref, sems.at[6]),
    ]
    large = [
        pltpu.make_async_copy(vectors_hbm.at[:, pl.ds(128 * q, 128)], strips.at[q], sems.at[q])
        for q in range(4)
    ]
    for copy in small + large:
        copy.start()
    lane = lax.broadcasted_iota(jnp.int32, (1, 256), 1)
    within = lane % 128
    cell_of_lane = (within % CY) * CX + jnp.where(lane >= 128, CX - 1, 0)
    cell = lax.broadcasted_iota(jnp.int32, (FACE, 256), 0)
    for step in range(4):
        chosen = jnp.where(within // CY == step, cell_of_lane, -1)
        choice_ref[step] = jnp.where(cell == chosen, 1.0, 0.0).astype(bf16)
    for copy in small:
        copy.wait()

    def faces_of(rows_of_layer, count):
        total = jnp.zeros((4 * count, 256), f32)
        for step in range(4):
            groups = [rows_of_layer(4 * group + step) for group in range(4)]
            total = total + product(jnp.concatenate(groups, axis=0), choice_ref[step], MATRIX)
        return [
            jnp.concatenate(
                [
                    total[count * group : count * (group + 1), 128 * side : 128 * (side + 1)]
                    for group in range(4)
                ],
                axis=1,
            )
            for side in range(2)
        ]

    def sigma_rows(z):
        high, low = halves(jnp.broadcast_to(sigma_ref[z : z + 1, :], (8, FACE)))
        return jnp.concatenate([high.astype(f32), low.astype(f32)], axis=0).astype(bf16)

    along = lax.broadcasted_iota(jnp.int32, (1, FACE), 1)
    sigma_faces = faces_of(sigma_rows, 16)
    for slot in range(2 * REACH):
        side = slot // REACH
        live_ref[slot : slot + 1] = jnp.where(along < counts_ref[slot], 1.0, 0.0)
        cell_index = index_ref[slot : slot + 1, :]
        wanted = (cell_index >> 9) * CY + ((cell_index >> 4) & (CY - 1))
        hot_ref[slot] = one_hot(wanted)
        found = product(sigma_faces[side].astype(bf16), hot_ref[slot], MATRIX)
        row = slot - REACH if side else 8 + REACH - 1 - slot
        tails_ref[row : row + 1] = found[:1] + found[8:9]
        tails_ref[4 + row : 5 + row] = wanted.astype(f32)
    for copy in large:
        copy.wait()
    for out_ref, z in ((bottom_ref, 0), (top_ref, CZ - 1)):
        out_ref[:K] = layer_of(strips, z)
        out_ref[K:] = jnp.broadcast_to(sigma_ref[z : z + 1, :], (8, FACE))
    faces = faces_of(lambda z: stacked(layer_of(strips, z)), 2 * K)
    for side, face_ref in ((0, behind_ref), (1, ahead_ref)):
        face_ref[...] = faces[side][:K] + faces[side][K:]
        table = faces[side].astype(bf16)
        for slot in range(REACH * side, REACH * (side + 1)):
            own_ref[slot] = product(table, hot_ref[slot], MATRIX).astype(bf16)


def own_kernel(strips, sigma_ref, storage_ref, top_ref, bottom_ref, below_ref, above_ref, own_ref, lower_ref):
    sigma = sigma_ref[...]
    lane = lax.broadcasted_iota(jnp.int32, (CZ, FACE), 1)
    layer = lax.broadcasted_iota(jnp.int32, (CZ, FACE), 0)
    along_x = jnp.where(
        lane % CX == CX - 1, 0.0, harmonic(sigma, pltpu.roll(sigma, FACE - 1, 1))
    )
    along_y = jnp.where(
        lane >= FACE - CX, 0.0, harmonic(sigma, pltpu.roll(sigma, FACE - CX, 1))
    )
    along_z = jnp.where(layer == CZ - 1, 0.0, harmonic(sigma, pltpu.roll(sigma, CZ - 1, 0)))
    level = lax.axis_index("coarse")
    downward = harmonic(bottom_ref[K : K + 1, :], below_ref[K : K + 1, :])
    downward = jnp.where(level == 0, 0.0, downward)
    upward = harmonic(top_ref[K : K + 1, :], above_ref[K : K + 1, :])
    upward = jnp.where(level == lax.axis_size("coarse") - 1, 0.0, upward)
    half = 0.5 * (
        storage_ref[...]
        + along_x
        + pltpu.roll(along_x, 1, 1)
        + along_y
        + pltpu.roll(along_y, CX, 1)
        + along_z
        + pltpu.roll(along_z, 1, 0)
        + jnp.where(layer == 0, downward, 0.0)
        + jnp.where(layer == CZ - 1, upward, 0.0)
    )
    total = jnp.zeros((2 * K, 2 * K), f32)
    below = layer_of(strips, 0)
    for z in range(CZ):
        now = below
        applied = half[z : z + 1] * now
        applied = applied - along_x[z : z + 1] * pltpu.roll(now, FACE - 1, 1)
        applied = applied - along_y[z : z + 1] * pltpu.roll(now, FACE - CX, 1)
        if z < CZ - 1:
            below = layer_of(strips, z + 1)
            applied = applied - along_z[z : z + 1] * below
        total = total + product(stacked(now), stacked(applied), GRAM)
    own = quadrants(total)
    own_ref[...] = own + own.T
    weighted = stacked(bottom_ref[:K, :] * downward)
    lower_ref[...] = -quadrants(product(weighted, stacked(below_ref[:K, :]), GRAM))


def pack_kernel(ahead, behind, ahead2, behind2, ahead4, behind4, out_ref):
    mine = lax.axis_index("sub") % 2
    for core, chosen in ((0, (ahead, ahead2, behind2, behind4)), (1, (ahead2, ahead4, behind, behind2))):
        @pl.when(mine == core)
        def _(chosen=chosen):
            for at, ref in enumerate(chosen):
                out_ref[K * at : K * (at + 1)] = ref[...]


def pair_kernel(own, other, ahead_ref, behind_ref):
    ahead_ref[:8] = own[:8]
    ahead_ref[8:] = other[:8]
    behind_ref[:8] = own[8:]
    behind_ref[8:] = other[8:]


def join_kernel(first, second, out_ref):
    out_ref[:16] = first[...]
    out_ref[16:] = second[...]


OFFSETS = (-4, -3, -2, -1, 1, 2, 3, 4)


def tails_by_slot(other, before, after, swapped):
    even = lax.axis_index("sub") % 2 == 0
    low, high = slice(0, 8), slice(8, 16)
    before1 = jnp.where(even, before[...], swapped[:16])
    before2 = jnp.where(even, swapped[:16], before[...])
    after1 = jnp.where(even, after[...], swapped[16:])
    after2 = jnp.where(even, swapped[16:], after[...])
    on_even = (before2[high], before2[low], before1[low], before1[high], other[high], after1[low], after1[high], after2[high])
    on_odd = (before2[low], before1[low], before1[high], other[low], after1[low], after1[high], after2[high], after2[low])
    return [jnp.where(even, x, y) for x, y in zip(on_even, on_odd, strict=True)]


def partner_face(refs, offset):
    ahead2, behind2, ahead4, behind4, swapped = refs
    if offset % 2:
        at = {-1: 0, -3: 1, 1: 2, 3: 3}[offset]
        return swapped[K * at : K * at + K]
    return {-2: ahead2, -4: ahead4, 2: behind2, 4: behind4}[offset][...]


def weighted_rows(own_ref, slot, weight):
    rows = own_ref[slot]
    return stacked((rows[:K].astype(f32) + rows[K:].astype(f32)) * weight)


def block_kernel(live_ref, own_block, lower_block, own_ref, own_tails, *refs):
    *tails, out_ref, weight_ref, index_ref = refs
    total = jnp.zeros((2 * K, 2 * K), f32)
    found = tails_by_slot(*tails)
    for slot, offset in enumerate(OFFSETS):
        reach = abs(offset) - 1
        row = reach if offset > 0 else 8 + reach
        pair = harmonic(own_tails[row : row + 1], found[slot][reach : reach + 1])
        weight = jnp.where(live_ref[slot : slot + 1] > 0.0, pair, 0.0)
        weight_ref[slot : slot + 1] = weight
        index_ref[slot : slot + 1] = found[slot][4 + reach : 5 + reach].astype(jnp.int32)
        total = total + product(weighted_rows(own_ref, slot, weight), own_ref[slot], GRAM)
    level = lax.axis_index("coarse")
    extra = quadrants(total)
    own = own_block[...] + 0.5 * (extra + extra.T)
    lower = lower_block[...]
    even = level % 2 == 0
    payload = jnp.where(
        even, jnp.concatenate([own, lower], axis=1), jnp.concatenate([lower, own], axis=1)
    )
    for copy in range(8):
        out_ref[copy] = payload


def panel_kernel(weight_ref, index_ref, own_ref, *refs):
    faces, inverse, out_ref = refs[:5], refs[5], refs[6]
    blocks = []
    for slot, offset in enumerate(OFFSETS):
        select = one_hot(index_ref[slot : slot + 1, :])
        found = product(stacked(partner_face(faces, offset)), select, MATRIX).astype(bf16)
        weighted = weighted_rows(own_ref, slot, -weight_ref[slot : slot + 1])
        blocks.append(quadrants(product(weighted, found, GRAM)))
    high, low = halves(jnp.concatenate(blocks, axis=1))
    left_high, left_low = halves(inverse[:, :K])
    left = jnp.concatenate([left_high, left_low, left_high], axis=1)
    out_ref[...] = product(left, jnp.concatenate([high, high, low], axis=0), MATRIX)


def thirds(x):
    high = x.astype(bf16)
    rest = x - high.astype(f32)
    middle = rest.astype(bf16)
    return high, middle, (rest - middle.astype(f32)).astype(bf16)


def fine_product(left, right):
    a, b, c = thirds(left)
    p, q, r = thirds(right)
    first = product(jnp.concatenate([a, b, c], axis=0), p, MATRIX)
    second = product(jnp.concatenate([a, b], axis=0), q, MATRIX)
    small = product(a, r, MATRIX) + first[2 * K :] + second[K:]
    return first[:K] + (first[K : 2 * K] + second[:K] + small)


def lane_of(x, lane):
    index = jnp.full(x.shape, lane, jnp.int32)
    return jnp.take_along_axis(x, index, axis=1, mode="promise_in_bounds")


def sublane_of(x, sublane):
    index = jnp.full(x.shape, sublane, jnp.int32)
    return jnp.take_along_axis(x, index, axis=0, mode="promise_in_bounds")


def eliminate(rows, right, offset, lane, sub):
    wide = (8, 128)
    kept_rows, kept_right_rows = [], []
    for panel in range(8):
        first = offset + 8 * panel
        column = [
            {
                g: lane_of(rows[g], first + k)
                for g in range(panel, 8)
            }
            for k in range(8)
        ]
        pivot = [[None] * 8 for _ in range(8)]
        for i in range(8):
            for k in range(i, 8):
                pivot[i][k] = sublane_of(column[i][panel], k)
        left_row = [sublane_of(rows[panel], k) for k in range(8)]
        right_row = [sublane_of(right[panel], k) for k in range(8)]
        kept = jnp.zeros(wide, f32)
        kept_right = jnp.zeros(wide, f32)
        for i in range(8):
            scale = lax.rsqrt(pivot[i][i])
            inverse = 1.0 / pivot[i][i]
            kept = jnp.where(sub == i, left_row[i] * scale, kept)
            kept_right = jnp.where(sub == i, right_row[i] * scale, kept_right)
            left_row[i] = left_row[i] * inverse
            right_row[i] = right_row[i] * inverse
            scaled = [None] * 8
            for l in range(i + 1, 8):
                scaled[l] = pivot[i][l] * inverse
            for k in range(8):
                if k == i:
                    continue
                by = pivot[i][k] if k > i else pivot[k][i]
                left_row[k] = left_row[k] - by * left_row[i]
                right_row[k] = right_row[k] - by * right_row[i]
                for l in range(max(i + 1, k), 8):
                    pivot[k][l] = pivot[k][l] - by * scaled[l]
            pivot[i] = scaled
        for g in range(panel + 1, 8):
            for k in range(8):
                rows[g] = rows[g] - column[k][g] * left_row[k]
                right[g] = right[g] - column[k][g] * right_row[k]
        live = (lane >= first + sub) if offset else ((lane >= first + sub) | (lane >= K))
        if offset:
            live = live | (lane < K)
        kept_rows.append(jnp.where(live, kept, 0.0))
        kept_right_rows.append(kept_right)
    return jnp.concatenate(kept_rows, axis=0), jnp.concatenate(kept_right_rows, axis=0)


def half_factor(begin, level, blocks_ref, factor_ref, cross, top, top_right, inverse):
    lane = lax.broadcasted_iota(jnp.int32, (8, 128), 1)
    sub = lax.broadcasted_iota(jnp.int32, (8, 128), 0)
    wide_lane = lax.broadcasted_iota(jnp.int32, (K, 2 * K), 1)
    wide_sub = lax.broadcasted_iota(jnp.int32, (K, 2 * K), 0)
    zero = jnp.zeros((K, 2 * K), f32)
    at = [pl.ds(8 * g, 8) for g in range(8)]
    for c in range(4 * begin + 1, min(4 * begin + 5, 8)):
        block = blocks_ref[c]
        if c % 2 == 1:
            cross[c - 1] = jnp.concatenate([zero, block], axis=0).T[:K]
        else:
            cross[c - 1] = jnp.concatenate([block, zero], axis=0).T[K:]
    if begin:
        cross[7] = zero

    def unit(c):
        return jnp.where((wide_lane == wide_sub) & (level == c), 1.0, 0.0)

    if not begin:
        top[...] = blocks_ref[0]
        top_right[...] = unit(0)

    @pl.loop(2 * begin, 2 * begin + 2)
    def _(q):
        c = 2 * q
        last = q == 3
        rows = [jnp.where(lane < K, top[at[g], :], cross[c, at[g], :]) for g in range(8)]
        right = [top_right[at[g], :] for g in range(8)]
        even, even_right = eliminate(rows, right, 0, lane, sub)
        even_turned = even.T
        taken = fine_product(even_turned[K:], jnp.concatenate([even, even_right], axis=1))
        under = blocks_ref[c + 1] - taken[:, : 2 * K]
        under_right = unit(c + 1) - taken[:, 2 * K :]
        rows = [jnp.where(lane < K, cross[c + 1, at[g], :], under[8 * g : 8 * g + 8]) for g in range(8)]
        right = [under_right[8 * g : 8 * g + 8] for g in range(8)]
        odd, odd_right = eliminate(rows, right, K, lane, sub)
        odd_turned = odd.T
        taken = fine_product(odd_turned[:K], jnp.concatenate([odd, odd_right], axis=1))
        top[...] = jnp.where(last, 0.0, blocks_ref[jnp.minimum(c + 2, 7)]) - taken[:, : 2 * K]
        top_right[...] = unit(c + 2) - taken[:, 2 * K :]
        start = pl.multiple_of(128 * q, 128)
        inverse[pl.ds(start, K), :] = even_right
        inverse[pl.ds(start + K, K), :] = odd_right
        both = jnp.concatenate([even_turned, odd_turned], axis=1)
        cols = pl.ds(start, 128)
        factor_ref[pl.ds(start, K), cols] = jnp.where(wide_lane < K, both[:K], 0.0)
        factor_ref[pl.ds(start + K, K), cols] = both[K:]

        @pl.when(q < 3)
        def _():
            factor_ref[pl.ds(start + 128, K), cols] = jnp.where(wide_lane < K, 0.0, both[:K])


def first_half(blocks_ref, factor_ref, inverse, top, top_right, cross):
    factor_ref[...] = jnp.zeros((5 * K, 4 * K), f32)
    half_factor(0, lax.axis_index("coarse"), blocks_ref, factor_ref, cross, top, top_right, inverse)


def second_half(blocks_ref, part_ref, first_inverse, first_top, first_right, factor_ref, inverse, cross, top, top_right):
    factor_ref[: 5 * K, : 4 * K] = part_ref[...]
    factor_ref[5 * K :, : 4 * K] = jnp.zeros((3 * K, 4 * K), f32)
    factor_ref[:, 4 * K :] = jnp.zeros((8 * K, 4 * K), f32)
    inverse[: 4 * K, :] = first_inverse[...]
    top[...] = first_top[...]
    top_right[...] = first_right[...]
    half_factor(1, lax.axis_index("coarse"), blocks_ref, factor_ref, cross, top, top_right, inverse)


HBM = pl.BlockSpec(memory_space=pltpu.HBM)


def call(kernel, name, outs, operands, hbm=0, flops=10**8, scratch=(), limit=16):
    return pl.pallas_call(
        kernel,
        out_shape=outs,
        in_specs=[HBM] * hbm + [VMEM] * (len(operands) - hbm),
        out_specs=jax.tree.map(lambda _: VMEM, outs),
        scratch_shapes=scratch,
        compiler_params=pltpu.CompilerParams(vmem_limit_bytes=limit * 2**20),
        cost_estimate=pl.CostEstimate(flops=flops, bytes_accessed=2 * 10**6, transcendentals=1000),
        name=name,
    )(*operands)


def array(*shape, dtype=f32):
    return jax.ShapeDtypeStruct(shape, dtype)


FIRST = (array(5 * K, 4 * K), array(4 * K, 2 * K), array(K, 2 * K), array(K, 2 * K))


def passed_along(block, axis, distance):
    count = lax.axis_size(axis)
    return lax.ppermute(block, axis, [(i, (i + distance) % count) for i in range(count)])


def body(deflation, conductivity, storage, interface_rows, interface_counts):
    vectors = deflation[0].reshape(K * CZ, FACE)
    sigma = conductivity[0]
    counts = interface_counts.reshape(2 * REACH)
    strips, mine, ahead, behind, own_tails, top, bottom, live = call(
        pick_kernel,
        "pick",
        (
            array(4, K * CZ, 128),
            array(8, 2 * K, FACE, dtype=bf16),
            array(K, FACE),
            array(K, FACE),
            array(16, FACE),
            array(ROWS, FACE),
            array(ROWS, FACE),
            array(8, FACE),
        ),
        tuple(
            pltpu.with_memory_space_constraint(x, pltpu.HBM)
            for x in (vectors, sigma, interface_rows[0, 0], counts)
        ),
        hbm=4,
        scratch=(
            pltpu.VMEM((CZ, FACE), f32),
            pltpu.VMEM((2 * REACH, FACE), jnp.int32),
            pltpu.SMEM((2 * REACH,), jnp.int32),
            pltpu.VMEM((4, FACE, 256), bf16),
            pltpu.VMEM((2 * REACH, FACE, FACE), bf16),
            pltpu.SemaphoreType.DMA((7,)),
        ),
    )
    count = lax.axis_size("sub")
    swap = [(i, i ^ 1) for i in range(count)]
    other_tails = lax.ppermute(own_tails, "sub", swap)
    below = passed_along(top, "coarse", 1)
    above = passed_along(bottom, "coarse", -1)
    go_ahead, go_behind = call(
        pair_kernel, "pair", (array(16, FACE), array(16, FACE)), (own_tails, other_tails), flops=10**6
    )
    far = [(i, (i + 2 + 2 * (i % 2)) % count) for i in range(count)]
    before = lax.ppermute(go_ahead, "sub", far)
    after = lax.ppermute(go_behind, "sub", [(j, i) for i, j in far])
    own, lower = call(
        own_kernel,
        "own",
        (array(K, K), array(K, K)),
        (strips, sigma, storage[0], top, bottom, below, above),
    )
    (before, after), (own, lower) = lax.optimization_barrier(((before, after), (own, lower)))
    both = call(join_kernel, "join", array(32, FACE), (before, after), flops=10**6)
    swapped_tails = lax.ppermute(both, "sub", swap)
    payload, weight, index = call(
        block_kernel,
        "block",
        (array(8, K, 2 * K), array(8, FACE), array(8, FACE, dtype=jnp.int32)),
        (live, own, lower, mine, own_tails, other_tails, before, after, swapped_tails),
    )
    (ahead, behind), payload = lax.optimization_barrier(((ahead, behind), payload))
    blocks = lax.all_to_all(payload, "coarse", 0, 0)
    faces = (
        passed_along(ahead, "sub", 2),
        passed_along(behind, "sub", -2),
        passed_along(ahead, "sub", 4),
        passed_along(behind, "sub", -4),
    )
    state = call(
        first_half,
        "factor_first",
        FIRST,
        (blocks,),
        flops=10**9,
        scratch=(pltpu.VMEM((8, K, 2 * K), f32),),
    )
    faces, state = lax.optimization_barrier((faces, state))
    packed = call(pack_kernel, "faces", array(4 * K, FACE), (ahead, behind, *faces), flops=10**6)
    faces = (*faces, lax.ppermute(packed, "sub", swap))
    factor, inverse = call(
        second_half,
        "factor_second",
        (array(8 * K, 8 * K), array(8 * K, 2 * K)),
        (blocks, *state),
        flops=10**9,
        scratch=(pltpu.VMEM((8, K, 2 * K), f32), pltpu.VMEM((K, 2 * K), f32), pltpu.VMEM((K, 2 * K), f32)),
    )
    panel = call(
        panel_kernel,
        "panel",
        array(8 * K, 8 * K),
        (weight, index, mine, *faces, inverse),
    )
    return (factor[None], panel[None, None])


def solution(mesh):
    placed = (
        P("sub", None, "coarse", None),
        P("sub", "coarse", None),
        P("sub", "coarse", None),
        P("sub", "coarse", None, None),
        P("sub", "coarse", None),
    )
    return jax.shard_map(
        body,
        mesh=mesh,
        in_specs=placed,
        out_specs=(P("sub", None, None), P("sub", "coarse", None, None)),
        check_vma=False,
    )
```

```python
import functools

import jax
import jax.numpy as jnp
from jax import lax
from jax.experimental import pallas as pl
from jax.experimental.pallas import tpu as pltpu
from jax.sharding import PartitionSpec as P

K = 64
CX = 16
CY = 32
CZ = 16
FACE = 512
REACH = 4
ROWS = K + 8

f32 = jnp.float32
bf16 = jnp.bfloat16
VMEM = pl.BlockSpec(memory_space=pltpu.VMEM)
MATRIX = (((1,), (0,)), ((), ()))
GRAM = (((1,), (1,)), ((), ()))


def product(left, right, dims):
    return lax.dot_general(left, right, dims, preferred_element_type=f32)


def harmonic(first, second):
    return 2.0 * first * second / (first + second)


def halves(x):
    high = x.astype(bf16)
    return high, (x - high.astype(f32)).astype(bf16)


def stacked(x):
    return jnp.concatenate(halves(x), axis=0)


def quadrants(square):
    half = square[:K] + square[K:]
    return half[:, :K] + half[:, K:]


def gathered(table, index):
    strips = []
    for q in range(4):
        wanted = jnp.broadcast_to(index[:, 128 * q : 128 * (q + 1)], (8, 128))
        found = None
        for strip in range(4):
            part = jnp.take_along_axis(
                table[:, 128 * strip : 128 * (strip + 1)],
                wanted & 127,
                axis=1,
                mode="promise_in_bounds",
            )
            found = part if strip == 0 else jnp.where(wanted >> 7 == strip, part, found)
        strips.append(found)
    return jnp.concatenate(strips, axis=1)


def one_hot(index):
    place = lax.broadcasted_iota(jnp.int32, (FACE, FACE), 0)
    return jnp.where(place == index, 1.0, 0.0).astype(bf16)


def layer_of(strips, z):
    return jnp.concatenate([strips[q, pl.ds(z, K, stride=CZ), :] for q in range(4)], axis=1)


def face_kernel(vectors_hbm, sigma_hbm, index_hbm, counts_hbm, strips, ahead_ref, behind_ref, tails_ref, top_ref, bottom_ref, live_ref, wanted_ref, sigma_ref, index_ref, counts_ref, choice_ref, sems):
    small = [
        pltpu.make_async_copy(sigma_hbm, sigma_ref, sems.at[4]),
        pltpu.make_async_copy(index_hbm, index_ref, sems.at[5]),
        pltpu.make_async_copy(counts_hbm, counts_ref, sems.at[6]),
    ]
    large = [
        pltpu.make_async_copy(vectors_hbm.at[:, pl.ds(128 * q, 128)], strips.at[q], sems.at[q])
        for q in range(4)
    ]
    for copy in small + large:
        copy.start()
    lane = lax.broadcasted_iota(jnp.int32, (1, 256), 1)
    within = lane % 128
    cell_of_lane = (within % CY) * CX + jnp.where(lane >= 128, CX - 1, 0)
    cell = lax.broadcasted_iota(jnp.int32, (FACE, 256), 0)
    for step in range(4):
        chosen = jnp.where(within // CY == step, cell_of_lane, -1)
        choice_ref[step] = jnp.where(cell == chosen, 1.0, 0.0).astype(bf16)
    for copy in small:
        copy.wait()

    def faces_of(rows_of_layer, count):
        total = jnp.zeros((4 * count, 256), f32)
        for step in range(4):
            groups = [rows_of_layer(4 * group + step) for group in range(4)]
            total = total + product(jnp.concatenate(groups, axis=0), choice_ref[step], MATRIX)
        return [
            jnp.concatenate(
                [
                    total[count * group : count * (group + 1), 128 * side : 128 * (side + 1)]
                    for group in range(4)
                ],
                axis=1,
            )
            for side in range(2)
        ]

    def sigma_rows(z):
        high, low = halves(jnp.broadcast_to(sigma_ref[z : z + 1, :], (8, FACE)))
        return jnp.concatenate([high.astype(f32), low.astype(f32)], axis=0).astype(bf16)

    along = lax.broadcasted_iota(jnp.int32, (1, FACE), 1)
    sigma_faces = faces_of(sigma_rows, 16)
    for slot in range(2 * REACH):
        side = slot // REACH
        live_ref[slot : slot + 1] = jnp.where(along < counts_ref[slot], 1.0, 0.0)
        cell_index = index_ref[slot : slot + 1, :]
        wanted = (cell_index >> 9) * CY + ((cell_index >> 4) & (CY - 1))
        wanted_ref[slot : slot + 1] = wanted
        found = gathered(sigma_faces[side][:8] + sigma_faces[side][8:], wanted)
        row = slot - REACH if side else 8 + REACH - 1 - slot
        tails_ref[row : row + 1] = found[:1]
        tails_ref[4 + row : 5 + row] = wanted.astype(f32)
    for copy in large:
        copy.wait()
    for out_ref, z in ((bottom_ref, 0), (top_ref, CZ - 1)):
        out_ref[:K] = layer_of(strips, z)
        out_ref[K:] = jnp.broadcast_to(sigma_ref[z : z + 1, :], (8, FACE))
    faces = faces_of(lambda z: stacked(layer_of(strips, z)), 2 * K)
    for side, face_ref in ((0, behind_ref), (1, ahead_ref)):
        face_ref[...] = faces[side][:K] + faces[side][K:]


def row_kernel(ahead_ref, behind_ref, wanted_ref, top_ref, bottom_ref, below_ref, above_ref, own_ref, square_ref, lower_ref):
    for side, face_ref in ((0, behind_ref), (1, ahead_ref)):
        table = stacked(face_ref[...])
        for slot in range(REACH * side, REACH * (side + 1)):
            select = one_hot(wanted_ref[slot : slot + 1, :])
            own_ref[slot] = product(table, select, MATRIX).astype(bf16)
    level = lax.axis_index("coarse")
    downward = harmonic(bottom_ref[K : K + 1, :], below_ref[K : K + 1, :])
    downward = jnp.where(level == 0, 0.0, downward)
    upward = harmonic(top_ref[K : K + 1, :], above_ref[K : K + 1, :])
    upward = jnp.where(level == lax.axis_size("coarse") - 1, 0.0, upward)
    top, bottom = top_ref[:K, :], bottom_ref[:K, :]
    weighted = stacked(bottom * downward)
    square = product(stacked(top * upward), stacked(top), GRAM)
    square_ref[...] = quadrants(square + product(weighted, stacked(bottom), GRAM))
    lower_ref[...] = -quadrants(product(weighted, stacked(below_ref[:K, :]), GRAM))


def own_kernel(strips, sigma_ref, storage_ref, own_ref):
    sigma = sigma_ref[...]
    lane = lax.broadcasted_iota(jnp.int32, (CZ, FACE), 1)
    layer = lax.broadcasted_iota(jnp.int32, (CZ, FACE), 0)
    along_x = jnp.where(
        lane % CX == CX - 1, 0.0, harmonic(sigma, pltpu.roll(sigma, FACE - 1, 1))
    )
    along_y = jnp.where(
        lane >= FACE - CX, 0.0, harmonic(sigma, pltpu.roll(sigma, FACE - CX, 1))
    )
    along_z = jnp.where(layer == CZ - 1, 0.0, harmonic(sigma, pltpu.roll(sigma, CZ - 1, 0)))
    half = 0.5 * (
        storage_ref[...]
        + along_x
        + pltpu.roll(along_x, 1, 1)
        + along_y
        + pltpu.roll(along_y, CX, 1)
        + along_z
        + pltpu.roll(along_z, 1, 0)
    )
    total = jnp.zeros((2 * K, 2 * K), f32)
    below = layer_of(strips, 0)
    for z in range(CZ):
        now = below
        applied = half[z : z + 1] * now
        applied = applied - along_x[z : z + 1] * pltpu.roll(now, FACE - 1, 1)
        applied = applied - along_y[z : z + 1] * pltpu.roll(now, FACE - CX, 1)
        if z < CZ - 1:
            below = layer_of(strips, z + 1)
            applied = applied - along_z[z : z + 1] * below
        total = total + product(stacked(now), stacked(applied), GRAM)
    own = quadrants(total)
    own_ref[...] = own + own.T


def pack_kernel(ahead, behind, ahead2, behind2, ahead4, behind4, out_ref):
    mine = lax.axis_index("sub") % 2
    for core, chosen in ((0, (ahead, ahead2, behind2, behind4)), (1, (ahead2, ahead4, behind, behind2))):
        @pl.when(mine == core)
        def _(chosen=chosen):
            for at, ref in enumerate(chosen):
                out_ref[K * at : K * (at + 1)] = ref[...]


def pair_kernel(own, other, ahead_ref, behind_ref):
    ahead_ref[:8] = own[:8]
    ahead_ref[8:] = other[:8]
    behind_ref[:8] = own[8:]
    behind_ref[8:] = other[8:]


def join_kernel(first, second, out_ref):
    out_ref[:16] = first[...]
    out_ref[16:] = second[...]


OFFSETS = (-4, -3, -2, -1, 1, 2, 3, 4)


def tails_by_slot(other, before, after, swapped):
    even = lax.axis_index("sub") % 2 == 0
    low, high = slice(0, 8), slice(8, 16)
    before1 = jnp.where(even, before[...], swapped[:16])
    before2 = jnp.where(even, swapped[:16], before[...])
    after1 = jnp.where(even, after[...], swapped[16:])
    after2 = jnp.where(even, swapped[16:], after[...])
    on_even = (before2[high], before2[low], before1[low], before1[high], other[high], after1[low], after1[high], after2[high])
    on_odd = (before2[low], before1[low], before1[high], other[low], after1[low], after1[high], after2[high], after2[low])
    return [jnp.where(even, x, y) for x, y in zip(on_even, on_odd, strict=True)]


def partner_face(refs, offset):
    ahead2, behind2, ahead4, behind4, swapped = refs
    if offset % 2:
        at = {-1: 0, -3: 1, 1: 2, 3: 3}[offset]
        return swapped[K * at : K * at + K]
    return {-2: ahead2, -4: ahead4, 2: behind2, 4: behind4}[offset][...]


def weighted_rows(own_ref, slot, weight):
    rows = own_ref[slot]
    return stacked((rows[:K].astype(f32) + rows[K:].astype(f32)) * weight)


def block_kernel(live_ref, own_block, square_block, lower_block, own_ref, own_tails, *refs):
    *tails, out_ref, weight_ref, index_ref = refs
    total = jnp.zeros((2 * K, 2 * K), f32)
    found = tails_by_slot(*tails)
    for slot, offset in enumerate(OFFSETS):
        reach = abs(offset) - 1
        row = reach if offset > 0 else 8 + reach
        pair = harmonic(own_tails[row : row + 1], found[slot][reach : reach + 1])
        weight = jnp.where(live_ref[slot : slot + 1] > 0.0, pair, 0.0)
        weight_ref[slot : slot + 1] = weight
        index_ref[slot : slot + 1] = found[slot][4 + reach : 5 + reach].astype(jnp.int32)
        total = total + product(weighted_rows(own_ref, slot, weight), own_ref[slot], GRAM)
    level = lax.axis_index("coarse")
    extra = quadrants(total) + square_block[...]
    own = own_block[...] + 0.5 * (extra + extra.T)
    lower = lower_block[...]
    even = level % 2 == 0
    payload = jnp.where(
        even, jnp.concatenate([own, lower], axis=1), jnp.concatenate([lower, own], axis=1)
    )
    for copy in range(8):
        out_ref[copy] = payload


def panel_kernel(weight_ref, index_ref, own_ref, *refs):
    faces, inverse, out_ref = refs[:5], refs[5], refs[6]
    blocks = []
    for slot, offset in enumerate(OFFSETS):
        select = one_hot(index_ref[slot : slot + 1, :])
        found = product(stacked(partner_face(faces, offset)), select, MATRIX).astype(bf16)
        weighted = weighted_rows(own_ref, slot, -weight_ref[slot : slot + 1])
        blocks.append(quadrants(product(weighted, found, GRAM)))
    high, low = halves(jnp.concatenate(blocks, axis=1))
    left_high, left_low = halves(inverse[:, :K])
    left = jnp.concatenate([left_high, left_low, left_high], axis=1)
    out_ref[...] = product(left, jnp.concatenate([high, high, low], axis=0), MATRIX)


def thirds(x):
    high = x.astype(bf16)
    rest = x - high.astype(f32)
    middle = rest.astype(bf16)
    return high, middle, (rest - middle.astype(f32)).astype(bf16)


def fine_product(left, right):
    a, b, c = thirds(left)
    p, q, r = thirds(right)
    first = product(jnp.concatenate([a, b, c], axis=0), p, MATRIX)
    second = product(jnp.concatenate([a, b], axis=0), q, MATRIX)
    small = product(a, r, MATRIX) + first[2 * K :] + second[K:]
    return first[:K] + (first[K : 2 * K] + second[:K] + small)


def lane_of(x, lane):
    index = jnp.full(x.shape, lane, jnp.int32)
    return jnp.take_along_axis(x, index, axis=1, mode="promise_in_bounds")


def sublane_of(x, sublane):
    index = jnp.full(x.shape, sublane, jnp.int32)
    return jnp.take_along_axis(x, index, axis=0, mode="promise_in_bounds")


def eliminate(rows, right, offset, lane, sub):
    wide = (8, 128)
    kept_rows, kept_right_rows = [], []
    for panel in range(8):
        first = offset + 8 * panel
        column = [
            {
                g: lane_of(rows[g], first + k)
                for g in range(panel, 8)
            }
            for k in range(8)
        ]
        pivot = [[None] * 8 for _ in range(8)]
        for i in range(8):
            for k in range(i, 8):
                pivot[i][k] = sublane_of(column[i][panel], k)
        left_row = [sublane_of(rows[panel], k) for k in range(8)]
        right_row = [sublane_of(right[panel], k) for k in range(8)]
        kept = jnp.zeros(wide, f32)
        kept_right = jnp.zeros(wide, f32)
        for i in range(8):
            scale = lax.rsqrt(pivot[i][i])
            inverse = 1.0 / pivot[i][i]
            kept = jnp.where(sub == i, left_row[i] * scale, kept)
            kept_right = jnp.where(sub == i, right_row[i] * scale, kept_right)
            left_row[i] = left_row[i] * inverse
            right_row[i] = right_row[i] * inverse
            scaled = [None] * 8
            for l in range(i + 1, 8):
                scaled[l] = pivot[i][l] * inverse
            for k in range(8):
                if k == i:
                    continue
                by = pivot[i][k] if k > i else pivot[k][i]
                left_row[k] = left_row[k] - by * left_row[i]
                right_row[k] = right_row[k] - by * right_row[i]
                for l in range(max(i + 1, k), 8):
                    pivot[k][l] = pivot[k][l] - by * scaled[l]
            pivot[i] = scaled
        for g in range(panel + 1, 8):
            for k in range(8):
                rows[g] = rows[g] - column[k][g] * left_row[k]
                right[g] = right[g] - column[k][g] * right_row[k]
        live = (lane >= first + sub) if offset else ((lane >= first + sub) | (lane >= K))
        if offset:
            live = live | (lane < K)
        kept_rows.append(jnp.where(live, kept, 0.0))
        kept_right_rows.append(kept_right)
    return jnp.concatenate(kept_rows, axis=0), jnp.concatenate(kept_right_rows, axis=0)


def half_factor(begin, level, blocks_ref, factor_ref, cross, top, top_right, inverse):
    lane = lax.broadcasted_iota(jnp.int32, (8, 128), 1)
    sub = lax.broadcasted_iota(jnp.int32, (8, 128), 0)
    wide_lane = lax.broadcasted_iota(jnp.int32, (K, 2 * K), 1)
    wide_sub = lax.broadcasted_iota(jnp.int32, (K, 2 * K), 0)
    zero = jnp.zeros((K, 2 * K), f32)
    at = [pl.ds(8 * g, 8) for g in range(8)]
    for c in range(4 * begin + 1, min(4 * begin + 5, 8)):
        block = blocks_ref[c]
        if c % 2 == 1:
            cross[c - 1] = jnp.concatenate([zero, block], axis=0).T[:K]
        else:
            cross[c - 1] = jnp.concatenate([block, zero], axis=0).T[K:]
    if begin:
        cross[7] = zero

    def unit(c):
        return jnp.where((wide_lane == wide_sub) & (level == c), 1.0, 0.0)

    if not begin:
        top[...] = blocks_ref[0]
        top_right[...] = unit(0)

    @pl.loop(2 * begin, 2 * begin + 2)
    def _(q):
        c = 2 * q
        last = q == 3
        rows = [jnp.where(lane < K, top[at[g], :], cross[c, at[g], :]) for g in range(8)]
        right = [top_right[at[g], :] for g in range(8)]
        even, even_right = eliminate(rows, right, 0, lane, sub)
        even_turned = even.T
        taken = fine_product(even_turned[K:], jnp.concatenate([even, even_right], axis=1))
        under = blocks_ref[c + 1] - taken[:, : 2 * K]
        under_right = unit(c + 1) - taken[:, 2 * K :]
        rows = [jnp.where(lane < K, cross[c + 1, at[g], :], under[8 * g : 8 * g + 8]) for g in range(8)]
        right = [under_right[8 * g : 8 * g + 8] for g in range(8)]
        odd, odd_right = eliminate(rows, right, K, lane, sub)
        odd_turned = odd.T
        taken = fine_product(odd_turned[:K], jnp.concatenate([odd, odd_right], axis=1))
        top[...] = jnp.where(last, 0.0, blocks_ref[jnp.minimum(c + 2, 7)]) - taken[:, : 2 * K]
        top_right[...] = unit(c + 2) - taken[:, 2 * K :]
        start = pl.multiple_of(128 * q, 128)
        inverse[pl.ds(start, K), :] = even_right
        inverse[pl.ds(start + K, K), :] = odd_right
        both = jnp.concatenate([even_turned, odd_turned], axis=1)
        cols = pl.ds(start, 128)
        factor_ref[pl.ds(start, K), cols] = jnp.where(wide_lane < K, both[:K], 0.0)
        factor_ref[pl.ds(start + K, K), cols] = both[K:]

        @pl.when(q < 3)
        def _():
            factor_ref[pl.ds(start + 128, K), cols] = jnp.where(wide_lane < K, 0.0, both[:K])


def first_half(blocks_ref, factor_ref, inverse, top, top_right, cross):
    factor_ref[...] = jnp.zeros((5 * K, 4 * K), f32)
    half_factor(0, lax.axis_index("coarse"), blocks_ref, factor_ref, cross, top, top_right, inverse)


def second_half(blocks_ref, part_ref, first_inverse, first_top, first_right, factor_ref, inverse, cross, top, top_right):
    factor_ref[: 5 * K, : 4 * K] = part_ref[...]
    factor_ref[5 * K :, : 4 * K] = jnp.zeros((3 * K, 4 * K), f32)
    factor_ref[:, 4 * K :] = jnp.zeros((8 * K, 4 * K), f32)
    inverse[: 4 * K, :] = first_inverse[...]
    top[...] = first_top[...]
    top_right[...] = first_right[...]
    half_factor(1, lax.axis_index("coarse"), blocks_ref, factor_ref, cross, top, top_right, inverse)


HBM = pl.BlockSpec(memory_space=pltpu.HBM)


def call(kernel, name, outs, operands, hbm=0, flops=10**8, scratch=(), limit=16):
    return pl.pallas_call(
        kernel,
        out_shape=outs,
        in_specs=[HBM] * hbm + [VMEM] * (len(operands) - hbm),
        out_specs=jax.tree.map(lambda _: VMEM, outs),
        scratch_shapes=scratch,
        compiler_params=pltpu.CompilerParams(vmem_limit_bytes=limit * 2**20),
        cost_estimate=pl.CostEstimate(flops=flops, bytes_accessed=2 * 10**6, transcendentals=1000),
        name=name,
    )(*operands)


def array(*shape, dtype=f32):
    return jax.ShapeDtypeStruct(shape, dtype)


FIRST = (array(5 * K, 4 * K), array(4 * K, 2 * K), array(K, 2 * K), array(K, 2 * K))


def passed_along(block, axis, distance):
    count = lax.axis_size(axis)
    return lax.ppermute(block, axis, [(i, (i + distance) % count) for i in range(count)])


def body(deflation, conductivity, storage, interface_rows, interface_counts):
    vectors = deflation[0].reshape(K * CZ, FACE)
    sigma = conductivity[0]
    counts = interface_counts.reshape(2 * REACH)
    strips, ahead, behind, own_tails, top, bottom, live, wanted = call(
        face_kernel,
        "face",
        (
            array(4, K * CZ, 128),
            array(K, FACE),
            array(K, FACE),
            array(16, FACE),
            array(ROWS, FACE),
            array(ROWS, FACE),
            array(8, FACE),
            array(8, FACE, dtype=jnp.int32),
        ),
        tuple(
            pltpu.with_memory_space_constraint(x, pltpu.HBM)
            for x in (vectors, sigma, interface_rows[0, 0], counts)
        ),
        hbm=4,
        scratch=(
            pltpu.VMEM((CZ, FACE), f32),
            pltpu.VMEM((2 * REACH, FACE), jnp.int32),
            pltpu.SMEM((2 * REACH,), jnp.int32),
            pltpu.VMEM((4, FACE, 256), bf16),
            pltpu.SemaphoreType.DMA((7,)),
        ),
    )
    count = lax.axis_size("sub")
    swap = [(i, i ^ 1) for i in range(count)]
    below = passed_along(top, "coarse", 1)
    above = passed_along(bottom, "coarse", -1)
    other_tails = lax.ppermute(own_tails, "sub", swap)
    own = call(own_kernel, "own", array(K, K), (strips, sigma, storage[0]))
    (other_tails, below, above), own = lax.optimization_barrier(((other_tails, below, above), own))
    go_ahead, go_behind = call(
        pair_kernel, "pair", (array(16, FACE), array(16, FACE)), (own_tails, other_tails), flops=10**6
    )
    far = [(i, (i + 2 + 2 * (i % 2)) % count) for i in range(count)]
    before = lax.ppermute(go_ahead, "sub", far)
    after = lax.ppermute(go_behind, "sub", [(j, i) for i, j in far])
    mine, square, lower = call(
        row_kernel,
        "rows",
        (array(8, 2 * K, FACE, dtype=bf16), array(K, K), array(K, K)),
        (ahead, behind, wanted, top, bottom, below, above),
    )
    (before, after), mine = lax.optimization_barrier(((before, after), mine))
    both = call(join_kernel, "join", array(32, FACE), (before, after), flops=10**6)
    swapped_tails = lax.ppermute(both, "sub", swap)
    payload, weight, index = call(
        block_kernel,
        "block",
        (array(8, K, 2 * K), array(8, FACE), array(8, FACE, dtype=jnp.int32)),
        (live, own, square, lower, mine, own_tails, other_tails, before, after, swapped_tails),
    )
    (ahead, behind), payload = lax.optimization_barrier(((ahead, behind), payload))
    blocks = lax.all_to_all(payload, "coarse", 0, 0)
    faces = (
        passed_along(ahead, "sub", 2),
        passed_along(behind, "sub", -2),
        passed_along(ahead, "sub", 4),
        passed_along(behind, "sub", -4),
    )
    state = call(
        first_half,
        "factor_first",
        FIRST,
        (blocks,),
        flops=10**9,
        scratch=(pltpu.VMEM((8, K, 2 * K), f32),),
    )
    faces, state = lax.optimization_barrier((faces, state))
    packed = call(pack_kernel, "faces", array(4 * K, FACE), (ahead, behind, *faces), flops=10**6)
    faces = (*faces, lax.ppermute(packed, "sub", swap))
    factor, inverse = call(
        second_half,
        "factor_second",
        (array(8 * K, 8 * K), array(8 * K, 2 * K)),
        (blocks, *state),
        flops=10**9,
        scratch=(pltpu.VMEM((8, K, 2 * K), f32), pltpu.VMEM((K, 2 * K), f32), pltpu.VMEM((K, 2 * K), f32)),
    )
    panel = call(
        panel_kernel,
        "panel",
        array(8 * K, 8 * K),
        (weight, index, mine, *faces, inverse),
    )
    return (factor[None], panel[None, None])


def solution(mesh):
    placed = (
        P("sub", None, "coarse", None),
        P("sub", "coarse", None),
        P("sub", "coarse", None),
        P("sub", "coarse", None, None),
        P("sub", "coarse", None),
    )
    return jax.shard_map(
        body,
        mesh=mesh,
        in_specs=placed,
        out_specs=(P("sub", None, None), P("sub", "coarse", None, None)),
        check_vma=False,
    )
```

```python
import functools

import jax
import jax.numpy as jnp
from jax import lax
from jax.experimental import pallas as pl
from jax.experimental.pallas import tpu as pltpu
from jax.sharding import PartitionSpec as P

K = 64
CX = 16
CY = 32
CZ = 16
FACE = 512
REACH = 4
ROWS = K + 8

f32 = jnp.float32
bf16 = jnp.bfloat16
VMEM = pl.BlockSpec(memory_space=pltpu.VMEM)
MATRIX = (((1,), (0,)), ((), ()))
GRAM = (((1,), (1,)), ((), ()))


def product(left, right, dims):
    return lax.dot_general(left, right, dims, preferred_element_type=f32)


def harmonic(first, second):
    return 2.0 * first * second / (first + second)


def halves(x):
    high = x.astype(bf16)
    return high, (x - high.astype(f32)).astype(bf16)


def stacked(x):
    return jnp.concatenate(halves(x), axis=0)


def quadrants(square):
    half = square[:K] + square[K:]
    return half[:, :K] + half[:, K:]


def gathered(table, index):
    strips = []
    for q in range(4):
        wanted = jnp.broadcast_to(index[:, 128 * q : 128 * (q + 1)], (8, 128))
        found = None
        for strip in range(4):
            part = jnp.take_along_axis(
                table[:, 128 * strip : 128 * (strip + 1)],
                wanted & 127,
                axis=1,
                mode="promise_in_bounds",
            )
            found = part if strip == 0 else jnp.where(wanted >> 7 == strip, part, found)
        strips.append(found)
    return jnp.concatenate(strips, axis=1)


def one_hot(index):
    place = lax.broadcasted_iota(jnp.int32, (FACE, FACE), 0)
    return jnp.where(place == index, 1.0, 0.0).astype(bf16)


def layer_of(strips, z):
    return jnp.concatenate([strips[q, pl.ds(z, K, stride=CZ), :] for q in range(4)], axis=1)


def face_kernel(vectors_hbm, sigma_hbm, index_hbm, counts_hbm, strips, ahead_ref, behind_ref, tails_ref, top_ref, bottom_ref, live_ref, wanted_ref, sigma_ref, index_ref, counts_ref, choice_ref, sems):
    small = [
        pltpu.make_async_copy(sigma_hbm, sigma_ref, sems.at[4]),
        pltpu.make_async_copy(index_hbm, index_ref, sems.at[5]),
        pltpu.make_async_copy(counts_hbm, counts_ref, sems.at[6]),
    ]
    large = [
        pltpu.make_async_copy(vectors_hbm.at[:, pl.ds(128 * q, 128)], strips.at[q], sems.at[q])
        for q in range(4)
    ]
    for copy in small + large:
        copy.start()
    lane = lax.broadcasted_iota(jnp.int32, (1, 256), 1)
    within = lane % 128
    cell_of_lane = (within % CY) * CX + jnp.where(lane >= 128, CX - 1, 0)
    cell = lax.broadcasted_iota(jnp.int32, (FACE, 256), 0)
    for step in range(4):
        chosen = jnp.where(within // CY == step, cell_of_lane, -1)
        choice_ref[step] = jnp.where(cell == chosen, 1.0, 0.0).astype(bf16)
    for copy in small:
        copy.wait()

    def faces_of(rows_of_layer, count):
        total = jnp.zeros((4 * count, 256), f32)
        for step in range(4):
            groups = [rows_of_layer(4 * group + step) for group in range(4)]
            total = total + product(jnp.concatenate(groups, axis=0), choice_ref[step], MATRIX)
        return [
            jnp.concatenate(
                [
                    total[count * group : count * (group + 1), 128 * side : 128 * (side + 1)]
                    for group in range(4)
                ],
                axis=1,
            )
            for side in range(2)
        ]

    def sigma_rows(z):
        high, low = halves(jnp.broadcast_to(sigma_ref[z : z + 1, :], (8, FACE)))
        return jnp.concatenate([high.astype(f32), low.astype(f32)], axis=0).astype(bf16)

    along = lax.broadcasted_iota(jnp.int32, (1, FACE), 1)
    sigma_faces = faces_of(sigma_rows, 16)
    for slot in range(2 * REACH):
        side = slot // REACH
        live_ref[slot : slot + 1] = jnp.where(along < counts_ref[slot], 1.0, 0.0)
        cell_index = index_ref[slot : slot + 1, :]
        wanted = (cell_index >> 9) * CY + ((cell_index >> 4) & (CY - 1))
        wanted_ref[slot : slot + 1] = wanted
        found = gathered(sigma_faces[side][:8] + sigma_faces[side][8:], wanted)
        row = slot - REACH if side else 8 + REACH - 1 - slot
        tails_ref[row : row + 1] = found[:1]
        tails_ref[4 + row : 5 + row] = wanted.astype(f32)
    for copy in large:
        copy.wait()
    for out_ref, z in ((bottom_ref, 0), (top_ref, CZ - 1)):
        out_ref[:K] = layer_of(strips, z)
        out_ref[K:] = jnp.broadcast_to(sigma_ref[z : z + 1, :], (8, FACE))
    faces = faces_of(lambda z: stacked(layer_of(strips, z)), 2 * K)
    for side, face_ref in ((0, behind_ref), (1, ahead_ref)):
        face_ref[...] = faces[side][:K] + faces[side][K:]


def row_kernel(ahead_ref, behind_ref, wanted_ref, top_ref, bottom_ref, below_ref, above_ref, own_ref, exact_ref, square_ref, lower_ref):
    for side, face_ref in ((0, behind_ref), (1, ahead_ref)):
        table = stacked(face_ref[...])
        for slot in range(REACH * side, REACH * (side + 1)):
            select = one_hot(wanted_ref[slot : slot + 1, :])
            found = product(table, select, MATRIX)
            own_ref[slot] = found.astype(bf16)
            exact_ref[slot] = found[:K] + found[K:]
    level = lax.axis_index("coarse")
    downward = harmonic(bottom_ref[K : K + 1, :], below_ref[K : K + 1, :])
    downward = jnp.where(level == 0, 0.0, downward)
    upward = harmonic(top_ref[K : K + 1, :], above_ref[K : K + 1, :])
    upward = jnp.where(level == lax.axis_size("coarse") - 1, 0.0, upward)
    top, bottom = top_ref[:K, :], bottom_ref[:K, :]
    weighted = stacked(bottom * downward)
    square = product(stacked(top * upward), stacked(top), GRAM)
    square_ref[...] = quadrants(square + product(weighted, stacked(bottom), GRAM))
    lower_ref[...] = -quadrants(product(weighted, stacked(below_ref[:K, :]), GRAM))


def own_kernel(strips, sigma_ref, storage_ref, own_ref):
    sigma = sigma_ref[...]
    lane = lax.broadcasted_iota(jnp.int32, (CZ, FACE), 1)
    layer = lax.broadcasted_iota(jnp.int32, (CZ, FACE), 0)
    along_x = jnp.where(
        lane % CX == CX - 1, 0.0, harmonic(sigma, pltpu.roll(sigma, FACE - 1, 1))
    )
    along_y = jnp.where(
        lane >= FACE - CX, 0.0, harmonic(sigma, pltpu.roll(sigma, FACE - CX, 1))
    )
    along_z = jnp.where(layer == CZ - 1, 0.0, harmonic(sigma, pltpu.roll(sigma, CZ - 1, 0)))
    half = 0.5 * (
        storage_ref[...]
        + along_x
        + pltpu.roll(along_x, 1, 1)
        + along_y
        + pltpu.roll(along_y, CX, 1)
        + along_z
        + pltpu.roll(along_z, 1, 0)
    )
    total = jnp.zeros((2 * K, 2 * K), f32)
    below = layer_of(strips, 0)
    for z in range(CZ):
        now = below
        applied = half[z : z + 1] * now
        applied = applied - along_x[z : z + 1] * pltpu.roll(now, FACE - 1, 1)
        applied = applied - along_y[z : z + 1] * pltpu.roll(now, FACE - CX, 1)
        if z < CZ - 1:
            below = layer_of(strips, z + 1)
            applied = applied - along_z[z : z + 1] * below
        total = total + product(stacked(now), stacked(applied), GRAM)
    own = quadrants(total)
    own_ref[...] = own + own.T


def pack_kernel(ahead, behind, ahead2, behind2, ahead4, behind4, out_ref):
    mine = lax.axis_index("sub") % 2
    for core, chosen in ((0, (ahead, ahead2, behind2, behind4)), (1, (ahead2, ahead4, behind, behind2))):
        @pl.when(mine == core)
        def _(chosen=chosen):
            for at, ref in enumerate(chosen):
                out_ref[K * at : K * (at + 1)] = ref[...]


def pair_kernel(own, other, ahead_ref, behind_ref):
    ahead_ref[:8] = own[:8]
    ahead_ref[8:] = other[:8]
    behind_ref[:8] = own[8:]
    behind_ref[8:] = other[8:]


def join_kernel(first, second, out_ref):
    out_ref[:16] = first[...]
    out_ref[16:] = second[...]


OFFSETS = (-4, -3, -2, -1, 1, 2, 3, 4)


def tails_by_slot(other, before, after, swapped):
    even = lax.axis_index("sub") % 2 == 0
    low, high = slice(0, 8), slice(8, 16)
    before1 = jnp.where(even, before[...], swapped[:16])
    before2 = jnp.where(even, swapped[:16], before[...])
    after1 = jnp.where(even, after[...], swapped[16:])
    after2 = jnp.where(even, swapped[16:], after[...])
    on_even = (before2[high], before2[low], before1[low], before1[high], other[high], after1[low], after1[high], after2[high])
    on_odd = (before2[low], before1[low], before1[high], other[low], after1[low], after1[high], after2[high], after2[low])
    return [jnp.where(even, x, y) for x, y in zip(on_even, on_odd, strict=True)]


def partner_face(refs, offset):
    ahead2, behind2, ahead4, behind4, swapped = refs
    if offset % 2:
        at = {-1: 0, -3: 1, 1: 2, 3: 3}[offset]
        return swapped[K * at : K * at + K]
    return {-2: ahead2, -4: ahead4, 2: behind2, 4: behind4}[offset][...]


def block_kernel(live_ref, own_block, square_block, lower_block, own_ref, exact_ref, own_tails, *refs):
    *tails, out_ref, weighted_ref, index_ref = refs
    total = jnp.zeros((2 * K, 2 * K), f32)
    found = tails_by_slot(*tails)
    for slot, offset in enumerate(OFFSETS):
        reach = abs(offset) - 1
        row = reach if offset > 0 else 8 + reach
        pair = harmonic(own_tails[row : row + 1], found[slot][reach : reach + 1])
        weight = jnp.where(live_ref[slot : slot + 1] > 0.0, pair, 0.0)
        index_ref[slot : slot + 1] = found[slot][4 + reach : 5 + reach].astype(jnp.int32)
        weighted = stacked(exact_ref[slot] * weight)
        weighted_ref[slot] = weighted
        total = total + product(weighted, own_ref[slot], GRAM)
    level = lax.axis_index("coarse")
    extra = quadrants(total) + square_block[...]
    own = own_block[...] + 0.5 * (extra + extra.T)
    lower = lower_block[...]
    even = level % 2 == 0
    payload = jnp.where(
        even, jnp.concatenate([own, lower], axis=1), jnp.concatenate([lower, own], axis=1)
    )
    for copy in range(8):
        out_ref[copy] = payload


def panel_kernel(weighted_ref, index_ref, *refs):
    faces, (inverse, out_hbm, rows_ref, sems) = refs[:5], refs[5:]
    blocks = []
    for slot, offset in enumerate(OFFSETS):
        select = one_hot(index_ref[slot : slot + 1, :])
        found = product(stacked(partner_face(faces, offset)), select, MATRIX).astype(bf16)
        blocks.append(-quadrants(product(weighted_ref[slot], found, GRAM)))
    high, low = halves(jnp.concatenate(blocks, axis=1))
    down = jnp.concatenate([high, high, low], axis=0)
    copies = []
    for part in range(4):
        at = slice(128 * part, 128 * (part + 1))
        left_high, left_low = halves(inverse[at, :K])
        left = jnp.concatenate([left_high, left_low, left_high], axis=1)
        rows_ref[part] = product(left, down, MATRIX)
        copies.append(pltpu.make_async_copy(rows_ref.at[part], out_hbm.at[at], sems.at[part]))
        copies[-1].start()
    for copy in copies:
        copy.wait()


def thirds(x):
    high = x.astype(bf16)
    rest = x - high.astype(f32)
    middle = rest.astype(bf16)
    return high, middle, (rest - middle.astype(f32)).astype(bf16)


def fine_product(left, right):
    a, b, c = thirds(left)
    p, q, r = thirds(right)
    first = product(jnp.concatenate([a, b, c], axis=0), p, MATRIX)
    second = product(jnp.concatenate([a, b], axis=0), q, MATRIX)
    small = product(a, r, MATRIX) + first[2 * K :] + second[K:]
    return first[:K] + (first[K : 2 * K] + second[:K] + small)


def lane_of(x, lane):
    index = jnp.full(x.shape, lane, jnp.int32)
    return jnp.take_along_axis(x, index, axis=1, mode="promise_in_bounds")


def sublane_of(x, sublane):
    index = jnp.full(x.shape, sublane, jnp.int32)
    return jnp.take_along_axis(x, index, axis=0, mode="promise_in_bounds")


def eliminate(rows, right, offset, lane, sub):
    wide = (8, 128)
    kept_rows, kept_right_rows = [], []
    for panel in range(8):
        first = offset + 8 * panel
        column = [
            {
                g: lane_of(rows[g], first + k)
                for g in range(panel, 8)
            }
            for k in range(8)
        ]
        pivot = [[None] * 8 for _ in range(8)]
        for i in range(8):
            for k in range(i, 8):
                pivot[i][k] = sublane_of(column[i][panel], k)
        left_row = [sublane_of(rows[panel], k) for k in range(8)]
        right_row = [sublane_of(right[panel], k) for k in range(8)]
        kept = jnp.zeros(wide, f32)
        kept_right = jnp.zeros(wide, f32)
        for i in range(8):
            scale = lax.rsqrt(pivot[i][i])
            inverse = 1.0 / pivot[i][i]
            kept = jnp.where(sub == i, left_row[i] * scale, kept)
            kept_right = jnp.where(sub == i, right_row[i] * scale, kept_right)
            left_row[i] = left_row[i] * inverse
            right_row[i] = right_row[i] * inverse
            scaled = [None] * 8
            for l in range(i + 1, 8):
                scaled[l] = pivot[i][l] * inverse
            for k in range(8):
                if k == i:
                    continue
                by = pivot[i][k] if k > i else pivot[k][i]
                left_row[k] = left_row[k] - by * left_row[i]
                right_row[k] = right_row[k] - by * right_row[i]
                for l in range(max(i + 1, k), 8):
                    pivot[k][l] = pivot[k][l] - by * scaled[l]
            pivot[i] = scaled
        for g in range(panel + 1, 8):
            for k in range(8):
                rows[g] = rows[g] - column[k][g] * left_row[k]
                right[g] = right[g] - column[k][g] * right_row[k]
        live = (lane >= first + sub) if offset else ((lane >= first + sub) | (lane >= K))
        if offset:
            live = live | (lane < K)
        kept_rows.append(jnp.where(live, kept, 0.0))
        kept_right_rows.append(kept_right)
    return jnp.concatenate(kept_rows, axis=0), jnp.concatenate(kept_right_rows, axis=0)


def half_factor(begin, level, blocks_ref, factor_ref, cross, top, top_right, inverse):
    lane = lax.broadcasted_iota(jnp.int32, (8, 128), 1)
    sub = lax.broadcasted_iota(jnp.int32, (8, 128), 0)
    wide_lane = lax.broadcasted_iota(jnp.int32, (K, 2 * K), 1)
    wide_sub = lax.broadcasted_iota(jnp.int32, (K, 2 * K), 0)
    zero = jnp.zeros((K, 2 * K), f32)
    at = [pl.ds(8 * g, 8) for g in range(8)]
    for c in range(4 * begin + 1, min(4 * begin + 5, 8)):
        block = blocks_ref[c]
        if c % 2 == 1:
            cross[c - 1] = jnp.concatenate([zero, block], axis=0).T[:K]
        else:
            cross[c - 1] = jnp.concatenate([block, zero], axis=0).T[K:]
    if begin:
        cross[7] = zero

    def unit(c):
        return jnp.where((wide_lane == wide_sub) & (level == c), 1.0, 0.0)

    if not begin:
        top[...] = blocks_ref[0]
        top_right[...] = unit(0)

    @pl.loop(2 * begin, 2 * begin + 2)
    def _(q):
        c = 2 * q
        last = q == 3
        rows = [jnp.where(lane < K, top[at[g], :], cross[c, at[g], :]) for g in range(8)]
        right = [top_right[at[g], :] for g in range(8)]
        even, even_right = eliminate(rows, right, 0, lane, sub)
        even_turned = even.T
        taken = fine_product(even_turned[K:], jnp.concatenate([even, even_right], axis=1))
        under = blocks_ref[c + 1] - taken[:, : 2 * K]
        under_right = unit(c + 1) - taken[:, 2 * K :]
        rows = [jnp.where(lane < K, cross[c + 1, at[g], :], under[8 * g : 8 * g + 8]) for g in range(8)]
        right = [under_right[8 * g : 8 * g + 8] for g in range(8)]
        odd, odd_right = eliminate(rows, right, K, lane, sub)
        odd_turned = odd.T
        taken = fine_product(odd_turned[:K], jnp.concatenate([odd, odd_right], axis=1))
        top[...] = jnp.where(last, 0.0, blocks_ref[jnp.minimum(c + 2, 7)]) - taken[:, : 2 * K]
        top_right[...] = unit(c + 2) - taken[:, 2 * K :]
        start = pl.multiple_of(128 * q, 128)
        inverse[pl.ds(start, K), :] = even_right
        inverse[pl.ds(start + K, K), :] = odd_right
        both = jnp.concatenate([even_turned, odd_turned], axis=1)
        within = pl.multiple_of(start - 4 * K * begin, 128)
        cols = pl.ds(within, 128)
        factor_ref[pl.ds(within, K), cols] = jnp.where(wide_lane < K, both[:K], 0.0)
        factor_ref[pl.ds(within + K, K), cols] = both[K:]

        @pl.when(q < 3)
        def _():
            factor_ref[pl.ds(within + 128, K), cols] = jnp.where(wide_lane < K, 0.0, both[:K])


def first_half(blocks_ref, factor_ref, inverse, top, top_right, cross):
    factor_ref[...] = jnp.zeros((5 * K, 4 * K), f32)
    half_factor(0, lax.axis_index("coarse"), blocks_ref, factor_ref, cross, top, top_right, inverse)


def second_half(blocks_ref, part_ref, first_inverse, first_top, first_right, factor_hbm, inverse, cross, top, top_right, corner, blank, sems):
    blank[...] = jnp.zeros((4 * K, 4 * K), f32)
    copies = [
        pltpu.make_async_copy(part_ref, factor_hbm.at[: 5 * K, : 4 * K], sems.at[0]),
        pltpu.make_async_copy(blank, factor_hbm.at[: 4 * K, 4 * K :], sems.at[1]),
        pltpu.make_async_copy(blank.at[: 3 * K], factor_hbm.at[5 * K :, : 4 * K], sems.at[2]),
    ]
    for copy in copies:
        copy.start()
    corner[...] = jnp.zeros((4 * K, 4 * K), f32)
    inverse[: 4 * K, :] = first_inverse[...]
    top[...] = first_top[...]
    top_right[...] = first_right[...]
    half_factor(1, lax.axis_index("coarse"), blocks_ref, corner, cross, top, top_right, inverse)
    copies.append(pltpu.make_async_copy(corner, factor_hbm.at[4 * K :, 4 * K :], sems.at[3]))
    copies[-1].start()
    for copy in copies:
        copy.wait()


HBM = pl.BlockSpec(memory_space=pltpu.HBM)


def call(kernel, name, outs, operands, hbm=0, out=None, flops=10**8, scratch=(), limit=16):
    return pl.pallas_call(
        kernel,
        out_shape=outs,
        in_specs=[HBM] * hbm + [VMEM] * (len(operands) - hbm),
        out_specs=jax.tree.map(lambda _: VMEM, outs) if out is None else out,
        scratch_shapes=scratch,
        compiler_params=pltpu.CompilerParams(vmem_limit_bytes=limit * 2**20),
        cost_estimate=pl.CostEstimate(flops=flops, bytes_accessed=2 * 10**6, transcendentals=1000),
        name=name,
    )(*operands)


def array(*shape, dtype=f32):
    return jax.ShapeDtypeStruct(shape, dtype)


FIRST = (array(5 * K, 4 * K), array(4 * K, 2 * K), array(K, 2 * K), array(K, 2 * K))


def passed_along(block, axis, distance):
    count = lax.axis_size(axis)
    return lax.ppermute(block, axis, [(i, (i + distance) % count) for i in range(count)])


def body(deflation, conductivity, storage, interface_rows, interface_counts):
    vectors = deflation[0].reshape(K * CZ, FACE)
    sigma = conductivity[0]
    counts = interface_counts.reshape(2 * REACH)
    strips, ahead, behind, own_tails, top, bottom, live, wanted = call(
        face_kernel,
        "face",
        (
            array(4, K * CZ, 128),
            array(K, FACE),
            array(K, FACE),
            array(16, FACE),
            array(ROWS, FACE),
            array(ROWS, FACE),
            array(8, FACE),
            array(8, FACE, dtype=jnp.int32),
        ),
        tuple(
            pltpu.with_memory_space_constraint(x, pltpu.HBM)
            for x in (vectors, sigma, interface_rows[0, 0], counts)
        ),
        hbm=4,
        scratch=(
            pltpu.VMEM((CZ, FACE), f32),
            pltpu.VMEM((2 * REACH, FACE), jnp.int32),
            pltpu.SMEM((2 * REACH,), jnp.int32),
            pltpu.VMEM((4, FACE, 256), bf16),
            pltpu.SemaphoreType.DMA((7,)),
        ),
    )
    count = lax.axis_size("sub")
    swap = [(i, i ^ 1) for i in range(count)]
    below = passed_along(top, "coarse", 1)
    above = passed_along(bottom, "coarse", -1)
    other_tails = lax.ppermute(own_tails, "sub", swap)
    own = call(own_kernel, "own", array(K, K), (strips, sigma, storage[0]))
    other_tails, own = lax.optimization_barrier((other_tails, own))
    go_ahead, go_behind = call(
        pair_kernel, "pair", (array(16, FACE), array(16, FACE)), (own_tails, other_tails), flops=10**6
    )
    far = [(i, (i + 2 + 2 * (i % 2)) % count) for i in range(count)]
    before = lax.ppermute(go_ahead, "sub", far)
    after = lax.ppermute(go_behind, "sub", [(j, i) for i, j in far])
    mine, exact, square, lower = call(
        row_kernel,
        "rows",
        (array(8, 2 * K, FACE, dtype=bf16), array(8, K, FACE), array(K, K), array(K, K)),
        (ahead, behind, wanted, top, bottom, below, above),
    )
    (before, after), mine = lax.optimization_barrier(((before, after), mine))
    both = call(join_kernel, "join", array(32, FACE), (before, after), flops=10**6)
    swapped_tails = lax.ppermute(both, "sub", swap)
    payload, weighted, index = call(
        block_kernel,
        "block",
        (
            array(8, K, 2 * K),
            array(8, 2 * K, FACE, dtype=bf16),
            array(8, FACE, dtype=jnp.int32),
        ),
        (live, own, square, lower, mine, exact, own_tails, other_tails, before, after, swapped_tails),
    )
    (ahead, behind), payload = lax.optimization_barrier(((ahead, behind), payload))
    blocks = lax.all_to_all(payload, "coarse", 0, 0)
    faces = (
        passed_along(ahead, "sub", 2),
        passed_along(behind, "sub", -2),
        passed_along(ahead, "sub", 4),
        passed_along(behind, "sub", -4),
    )
    state = call(
        first_half,
        "factor_first",
        FIRST,
        (blocks,),
        flops=10**9,
        scratch=(pltpu.VMEM((8, K, 2 * K), f32),),
    )
    faces, state = lax.optimization_barrier((faces, state))
    packed = call(pack_kernel, "faces", array(4 * K, FACE), (ahead, behind, *faces), flops=10**6)
    faces = (*faces, lax.ppermute(packed, "sub", swap))
    factor, inverse = call(
        second_half,
        "factor_second",
        (array(8 * K, 8 * K), array(8 * K, 2 * K)),
        (blocks, *state),
        flops=10**9,
        out=(HBM, VMEM),
        scratch=(
            pltpu.VMEM((8, K, 2 * K), f32),
            pltpu.VMEM((K, 2 * K), f32),
            pltpu.VMEM((K, 2 * K), f32),
            pltpu.VMEM((4 * K, 4 * K), f32),
            pltpu.VMEM((4 * K, 4 * K), f32),
            pltpu.SemaphoreType.DMA((4,)),
        ),
    )
    panel = call(
        panel_kernel,
        "panel",
        array(8 * K, 8 * K),
        (weighted, index, *faces, inverse),
        out=HBM,
        scratch=(pltpu.VMEM((4, 2 * K, 8 * K), f32), pltpu.SemaphoreType.DMA((4,))),
    )
    return (factor[None], panel[None, None])


def solution(mesh):
    placed = (
        P("sub", None, "coarse", None),
        P("sub", "coarse", None),
        P("sub", "coarse", None),
        P("sub", "coarse", None, None),
        P("sub", "coarse", None),
    )
    return jax.shard_map(
        body,
        mesh=mesh,
        in_specs=placed,
        out_specs=(P("sub", None, None), P("sub", "coarse", None, None)),
        check_vma=False,
    )
```

```python
import functools

import jax
import jax.numpy as jnp
from jax import lax
from jax.experimental import pallas as pl
from jax.experimental.pallas import tpu as pltpu
from jax.sharding import PartitionSpec as P

K = 64
CX = 16
CY = 32
CZ = 16
FACE = 512
REACH = 4
ROWS = K + 8

f32 = jnp.float32
bf16 = jnp.bfloat16
VMEM = pl.BlockSpec(memory_space=pltpu.VMEM)
MATRIX = (((1,), (0,)), ((), ()))
GRAM = (((1,), (1,)), ((), ()))


def product(left, right, dims):
    return lax.dot_general(left, right, dims, preferred_element_type=f32)


def harmonic(first, second):
    return 2.0 * first * second / (first + second)


def halves(x):
    high = x.astype(bf16)
    return high, (x - high.astype(f32)).astype(bf16)


def stacked(x):
    return jnp.concatenate(halves(x), axis=0)


def quadrants(square):
    half = square[:K] + square[K:]
    return half[:, :K] + half[:, K:]


def gathered(table, index):
    strips = []
    for q in range(4):
        wanted = jnp.broadcast_to(index[:, 128 * q : 128 * (q + 1)], (8, 128))
        found = None
        for strip in range(4):
            part = jnp.take_along_axis(
                table[:, 128 * strip : 128 * (strip + 1)],
                wanted & 127,
                axis=1,
                mode="promise_in_bounds",
            )
            found = part if strip == 0 else jnp.where(wanted >> 7 == strip, part, found)
        strips.append(found)
    return jnp.concatenate(strips, axis=1)


def one_hot(index):
    place = lax.broadcasted_iota(jnp.int32, (FACE, FACE), 0)
    return jnp.where(place == index, 1.0, 0.0).astype(bf16)


def layer_of(strips, z):
    return jnp.concatenate([strips[q, pl.ds(z, K, stride=CZ), :] for q in range(4)], axis=1)


def face_kernel(vectors_hbm, sigma_hbm, index_hbm, counts_hbm, layers_ref, parts_ref, ahead_ref, behind_ref, tails_ref, top_ref, bottom_ref, live_ref, wanted_ref, sigma_ref, index_ref, counts_ref, choice_ref, strips, sems):
    small = [
        pltpu.make_async_copy(sigma_hbm, sigma_ref, sems.at[4]),
        pltpu.make_async_copy(index_hbm, index_ref, sems.at[5]),
        pltpu.make_async_copy(counts_hbm, counts_ref, sems.at[6]),
    ]
    large = [
        pltpu.make_async_copy(vectors_hbm.at[:, pl.ds(128 * q, 128)], strips.at[q], sems.at[q])
        for q in range(4)
    ]
    for copy in small + large:
        copy.start()
    lane = lax.broadcasted_iota(jnp.int32, (1, 256), 1)
    within = lane % 128
    cell_of_lane = (within % CY) * CX + jnp.where(lane >= 128, CX - 1, 0)
    cell = lax.broadcasted_iota(jnp.int32, (FACE, 256), 0)
    for step in range(4):
        chosen = jnp.where(within // CY == step, cell_of_lane, -1)
        choice_ref[step] = jnp.where(cell == chosen, 1.0, 0.0).astype(bf16)
    for copy in small:
        copy.wait()

    def faces_of(rows_of_layer, count):
        total = jnp.zeros((4 * count, 256), f32)
        for step in range(4):
            groups = [rows_of_layer(4 * group + step) for group in range(4)]
            total = total + product(jnp.concatenate(groups, axis=0), choice_ref[step], MATRIX)
        return [
            jnp.concatenate(
                [
                    total[count * group : count * (group + 1), 128 * side : 128 * (side + 1)]
                    for group in range(4)
                ],
                axis=1,
            )
            for side in range(2)
        ]

    def sigma_rows(z):
        high, low = halves(jnp.broadcast_to(sigma_ref[z : z + 1, :], (8, FACE)))
        return jnp.concatenate([high.astype(f32), low.astype(f32)], axis=0).astype(bf16)

    along = lax.broadcasted_iota(jnp.int32, (1, FACE), 1)
    sigma_faces = faces_of(sigma_rows, 16)
    for slot in range(2 * REACH):
        side = slot // REACH
        live_ref[slot : slot + 1] = jnp.where(along < counts_ref[slot], 1.0, 0.0)
        cell_index = index_ref[slot : slot + 1, :]
        wanted = (cell_index >> 9) * CY + ((cell_index >> 4) & (CY - 1))
        wanted_ref[slot : slot + 1] = wanted
        found = gathered(sigma_faces[side][:8] + sigma_faces[side][8:], wanted)
        row = slot - REACH if side else 8 + REACH - 1 - slot
        tails_ref[row : row + 1] = found[:1]
        tails_ref[4 + row : 5 + row] = wanted.astype(f32)
    for copy in large:
        copy.wait()

    def vector_rows(z):
        layer = layer_of(strips, z)
        layers_ref[z] = layer
        parts = stacked(layer)
        parts_ref[z] = parts
        for out_ref, at in ((bottom_ref, 0), (top_ref, CZ - 1)):
            if z == at:
                out_ref[:K] = layer
                out_ref[K:] = jnp.broadcast_to(sigma_ref[z : z + 1, :], (8, FACE))
        return parts

    faces = faces_of(vector_rows, 2 * K)
    for side, face_ref in ((0, behind_ref), (1, ahead_ref)):
        face_ref[...] = faces[side][:K] + faces[side][K:]


def row_kernel(ahead_ref, behind_ref, wanted_ref, top_ref, bottom_ref, below_ref, above_ref, own_ref, exact_ref, square_ref, lower_ref):
    for side, face_ref in ((0, behind_ref), (1, ahead_ref)):
        table = stacked(face_ref[...])
        for slot in range(REACH * side, REACH * (side + 1)):
            select = one_hot(wanted_ref[slot : slot + 1, :])
            found = product(table, select, MATRIX)
            own_ref[slot] = found.astype(bf16)
            exact_ref[slot] = found[:K] + found[K:]
    level = lax.axis_index("coarse")
    downward = harmonic(bottom_ref[K : K + 1, :], below_ref[K : K + 1, :])
    downward = jnp.where(level == 0, 0.0, downward)
    upward = harmonic(top_ref[K : K + 1, :], above_ref[K : K + 1, :])
    upward = jnp.where(level == lax.axis_size("coarse") - 1, 0.0, upward)
    top, bottom = top_ref[:K, :], bottom_ref[:K, :]
    weighted = stacked(bottom * downward)
    square = product(stacked(top * upward), stacked(top), GRAM)
    square_ref[...] = quadrants(square + product(weighted, stacked(bottom), GRAM))
    lower_ref[...] = -quadrants(product(weighted, stacked(below_ref[:K, :]), GRAM))


def own_kernel(layers_ref, parts_ref, sigma_ref, storage_ref, own_ref):
    sigma = sigma_ref[...]
    lane = lax.broadcasted_iota(jnp.int32, (CZ, FACE), 1)
    layer = lax.broadcasted_iota(jnp.int32, (CZ, FACE), 0)
    along_x = jnp.where(
        lane % CX == CX - 1, 0.0, harmonic(sigma, pltpu.roll(sigma, FACE - 1, 1))
    )
    along_y = jnp.where(
        lane >= FACE - CX, 0.0, harmonic(sigma, pltpu.roll(sigma, FACE - CX, 1))
    )
    along_z = jnp.where(layer == CZ - 1, 0.0, harmonic(sigma, pltpu.roll(sigma, CZ - 1, 0)))
    half = 0.5 * (
        storage_ref[...]
        + along_x
        + pltpu.roll(along_x, 1, 1)
        + along_y
        + pltpu.roll(along_y, CX, 1)
        + along_z
        + pltpu.roll(along_z, 1, 0)
    )
    total = jnp.zeros((2 * K, 2 * K), f32)
    below = layers_ref[0]
    for z in range(CZ):
        now = below
        applied = half[z : z + 1] * now
        applied = applied - along_x[z : z + 1] * pltpu.roll(now, FACE - 1, 1)
        applied = applied - along_y[z : z + 1] * pltpu.roll(now, FACE - CX, 1)
        if z < CZ - 1:
            below = layers_ref[z + 1]
            applied = applied - along_z[z : z + 1] * below
        total = total + product(parts_ref[z], stacked(applied), GRAM)
    own = quadrants(total)
    own_ref[...] = own + own.T


def pack_kernel(ahead, behind, ahead2, behind2, ahead4, behind4, out_ref):
    mine = lax.axis_index("sub") % 2
    for core, chosen in ((0, (ahead, ahead2, behind2, behind4)), (1, (ahead2, ahead4, behind, behind2))):
        @pl.when(mine == core)
        def _(chosen=chosen):
            for at, ref in enumerate(chosen):
                out_ref[K * at : K * (at + 1)] = ref[...]


def pair_kernel(own, other, ahead_ref, behind_ref):
    ahead_ref[:8] = own[:8]
    ahead_ref[8:] = other[:8]
    behind_ref[:8] = own[8:]
    behind_ref[8:] = other[8:]


def join_kernel(first, second, out_ref):
    out_ref[:16] = first[...]
    out_ref[16:] = second[...]


OFFSETS = (-4, -3, -2, -1, 1, 2, 3, 4)


def tails_by_slot(other, before, after, swapped):
    even = lax.axis_index("sub") % 2 == 0
    low, high = slice(0, 8), slice(8, 16)
    before1 = jnp.where(even, before[...], swapped[:16])
    before2 = jnp.where(even, swapped[:16], before[...])
    after1 = jnp.where(even, after[...], swapped[16:])
    after2 = jnp.where(even, swapped[16:], after[...])
    on_even = (before2[high], before2[low], before1[low], before1[high], other[high], after1[low], after1[high], after2[high])
    on_odd = (before2[low], before1[low], before1[high], other[low], after1[low], after1[high], after2[high], after2[low])
    return [jnp.where(even, x, y) for x, y in zip(on_even, on_odd, strict=True)]


def partner_face(refs, offset):
    ahead2, behind2, ahead4, behind4, swapped = refs
    if offset % 2:
        at = {-1: 0, -3: 1, 1: 2, 3: 3}[offset]
        return swapped[K * at : K * at + K]
    return {-2: ahead2, -4: ahead4, 2: behind2, 4: behind4}[offset][...]


def block_kernel(live_ref, own_block, square_block, lower_block, own_ref, exact_ref, own_tails, *refs):
    *tails, out_ref, weighted_ref, index_ref = refs
    total = jnp.zeros((2 * K, 2 * K), f32)
    found = tails_by_slot(*tails)
    for slot, offset in enumerate(OFFSETS):
        reach = abs(offset) - 1
        row = reach if offset > 0 else 8 + reach
        pair = harmonic(own_tails[row : row + 1], found[slot][reach : reach + 1])
        weight = jnp.where(live_ref[slot : slot + 1] > 0.0, pair, 0.0)
        index_ref[slot : slot + 1] = found[slot][4 + reach : 5 + reach].astype(jnp.int32)
        weighted_ref[slot] = stacked(exact_ref[slot] * weight)
    for slot in range(2 * REACH):
        total = total + product(weighted_ref[slot], own_ref[slot], GRAM)
    level = lax.axis_index("coarse")
    extra = quadrants(total) + square_block[...]
    own = own_block[...] + 0.5 * (extra + extra.T)
    lower = lower_block[...]
    even = level % 2 == 0
    payload = jnp.where(
        even, jnp.concatenate([own, lower], axis=1), jnp.concatenate([lower, own], axis=1)
    )
    for copy in range(8):
        out_ref[copy] = payload


def panel_kernel(weighted_ref, index_ref, *refs):
    faces, (inverse, out_hbm, found_ref, rows_ref, sems) = refs[:5], refs[5:]
    for slot, offset in enumerate(OFFSETS):
        select = one_hot(index_ref[slot : slot + 1, :])
        found_ref[slot] = product(stacked(partner_face(faces, offset)), select, MATRIX).astype(bf16)
    blocks = [
        -quadrants(product(weighted_ref[slot], found_ref[slot], GRAM)) for slot in range(2 * REACH)
    ]
    high, low = halves(jnp.concatenate(blocks, axis=1))
    down = jnp.concatenate([high, high, low], axis=0)
    copies = []
    for part in range(4):
        at = slice(128 * part, 128 * (part + 1))
        left_high, left_low = halves(inverse[at, :K])
        left = jnp.concatenate([left_high, left_low, left_high], axis=1)
        rows_ref[part] = product(left, down, MATRIX)
        copies.append(pltpu.make_async_copy(rows_ref.at[part], out_hbm.at[at], sems.at[part]))
        copies[-1].start()
    for copy in copies:
        copy.wait()


def thirds(x):
    high = x.astype(bf16)
    rest = x - high.astype(f32)
    middle = rest.astype(bf16)
    return high, middle, (rest - middle.astype(f32)).astype(bf16)


def fine_product(left, right):
    a, b, c = thirds(left)
    p, q, r = thirds(right)
    first = product(jnp.concatenate([a, b, c], axis=0), p, MATRIX)
    second = product(jnp.concatenate([a, b], axis=0), q, MATRIX)
    small = product(a, r, MATRIX) + first[2 * K :] + second[K:]
    return first[:K] + (first[K : 2 * K] + second[:K] + small)


def lane_of(x, lane):
    index = jnp.full(x.shape, lane, jnp.int32)
    return jnp.take_along_axis(x, index, axis=1, mode="promise_in_bounds")


def sublane_of(x, sublane):
    index = jnp.full(x.shape, sublane, jnp.int32)
    return jnp.take_along_axis(x, index, axis=0, mode="promise_in_bounds")


def eliminate(rows, right, offset, lane, sub):
    wide = (8, 128)
    kept_rows, kept_right_rows = [], []
    for panel in range(8):
        first = offset + 8 * panel
        column = [
            {
                g: lane_of(rows[g], first + k)
                for g in range(panel, 8)
            }
            for k in range(8)
        ]
        pivot = [[None] * 8 for _ in range(8)]
        for i in range(8):
            for k in range(i, 8):
                pivot[i][k] = sublane_of(column[i][panel], k)
        left_row = [sublane_of(rows[panel], k) for k in range(8)]
        right_row = [sublane_of(right[panel], k) for k in range(8)]
        kept = jnp.zeros(wide, f32)
        kept_right = jnp.zeros(wide, f32)
        for i in range(8):
            scale = lax.rsqrt(pivot[i][i])
            inverse = 1.0 / pivot[i][i]
            kept = jnp.where(sub == i, left_row[i] * scale, kept)
            kept_right = jnp.where(sub == i, right_row[i] * scale, kept_right)
            left_row[i] = left_row[i] * inverse
            right_row[i] = right_row[i] * inverse
            scaled = [None] * 8
            for l in range(i + 1, 8):
                scaled[l] = pivot[i][l] * inverse
            for k in range(8):
                if k == i:
                    continue
                by = pivot[i][k] if k > i else pivot[k][i]
                left_row[k] = left_row[k] - by * left_row[i]
                right_row[k] = right_row[k] - by * right_row[i]
                for l in range(max(i + 1, k), 8):
                    pivot[k][l] = pivot[k][l] - by * scaled[l]
            pivot[i] = scaled
        for g in range(panel + 1, 8):
            for k in range(8):
                rows[g] = rows[g] - column[k][g] * left_row[k]
                right[g] = right[g] - column[k][g] * right_row[k]
        live = (lane >= first + sub) if offset else ((lane >= first + sub) | (lane >= K))
        if offset:
            live = live | (lane < K)
        kept_rows.append(jnp.where(live, kept, 0.0))
        kept_right_rows.append(kept_right)
    return jnp.concatenate(kept_rows, axis=0), jnp.concatenate(kept_right_rows, axis=0)


def half_factor(begin, level, blocks_ref, factor_ref, cross, top, top_right, inverse):
    lane = lax.broadcasted_iota(jnp.int32, (8, 128), 1)
    sub = lax.broadcasted_iota(jnp.int32, (8, 128), 0)
    wide_lane = lax.broadcasted_iota(jnp.int32, (K, 2 * K), 1)
    wide_sub = lax.broadcasted_iota(jnp.int32, (K, 2 * K), 0)
    zero = jnp.zeros((K, 2 * K), f32)
    at = [pl.ds(8 * g, 8) for g in range(8)]
    for c in range(4 * begin + 1, min(4 * begin + 5, 8)):
        block = blocks_ref[c]
        if c % 2 == 1:
            cross[c - 1] = jnp.concatenate([zero, block], axis=0).T[:K]
        else:
            cross[c - 1] = jnp.concatenate([block, zero], axis=0).T[K:]
    if begin:
        cross[7] = zero

    def unit(c):
        return jnp.where((wide_lane == wide_sub) & (level == c), 1.0, 0.0)

    if not begin:
        top[...] = blocks_ref[0]
        top_right[...] = unit(0)

    @pl.loop(2 * begin, 2 * begin + 2)
    def _(q):
        c = 2 * q
        last = q == 3
        rows = [jnp.where(lane < K, top[at[g], :], cross[c, at[g], :]) for g in range(8)]
        right = [top_right[at[g], :] for g in range(8)]
        even, even_right = eliminate(rows, right, 0, lane, sub)
        even_turned = even.T
        taken = fine_product(even_turned[K:], jnp.concatenate([even, even_right], axis=1))
        under = blocks_ref[c + 1] - taken[:, : 2 * K]
        under_right = unit(c + 1) - taken[:, 2 * K :]
        rows = [jnp.where(lane < K, cross[c + 1, at[g], :], under[8 * g : 8 * g + 8]) for g in range(8)]
        right = [under_right[8 * g : 8 * g + 8] for g in range(8)]
        odd, odd_right = eliminate(rows, right, K, lane, sub)
        odd_turned = odd.T
        taken = fine_product(odd_turned[:K], jnp.concatenate([odd, odd_right], axis=1))
        top[...] = jnp.where(last, 0.0, blocks_ref[jnp.minimum(c + 2, 7)]) - taken[:, : 2 * K]
        top_right[...] = unit(c + 2) - taken[:, 2 * K :]
        start = pl.multiple_of(128 * q, 128)
        inverse[pl.ds(start, K), :] = even_right
        inverse[pl.ds(start + K, K), :] = odd_right
        both = jnp.concatenate([even_turned, odd_turned], axis=1)
        within = pl.multiple_of(start - 4 * K * begin, 128)
        cols = pl.ds(within, 128)
        factor_ref[pl.ds(within, K), cols] = jnp.where(wide_lane < K, both[:K], 0.0)
        factor_ref[pl.ds(within + K, K), cols] = both[K:]

        @pl.when(q < 3)
        def _():
            factor_ref[pl.ds(within + 128, K), cols] = jnp.where(wide_lane < K, 0.0, both[:K])


def first_half(blocks_ref, factor_ref, inverse, top, top_right, cross):
    factor_ref[...] = jnp.zeros((5 * K, 4 * K), f32)
    half_factor(0, lax.axis_index("coarse"), blocks_ref, factor_ref, cross, top, top_right, inverse)


def second_half(blocks_ref, part_ref, first_inverse, first_top, first_right, factor_hbm, inverse, cross, top, top_right, corner, blank, sems):
    blank[...] = jnp.zeros((4 * K, 4 * K), f32)
    copies = [
        pltpu.make_async_copy(part_ref, factor_hbm.at[: 5 * K, : 4 * K], sems.at[0]),
        pltpu.make_async_copy(blank, factor_hbm.at[: 4 * K, 4 * K :], sems.at[1]),
        pltpu.make_async_copy(blank.at[: 3 * K], factor_hbm.at[5 * K :, : 4 * K], sems.at[2]),
    ]
    for copy in copies:
        copy.start()
    corner[...] = jnp.zeros((4 * K, 4 * K), f32)
    inverse[: 4 * K, :] = first_inverse[...]
    top[...] = first_top[...]
    top_right[...] = first_right[...]
    half_factor(1, lax.axis_index("coarse"), blocks_ref, corner, cross, top, top_right, inverse)
    copies.append(pltpu.make_async_copy(corner, factor_hbm.at[4 * K :, 4 * K :], sems.at[3]))
    copies[-1].start()
    for copy in copies:
        copy.wait()


HBM = pl.BlockSpec(memory_space=pltpu.HBM)


def call(kernel, name, outs, operands, hbm=0, out=None, flops=10**8, scratch=(), limit=16):
    return pl.pallas_call(
        kernel,
        out_shape=outs,
        in_specs=[HBM] * hbm + [VMEM] * (len(operands) - hbm),
        out_specs=jax.tree.map(lambda _: VMEM, outs) if out is None else out,
        scratch_shapes=scratch,
        compiler_params=pltpu.CompilerParams(vmem_limit_bytes=limit * 2**20),
        cost_estimate=pl.CostEstimate(flops=flops, bytes_accessed=2 * 10**6, transcendentals=1000),
        name=name,
    )(*operands)


def array(*shape, dtype=f32):
    return jax.ShapeDtypeStruct(shape, dtype)


FIRST = (array(5 * K, 4 * K), array(4 * K, 2 * K), array(K, 2 * K), array(K, 2 * K))


def passed_along(block, axis, distance):
    count = lax.axis_size(axis)
    return lax.ppermute(block, axis, [(i, (i + distance) % count) for i in range(count)])


def body(deflation, conductivity, storage, interface_rows, interface_counts):
    vectors = deflation[0].reshape(K * CZ, FACE)
    sigma = conductivity[0]
    counts = interface_counts.reshape(2 * REACH)
    layers, parts, ahead, behind, own_tails, top, bottom, live, wanted = call(
        face_kernel,
        "face",
        (
            array(CZ, K, FACE),
            array(CZ, 2 * K, FACE, dtype=bf16),
            array(K, FACE),
            array(K, FACE),
            array(16, FACE),
            array(ROWS, FACE),
            array(ROWS, FACE),
            array(8, FACE),
            array(8, FACE, dtype=jnp.int32),
        ),
        tuple(
            pltpu.with_memory_space_constraint(x, pltpu.HBM)
            for x in (vectors, sigma, interface_rows[0, 0], counts)
        ),
        hbm=4,
        scratch=(
            pltpu.VMEM((CZ, FACE), f32),
            pltpu.VMEM((2 * REACH, FACE), jnp.int32),
            pltpu.SMEM((2 * REACH,), jnp.int32),
            pltpu.VMEM((4, FACE, 256), bf16),
            pltpu.VMEM((4, K * CZ, 128), f32),
            pltpu.SemaphoreType.DMA((7,)),
        ),
    )
    count = lax.axis_size("sub")
    swap = [(i, i ^ 1) for i in range(count)]
    below = passed_along(top, "coarse", 1)
    above = passed_along(bottom, "coarse", -1)
    other_tails = lax.ppermute(own_tails, "sub", swap)
    own = call(own_kernel, "own", array(K, K), (layers, parts, sigma, storage[0]))
    other_tails, own = lax.optimization_barrier((other_tails, own))
    go_ahead, go_behind = call(
        pair_kernel, "pair", (array(16, FACE), array(16, FACE)), (own_tails, other_tails), flops=10**6
    )
    far = [(i, (i + 2 + 2 * (i % 2)) % count) for i in range(count)]
    before = lax.ppermute(go_ahead, "sub", far)
    after = lax.ppermute(go_behind, "sub", [(j, i) for i, j in far])
    mine, exact, square, lower = call(
        row_kernel,
        "rows",
        (array(8, 2 * K, FACE, dtype=bf16), array(8, K, FACE), array(K, K), array(K, K)),
        (ahead, behind, wanted, top, bottom, below, above),
    )
    (before, after), mine = lax.optimization_barrier(((before, after), mine))
    both = call(join_kernel, "join", array(32, FACE), (before, after), flops=10**6)
    swapped_tails = lax.ppermute(both, "sub", swap)
    payload, weighted, index = call(
        block_kernel,
        "block",
        (
            array(8, K, 2 * K),
            array(8, 2 * K, FACE, dtype=bf16),
            array(8, FACE, dtype=jnp.int32),
        ),
        (live, own, square, lower, mine, exact, own_tails, other_tails, before, after, swapped_tails),
    )
    (ahead, behind), payload = lax.optimization_barrier(((ahead, behind), payload))
    blocks = lax.all_to_all(payload, "coarse", 0, 0)
    faces = (
        passed_along(ahead, "sub", 2),
        passed_along(behind, "sub", -2),
        passed_along(ahead, "sub", 4),
        passed_along(behind, "sub", -4),
    )
    state = call(
        first_half,
        "factor_first",
        FIRST,
        (blocks,),
        flops=10**9,
        scratch=(pltpu.VMEM((8, K, 2 * K), f32),),
    )
    faces, state = lax.optimization_barrier((faces, state))
    packed = call(pack_kernel, "faces", array(4 * K, FACE), (ahead, behind, *faces), flops=10**6)
    faces = (*faces, lax.ppermute(packed, "sub", swap))
    factor, inverse = call(
        second_half,
        "factor_second",
        (array(8 * K, 8 * K), array(8 * K, 2 * K)),
        (blocks, *state),
        flops=10**9,
        out=(HBM, VMEM),
        scratch=(
            pltpu.VMEM((8, K, 2 * K), f32),
            pltpu.VMEM((K, 2 * K), f32),
            pltpu.VMEM((K, 2 * K), f32),
            pltpu.VMEM((4 * K, 4 * K), f32),
            pltpu.VMEM((4 * K, 4 * K), f32),
            pltpu.SemaphoreType.DMA((4,)),
        ),
    )
    panel = call(
        panel_kernel,
        "panel",
        array(8 * K, 8 * K),
        (weighted, index, *faces, inverse),
        out=HBM,
        scratch=(
            pltpu.VMEM((8, 2 * K, FACE), bf16),
            pltpu.VMEM((4, 2 * K, 8 * K), f32),
            pltpu.SemaphoreType.DMA((4,)),
        ),
    )
    return (factor[None], panel[None, None])


def solution(mesh):
    placed = (
        P("sub", None, "coarse", None),
        P("sub", "coarse", None),
        P("sub", "coarse", None),
        P("sub", "coarse", None, None),
        P("sub", "coarse", None),
    )
    return jax.shard_map(
        body,
        mesh=mesh,
        in_specs=placed,
        out_specs=(P("sub", None, None), P("sub", "coarse", None, None)),
        check_vma=False,
    )
```

```python
import functools

import jax
import jax.numpy as jnp
from jax import lax
from jax.experimental import pallas as pl
from jax.experimental.pallas import tpu as pltpu
from jax.sharding import PartitionSpec as P

K = 64
CX = 16
CY = 32
CZ = 16
FACE = 512
REACH = 4
ROWS = K + 8

f32 = jnp.float32
bf16 = jnp.bfloat16
VMEM = pl.BlockSpec(memory_space=pltpu.VMEM)
MATRIX = (((1,), (0,)), ((), ()))
GRAM = (((1,), (1,)), ((), ()))


def product(left, right, dims):
    return lax.dot_general(left, right, dims, preferred_element_type=f32)


def harmonic(first, second):
    return 2.0 * first * second / (first + second)


def halves(x):
    high = x.astype(bf16)
    return high, (x - high.astype(f32)).astype(bf16)


def stacked(x):
    return jnp.concatenate(halves(x), axis=0)


def quadrants(square):
    half = square[:K] + square[K:]
    return half[:, :K] + half[:, K:]


def gathered(table, index):
    strips = []
    for q in range(4):
        wanted = jnp.broadcast_to(index[:, 128 * q : 128 * (q + 1)], (8, 128))
        found = None
        for strip in range(4):
            part = jnp.take_along_axis(
                table[:, 128 * strip : 128 * (strip + 1)],
                wanted & 127,
                axis=1,
                mode="promise_in_bounds",
            )
            found = part if strip == 0 else jnp.where(wanted >> 7 == strip, part, found)
        strips.append(found)
    return jnp.concatenate(strips, axis=1)


def one_hot(index):
    place = lax.broadcasted_iota(jnp.int32, (FACE, FACE), 0)
    return jnp.where(place == index, 1.0, 0.0).astype(bf16)


def layer_of(strips, z):
    return jnp.concatenate([strips[q, pl.ds(z, K, stride=CZ), :] for q in range(4)], axis=1)


def face_kernel(vectors_hbm, sigma_hbm, index_hbm, counts_hbm, layers_ref, parts_ref, faces_ref, tails_ref, top_ref, bottom_ref, live_ref, wanted_ref, sigma_ref, index_ref, counts_ref, choice_ref, strips, sems):
    small = [
        pltpu.make_async_copy(sigma_hbm, sigma_ref, sems.at[4]),
        pltpu.make_async_copy(index_hbm, index_ref, sems.at[5]),
        pltpu.make_async_copy(counts_hbm, counts_ref, sems.at[6]),
    ]
    large = [
        pltpu.make_async_copy(vectors_hbm.at[:, pl.ds(128 * q, 128)], strips.at[q], sems.at[q])
        for q in range(4)
    ]
    for copy in small + large:
        copy.start()
    lane = lax.broadcasted_iota(jnp.int32, (1, 256), 1)
    within = lane % 128
    cell_of_lane = (within % CY) * CX + jnp.where(lane >= 128, CX - 1, 0)
    cell = lax.broadcasted_iota(jnp.int32, (FACE, 256), 0)
    for step in range(4):
        chosen = jnp.where(within // CY == step, cell_of_lane, -1)
        choice_ref[step] = jnp.where(cell == chosen, 1.0, 0.0).astype(bf16)
    for copy in small:
        copy.wait()

    def faces_of(rows_of_layer, count):
        total = jnp.zeros((4 * count, 256), f32)
        for step in range(4):
            groups = [rows_of_layer(4 * group + step) for group in range(4)]
            total = total + product(jnp.concatenate(groups, axis=0), choice_ref[step], MATRIX)
        return [
            jnp.concatenate(
                [
                    total[count * group : count * (group + 1), 128 * side : 128 * (side + 1)]
                    for group in range(4)
                ],
                axis=1,
            )
            for side in range(2)
        ]

    def sigma_rows(z):
        high, low = halves(jnp.broadcast_to(sigma_ref[z : z + 1, :], (8, FACE)))
        return jnp.concatenate([high.astype(f32), low.astype(f32)], axis=0).astype(bf16)

    along = lax.broadcasted_iota(jnp.int32, (1, FACE), 1)
    sigma_faces = faces_of(sigma_rows, 16)
    for slot in range(2 * REACH):
        side = slot // REACH
        live_ref[slot : slot + 1] = jnp.where(along < counts_ref[slot], 1.0, 0.0)
        cell_index = index_ref[slot : slot + 1, :]
        wanted = (cell_index >> 9) * CY + ((cell_index >> 4) & (CY - 1))
        wanted_ref[slot : slot + 1] = wanted
        found = gathered(sigma_faces[side][:8] + sigma_faces[side][8:], wanted)
        row = slot - REACH if side else 8 + REACH - 1 - slot
        tails_ref[row : row + 1] = found[:1]
        tails_ref[4 + row : 5 + row] = wanted.astype(f32)
    for copy in large:
        copy.wait()

    def vector_rows(z):
        layer = layer_of(strips, z)
        layers_ref[z] = layer
        parts = stacked(layer)
        parts_ref[z] = parts
        for out_ref, at in ((bottom_ref, 0), (top_ref, CZ - 1)):
            if z == at:
                out_ref[:K] = layer
                out_ref[K:] = jnp.broadcast_to(sigma_ref[z : z + 1, :], (8, FACE))
        return parts

    faces = faces_of(vector_rows, 2 * K)
    for side, at in ((0, slice(K, 2 * K)), (1, slice(0, K))):
        faces_ref[at] = faces[side][:K] + faces[side][K:]


def row_kernel(faces_ref, wanted_ref, top_ref, bottom_ref, below_ref, above_ref, own_ref, exact_ref, square_ref, lower_ref):
    for side, at in ((0, slice(K, 2 * K)), (1, slice(0, K))):
        table = stacked(faces_ref[at])
        for slot in range(REACH * side, REACH * (side + 1)):
            select = one_hot(wanted_ref[slot : slot + 1, :])
            found = product(table, select, MATRIX)
            own_ref[slot] = found.astype(bf16)
            exact_ref[slot] = found[:K] + found[K:]
    level = lax.axis_index("coarse")
    downward = harmonic(bottom_ref[K : K + 1, :], below_ref[K : K + 1, :])
    downward = jnp.where(level == 0, 0.0, downward)
    upward = harmonic(top_ref[K : K + 1, :], above_ref[K : K + 1, :])
    upward = jnp.where(level == lax.axis_size("coarse") - 1, 0.0, upward)
    top, bottom = top_ref[:K, :], bottom_ref[:K, :]
    weighted = stacked(bottom * downward)
    square = product(stacked(top * upward), stacked(top), GRAM)
    square_ref[...] = quadrants(square + product(weighted, stacked(bottom), GRAM))
    lower_ref[...] = -quadrants(product(weighted, stacked(below_ref[:K, :]), GRAM))


def own_kernel(layers_ref, parts_ref, sigma_ref, storage_ref, own_ref):
    sigma = sigma_ref[...]
    lane = lax.broadcasted_iota(jnp.int32, (CZ, FACE), 1)
    layer = lax.broadcasted_iota(jnp.int32, (CZ, FACE), 0)
    along_x = jnp.where(
        lane % CX == CX - 1, 0.0, harmonic(sigma, pltpu.roll(sigma, FACE - 1, 1))
    )
    along_y = jnp.where(
        lane >= FACE - CX, 0.0, harmonic(sigma, pltpu.roll(sigma, FACE - CX, 1))
    )
    along_z = jnp.where(layer == CZ - 1, 0.0, harmonic(sigma, pltpu.roll(sigma, CZ - 1, 0)))
    half = 0.5 * (
        storage_ref[...]
        + along_x
        + pltpu.roll(along_x, 1, 1)
        + along_y
        + pltpu.roll(along_y, CX, 1)
        + along_z
        + pltpu.roll(along_z, 1, 0)
    )
    total = jnp.zeros((2 * K, 2 * K), f32)
    below = layers_ref[0]
    for z in range(CZ):
        now = below
        applied = half[z : z + 1] * now
        applied = applied - along_x[z : z + 1] * pltpu.roll(now, FACE - 1, 1)
        applied = applied - along_y[z : z + 1] * pltpu.roll(now, FACE - CX, 1)
        if z < CZ - 1:
            below = layers_ref[z + 1]
            applied = applied - along_z[z : z + 1] * below
        total = total + product(parts_ref[z], stacked(applied), GRAM)
    own = quadrants(total)
    own_ref[...] = own + own.T


def pair_kernel(own, other, ahead_ref, behind_ref):
    half = own.shape[0] // 2
    ahead_ref[:half] = own[:half]
    ahead_ref[half:] = other[:half]
    behind_ref[:half] = own[half:]
    behind_ref[half:] = other[half:]


def join_kernel(first, second, out_ref):
    rows = first.shape[0]
    out_ref[:rows] = first[...]
    out_ref[rows:] = second[...]


OFFSETS = (-4, -3, -2, -1, 1, 2, 3, 4)


def by_slot(other, before, after, swapped):
    even = lax.axis_index("sub") % 2 == 0
    rows = other.shape[0]
    low, high = slice(0, rows // 2), slice(rows // 2, rows)
    before1 = jnp.where(even, before[...], swapped[:rows])
    before2 = jnp.where(even, swapped[:rows], before[...])
    after1 = jnp.where(even, after[...], swapped[rows:])
    after2 = jnp.where(even, swapped[rows:], after[...])
    on_even = (before2[high], before2[low], before1[low], before1[high], other[high], after1[low], after1[high], after2[high])
    on_odd = (before2[low], before1[low], before1[high], other[low], after1[low], after1[high], after2[high], after2[low])
    return [jnp.where(even, x, y) for x, y in zip(on_even, on_odd, strict=True)]


def block_kernel(live_ref, own_block, square_block, lower_block, own_ref, exact_ref, own_tails, *refs):
    *tails, out_ref, weighted_ref, index_ref = refs
    total = jnp.zeros((2 * K, 2 * K), f32)
    found = by_slot(*tails)
    for slot, offset in enumerate(OFFSETS):
        reach = abs(offset) - 1
        row = reach if offset > 0 else 8 + reach
        pair = harmonic(own_tails[row : row + 1], found[slot][reach : reach + 1])
        weight = jnp.where(live_ref[slot : slot + 1] > 0.0, pair, 0.0)
        index_ref[slot : slot + 1] = found[slot][4 + reach : 5 + reach].astype(jnp.int32)
        weighted_ref[slot] = stacked(exact_ref[slot] * weight)
    for slot in range(2 * REACH):
        total = total + product(weighted_ref[slot], own_ref[slot], GRAM)
    level = lax.axis_index("coarse")
    extra = quadrants(total) + square_block[...]
    own = own_block[...] + 0.5 * (extra + extra.T)
    lower = lower_block[...]
    even = level % 2 == 0
    payload = jnp.where(
        even, jnp.concatenate([own, lower], axis=1), jnp.concatenate([lower, own], axis=1)
    )
    for copy in range(8):
        out_ref[copy] = payload


def panel_kernel(weighted_ref, index_ref, *refs):
    faces, (inverse, out_hbm, found_ref, rows_ref, sems) = refs[:4], refs[4:]
    for slot, face in enumerate(by_slot(*faces)):
        select = one_hot(index_ref[slot : slot + 1, :])
        found_ref[slot] = product(stacked(face), select, MATRIX).astype(bf16)
    blocks = [
        -quadrants(product(weighted_ref[slot], found_ref[slot], GRAM)) for slot in range(2 * REACH)
    ]
    high, low = halves(jnp.concatenate(blocks, axis=1))
    down = jnp.concatenate([high, high, low], axis=0)
    copies = []
    for part in range(4):
        at = slice(128 * part, 128 * (part + 1))
        left_high, left_low = halves(inverse[at, :K])
        left = jnp.concatenate([left_high, left_low, left_high], axis=1)
        rows_ref[part] = product(left, down, MATRIX)
        copies.append(pltpu.make_async_copy(rows_ref.at[part], out_hbm.at[at], sems.at[part]))
        copies[-1].start()
    for copy in copies:
        copy.wait()


def thirds(x):
    high = x.astype(bf16)
    rest = x - high.astype(f32)
    middle = rest.astype(bf16)
    return high, middle, (rest - middle.astype(f32)).astype(bf16)


def fine_product(left, right):
    a, b, c = thirds(left)
    p, q, r = thirds(right)
    first = product(jnp.concatenate([a, b, c], axis=0), p, MATRIX)
    second = product(jnp.concatenate([a, b], axis=0), q, MATRIX)
    small = product(a, r, MATRIX) + first[2 * K :] + second[K:]
    return first[:K] + (first[K : 2 * K] + second[:K] + small)


def lane_of(x, lane):
    index = jnp.full(x.shape, lane, jnp.int32)
    return jnp.take_along_axis(x, index, axis=1, mode="promise_in_bounds")


def sublane_of(x, sublane):
    index = jnp.full(x.shape, sublane, jnp.int32)
    return jnp.take_along_axis(x, index, axis=0, mode="promise_in_bounds")


def eliminate(rows, right, offset, lane, sub):
    wide = (8, 128)
    kept_rows, kept_right_rows = [], []
    for panel in range(8):
        first = offset + 8 * panel
        column = [
            {
                g: lane_of(rows[g], first + k)
                for g in range(panel, 8)
            }
            for k in range(8)
        ]
        pivot = [[None] * 8 for _ in range(8)]
        for i in range(8):
            for k in range(i, 8):
                pivot[i][k] = sublane_of(column[i][panel], k)
        left_row = [sublane_of(rows[panel], k) for k in range(8)]
        right_row = [sublane_of(right[panel], k) for k in range(8)]
        kept = jnp.zeros(wide, f32)
        kept_right = jnp.zeros(wide, f32)
        for i in range(8):
            scale = lax.rsqrt(pivot[i][i])
            inverse = 1.0 / pivot[i][i]
            kept = jnp.where(sub == i, left_row[i] * scale, kept)
            kept_right = jnp.where(sub == i, right_row[i] * scale, kept_right)
            left_row[i] = left_row[i] * inverse
            right_row[i] = right_row[i] * inverse
            scaled = [None] * 8
            for l in range(i + 1, 8):
                scaled[l] = pivot[i][l] * inverse
            for k in range(8):
                if k == i:
                    continue
                by = pivot[i][k] if k > i else pivot[k][i]
                left_row[k] = left_row[k] - by * left_row[i]
                right_row[k] = right_row[k] - by * right_row[i]
                for l in range(max(i + 1, k), 8):
                    pivot[k][l] = pivot[k][l] - by * scaled[l]
            pivot[i] = scaled
        for g in range(panel + 1, 8):
            for k in range(8):
                rows[g] = rows[g] - column[k][g] * left_row[k]
                right[g] = right[g] - column[k][g] * right_row[k]
        live = (lane >= first + sub) if offset else ((lane >= first + sub) | (lane >= K))
        if offset:
            live = live | (lane < K)
        kept_rows.append(jnp.where(live, kept, 0.0))
        kept_right_rows.append(kept_right)
    return jnp.concatenate(kept_rows, axis=0), jnp.concatenate(kept_right_rows, axis=0)


def half_factor(begin, level, blocks_ref, factor_ref, cross, top, top_right, inverse):
    lane = lax.broadcasted_iota(jnp.int32, (8, 128), 1)
    sub = lax.broadcasted_iota(jnp.int32, (8, 128), 0)
    wide_lane = lax.broadcasted_iota(jnp.int32, (K, 2 * K), 1)
    wide_sub = lax.broadcasted_iota(jnp.int32, (K, 2 * K), 0)
    zero = jnp.zeros((K, 2 * K), f32)
    at = [pl.ds(8 * g, 8) for g in range(8)]
    for c in range(4 * begin + 1, min(4 * begin + 5, 8)):
        block = blocks_ref[c]
        if c % 2 == 1:
            cross[c - 1] = jnp.concatenate([zero, block], axis=0).T[:K]
        else:
            cross[c - 1] = jnp.concatenate([block, zero], axis=0).T[K:]
    if begin:
        cross[7] = zero

    def unit(c):
        return jnp.where((wide_lane == wide_sub) & (level == c), 1.0, 0.0)

    if not begin:
        top[...] = blocks_ref[0]
        top_right[...] = unit(0)

    @pl.loop(2 * begin, 2 * begin + 2)
    def _(q):
        c = 2 * q
        last = q == 3
        rows = [jnp.where(lane < K, top[at[g], :], cross[c, at[g], :]) for g in range(8)]
        right = [top_right[at[g], :] for g in range(8)]
        even, even_right = eliminate(rows, right, 0, lane, sub)
        even_turned = even.T
        taken = fine_product(even_turned[K:], jnp.concatenate([even, even_right], axis=1))
        under = blocks_ref[c + 1] - taken[:, : 2 * K]
        under_right = unit(c + 1) - taken[:, 2 * K :]
        rows = [jnp.where(lane < K, cross[c + 1, at[g], :], under[8 * g : 8 * g + 8]) for g in range(8)]
        right = [under_right[8 * g : 8 * g + 8] for g in range(8)]
        odd, odd_right = eliminate(rows, right, K, lane, sub)
        odd_turned = odd.T
        taken = fine_product(odd_turned[:K], jnp.concatenate([odd, odd_right], axis=1))
        top[...] = jnp.where(last, 0.0, blocks_ref[jnp.minimum(c + 2, 7)]) - taken[:, : 2 * K]
        top_right[...] = unit(c + 2) - taken[:, 2 * K :]
        start = pl.multiple_of(128 * q, 128)
        inverse[pl.ds(start, K), :] = even_right
        inverse[pl.ds(start + K, K), :] = odd_right
        both = jnp.concatenate([even_turned, odd_turned], axis=1)
        within = pl.multiple_of(start - 4 * K * begin, 128)
        cols = pl.ds(within, 128)
        factor_ref[pl.ds(within, K), cols] = jnp.where(wide_lane < K, both[:K], 0.0)
        factor_ref[pl.ds(within + K, K), cols] = both[K:]

        @pl.when(q < 3)
        def _():
            factor_ref[pl.ds(within + 128, K), cols] = jnp.where(wide_lane < K, 0.0, both[:K])


def first_half(blocks_ref, factor_ref, inverse, top, top_right, cross):
    factor_ref[...] = jnp.zeros((5 * K, 4 * K), f32)
    half_factor(0, lax.axis_index("coarse"), blocks_ref, factor_ref, cross, top, top_right, inverse)


def second_half(blocks_ref, part_ref, first_inverse, first_top, first_right, factor_hbm, inverse, cross, top, top_right, corner, blank, sems):
    blank[...] = jnp.zeros((4 * K, 4 * K), f32)
    copies = [
        pltpu.make_async_copy(part_ref, factor_hbm.at[: 5 * K, : 4 * K], sems.at[0]),
        pltpu.make_async_copy(blank, factor_hbm.at[: 4 * K, 4 * K :], sems.at[1]),
        pltpu.make_async_copy(blank.at[: 3 * K], factor_hbm.at[5 * K :, : 4 * K], sems.at[2]),
    ]
    for copy in copies:
        copy.start()
    corner[...] = jnp.zeros((4 * K, 4 * K), f32)
    inverse[: 4 * K, :] = first_inverse[...]
    top[...] = first_top[...]
    top_right[...] = first_right[...]
    half_factor(1, lax.axis_index("coarse"), blocks_ref, corner, cross, top, top_right, inverse)
    copies.append(pltpu.make_async_copy(corner, factor_hbm.at[4 * K :, 4 * K :], sems.at[3]))
    copies[-1].start()
    for copy in copies:
        copy.wait()


HBM = pl.BlockSpec(memory_space=pltpu.HBM)


def call(kernel, name, outs, operands, hbm=0, out=None, flops=10**8, scratch=(), limit=16):
    return pl.pallas_call(
        kernel,
        out_shape=outs,
        in_specs=[HBM] * hbm + [VMEM] * (len(operands) - hbm),
        out_specs=jax.tree.map(lambda _: VMEM, outs) if out is None else out,
        scratch_shapes=scratch,
        compiler_params=pltpu.CompilerParams(vmem_limit_bytes=limit * 2**20),
        cost_estimate=pl.CostEstimate(flops=flops, bytes_accessed=2 * 10**6, transcendentals=1000),
        name=name,
    )(*operands)


def array(*shape, dtype=f32):
    return jax.ShapeDtypeStruct(shape, dtype)


FIRST = (array(5 * K, 4 * K), array(4 * K, 2 * K), array(K, 2 * K), array(K, 2 * K))


def passed_along(block, axis, distance):
    count = lax.axis_size(axis)
    return lax.ppermute(block, axis, [(i, (i + distance) % count) for i in range(count)])


def body(deflation, conductivity, storage, interface_rows, interface_counts):
    vectors = deflation[0].reshape(K * CZ, FACE)
    sigma = conductivity[0]
    counts = interface_counts.reshape(2 * REACH)
    layers, parts, own_faces, own_tails, top, bottom, live, wanted = call(
        face_kernel,
        "face",
        (
            array(CZ, K, FACE),
            array(CZ, 2 * K, FACE, dtype=bf16),
            array(2 * K, FACE),
            array(16, FACE),
            array(ROWS, FACE),
            array(ROWS, FACE),
            array(8, FACE),
            array(8, FACE, dtype=jnp.int32),
        ),
        tuple(
            pltpu.with_memory_space_constraint(x, pltpu.HBM)
            for x in (vectors, sigma, interface_rows[0, 0], counts)
        ),
        hbm=4,
        scratch=(
            pltpu.VMEM((CZ, FACE), f32),
            pltpu.VMEM((2 * REACH, FACE), jnp.int32),
            pltpu.SMEM((2 * REACH,), jnp.int32),
            pltpu.VMEM((4, FACE, 256), bf16),
            pltpu.VMEM((4, K * CZ, 128), f32),
            pltpu.SemaphoreType.DMA((7,)),
        ),
    )
    count = lax.axis_size("sub")
    swap = [(i, i ^ 1) for i in range(count)]
    below = passed_along(top, "coarse", 1)
    above = passed_along(bottom, "coarse", -1)
    other_tails = lax.ppermute(own_tails, "sub", swap)
    own = call(own_kernel, "own", array(K, K), (layers, parts, sigma, storage[0]))
    other_tails, own = lax.optimization_barrier((other_tails, own))
    far = [(i, (i + 2 + 2 * (i % 2)) % count) for i in range(count)]

    def paired(own, other):
        half = array(own.shape[0], FACE)
        return call(pair_kernel, "pair", (half, half), (own, other), flops=10**6)

    def sent(ahead, behind):
        return (
            lax.ppermute(ahead, "sub", far),
            lax.ppermute(behind, "sub", [(j, i) for i, j in far]),
        )

    def joined(before, after):
        out = array(2 * before.shape[0], FACE)
        return lax.ppermute(
            call(join_kernel, "join", out, (before, after), flops=10**6), "sub", swap
        )

    before, after = sent(*paired(own_tails, other_tails))
    other_faces = lax.ppermute(own_faces, "sub", swap)
    mine, exact, square, lower = call(
        row_kernel,
        "rows",
        (array(8, 2 * K, FACE, dtype=bf16), array(8, K, FACE), array(K, K), array(K, K)),
        (own_faces, wanted, top, bottom, below, above),
    )
    (before, after), going, mine = lax.optimization_barrier(
        ((before, after), paired(own_faces, other_faces), mine)
    )
    swapped_tails = joined(before, after)
    payload, weighted, index = call(
        block_kernel,
        "block",
        (
            array(8, K, 2 * K),
            array(8, 2 * K, FACE, dtype=bf16),
            array(8, FACE, dtype=jnp.int32),
        ),
        (live, own, square, lower, mine, exact, own_tails, other_tails, before, after, swapped_tails),
    )
    going, payload = lax.optimization_barrier((going, payload))
    blocks = lax.all_to_all(payload, "coarse", 0, 0)
    faces = sent(*going)
    state = call(
        first_half,
        "factor_first",
        FIRST,
        (blocks,),
        flops=10**9,
        scratch=(pltpu.VMEM((8, K, 2 * K), f32),),
    )
    faces, state = lax.optimization_barrier((faces, state))
    faces = (other_faces, *faces, joined(*faces))
    factor, inverse = call(
        second_half,
        "factor_second",
        (array(8 * K, 8 * K), array(8 * K, 2 * K)),
        (blocks, *state),
        flops=10**9,
        out=(HBM, VMEM),
        scratch=(
            pltpu.VMEM((8, K, 2 * K), f32),
            pltpu.VMEM((K, 2 * K), f32),
            pltpu.VMEM((K, 2 * K), f32),
            pltpu.VMEM((4 * K, 4 * K), f32),
            pltpu.VMEM((4 * K, 4 * K), f32),
            pltpu.SemaphoreType.DMA((4,)),
        ),
    )
    panel = call(
        panel_kernel,
        "panel",
        array(8 * K, 8 * K),
        (weighted, index, *faces, inverse),
        out=HBM,
        scratch=(
            pltpu.VMEM((8, 2 * K, FACE), bf16),
            pltpu.VMEM((4, 2 * K, 8 * K), f32),
            pltpu.SemaphoreType.DMA((4,)),
        ),
    )
    return (factor[None], panel[None, None])


def solution(mesh):
    placed = (
        P("sub", None, "coarse", None),
        P("sub", "coarse", None),
        P("sub", "coarse", None),
        P("sub", "coarse", None, None),
        P("sub", "coarse", None),
    )
    return jax.shard_map(
        body,
        mesh=mesh,
        in_specs=placed,
        out_specs=(P("sub", None, None), P("sub", "coarse", None, None)),
        check_vma=False,
    )
```
